32 devices in a mesh: seq: 4 (over z), head: 4 (over y, x), rep: 2 (over core).
Axes of the slice: x: 2, y: 2, z: 4, core: 2. Of those that a mesh axis runs over, the one named last changes fastest.
Arguments:
- hidden: bfloat16 [8192, 8192], P(('seq', 'rep')), may hold values from -6 to 6
- key_weight: bfloat16 [8192, 1024], P(('seq', 'rep'), 'head'), may hold values from -0.0625 to 0.0625
- value_weight: bfloat16 [8192, 1024], P(('seq', 'rep'), 'head'), may hold values from -0.0625 to 0.0625
- group_scale: float32 [2, 1024], P(None, 'head'), may hold values from 0.05 to 0.4
- new_kv: bfloat16 [4, 32, 2, 1024], P(None, 'seq', None, 'head'), may hold values from -6 to 6
- decode_query: bfloat16 [4, 32, 8192], P(None, 'seq', 'head'), may hold values from -400 to 400
- page_table: int32 [32, 32], replicated, may hold values from 0 to 255, as said below
- lengths: int32 [32], replicated, may hold values from 1 to 1024
Outputs:
- kv_cache: bfloat16 [8192, 2, 1024], P(('seq', 'rep'), None, 'head')
- smoothing: float32 [1024], P('head')
- attention: bfloat16 [4, 32, 8192], P(None, 'seq', 'head')
The draws below stay inside these ranges and needn't reach their ends.
Inputs may be any that keep to these rules, and one draw needn't show every extreme that they name: `page_table`: page p holds prefilled tokens p * 32 to p * 32 + 31. Slot j of request r is live when j * 32 < lengths[r]. Over the live slots of one parity of j of the 8 requests r with one value of r // 8, at most 16 pages lie in any one block of 32 consecutive pages; this bound is reached.
All inputs are finite; a program needn't handle non-finite values.
Results may differ from the reference program's by a relative error of at most 0.007.
The reference program's roundings to bfloat16 on the way count: a program that leaves them out, or rounds other values in their place, can miss the bound.
Values may be sent and summed in bfloat16 or wider, within the bound.
No kernel may reach another device: no remote copies, remote signals or barrier semaphores. Data moves between devices by JAX's collectives and lax.ppermute only.
A program may use at most 128 MiB of HBM per device.

```python
import math
import jax
import jax.numpy as jnp
from jax import lax

D = 8192
KVH = 8
HD = 128
QH = 64
PTOK_DEV = 1024
REQ_DEV = 8
PAGE = 32
MAXPAGES = 32
STEPS = 4
TOKENS = 8192
BATCH = 32
N_SEQ = 4
N_REP = 2


def page_plan(key):
    base_key = jax.random.fold_in(key, 7)
    key_length, key_full, key_order, key_spare, key_page = jax.random.split(base_key, 5)
    groups = N_SEQ
    owners = N_REP
    sources = N_SEQ * N_REP
    pages_dev = PTOK_DEV // PAGE
    entries = REQ_DEV * MAXPAGES
    lengths = jax.random.randint(key_length, (BATCH,), 1, MAXPAGES * PAGE + 1, dtype=jnp.int32)
    full_group = jax.random.randint(key_full, (), 0, groups, dtype=jnp.int32)
    group_of = jnp.arange(BATCH, dtype=jnp.int32) // REQ_DEV
    lengths = jnp.where(group_of == full_group, MAXPAGES * PAGE, lengths).astype(jnp.int32)
    slot_ids = jnp.arange(MAXPAGES, dtype=jnp.int32)
    live_slots = (slot_ids[None, :] * PAGE < lengths[:, None]).reshape(groups, entries)
    owner_of = jnp.broadcast_to(slot_ids % owners, (BATCH, MAXPAGES)).reshape(groups, entries)
    orders = jax.vmap(lambda subkey: jax.random.permutation(subkey, sources))(jax.random.split(key_order, groups * owners))
    orders = orders.reshape(groups, owners, sources).astype(jnp.int32)
    source_ids = jax.random.randint(key_spare, (groups, entries), 0, sources, dtype=jnp.int32)
    for owner_value in range(owners):
        owned_mask = live_slots & (owner_of == owner_value)
        counted = jnp.cumsum(owned_mask.astype(jnp.int32), axis=1) - 1
        picked = jnp.take_along_axis(orders[:, owner_value, :], jnp.maximum(counted, 0) % sources, axis=1)
        source_ids = jnp.where(owned_mask, picked, source_ids)
    within = jax.random.randint(key_page, (groups, entries), 0, pages_dev, dtype=jnp.int32)
    page_ids = (source_ids * pages_dev + within).reshape(BATCH, MAXPAGES).astype(jnp.int32)
    return (page_ids, lengths)


def draw_page_table(key, part):
    return page_plan(key)[0]


def draw_lengths(key, part):
    return page_plan(key)[1]


def draw_decode_query(key, part):
    base_key = jax.random.fold_in(key, 31)
    drawn = jnp.clip(jax.random.normal(base_key, (STEPS, BATCH, QH * HD), jnp.float32), -5.0, 5.0)
    return drawn.astype(jnp.bfloat16)


def shard_levels(key, shape, cuts, low, largest):
    def one(position, shards_of):
        steps = jax.random.uniform(jax.random.fold_in(jax.random.fold_in(key, 6), position), (shards_of,), jnp.float32, low / len(cuts), largest / len(cuts))
        return jnp.repeat(jnp.exp(steps), shape[position] // shards_of).reshape((-1,) + (1,) * (len(shape) - position - 1))

    level = one(*cuts[0])
    for cut in cuts[1:]:
        level = level * one(*cut)
    return level


def normal_values(rng, extent, deviation, bound, shards=(), kind=jnp.bfloat16):
    values = jax.random.normal(rng, extent, jnp.float32) * deviation
    if len(shards) > 0:
        values = shard_levels(rng, extent, shards, -0.22, 0.18) * values
    return jnp.clip(values, min=-bound, max=bound).astype(kind)


def setup_inputs(seed: int = 0) -> dict:
    arg_keys = jax.random.split(jax.random.key(seed), 9)
    hidden = normal_values(arg_keys[0], (TOKENS, D), 1.0, 6.0, ((0, 8),))
    key_weight = normal_values(arg_keys[1], (D, KVH * HD), D ** -0.5, 0.0625, ((0, 8), (1, 4)))
    value_weight = normal_values(arg_keys[2], (D, KVH * HD), D ** -0.5, 0.0625, ((0, 8), (1, 4)))
    group_scale = jnp.clip(jnp.exp(math.log(0.4) - 2.0794415 * jax.random.uniform(arg_keys[3], (2, KVH * HD), jnp.float32) ** shard_levels(arg_keys[3], (2, KVH * HD), ((1, 4),), -0.2, 0.2)), 0.05, 0.4)
    new_kv = normal_values(arg_keys[4], (STEPS, BATCH, 2, KVH * HD), 1.0, 6.0, ((1, 4), (3, 4)))
    decode_query = draw_decode_query(jax.random.fold_in(arg_keys[8], 71), 0)
    page_table = draw_page_table(jax.random.fold_in(arg_keys[8], 71), 0)
    lengths = draw_lengths(jax.random.fold_in(arg_keys[8], 71), 0)
    return dict(hidden=hidden, key_weight=key_weight, value_weight=value_weight, group_scale=group_scale, new_kv=new_kv, decode_query=decode_query, page_table=page_table, lengths=lengths)


EPSILON = 1e-05
NEGATIVE = -1e+30

def clipped(raw_keys, raw_values, smooth, group_scale):
    keys_out = jnp.clip(raw_keys / smooth, -8.0 * group_scale[0], 7.0 * group_scale[0])
    values_out = jnp.clip(raw_values, -8.0 * group_scale[1], 7.0 * group_scale[1])
    return (keys_out, values_out)

def reference(hidden, key_weight, value_weight, group_scale, new_kv, decode_query, page_table, lengths):
    raw_keys = jnp.dot(hidden, key_weight, preferred_element_type=jnp.float32)
    raw_values = jnp.dot(hidden, value_weight, preferred_element_type=jnp.float32)
    smoothing = jnp.sqrt(lax.optimization_barrier(jnp.max(jnp.abs(raw_keys), axis=0)) + EPSILON)
    keys_clip, values_clip = clipped(raw_keys, raw_values, smoothing, group_scale)
    kv_cache = jnp.stack([keys_clip, values_clip], axis=1).astype(jnp.bfloat16)
    fresh_keys, fresh_values = clipped(new_kv[:, :, 0].astype(jnp.float32), new_kv[:, :, 1].astype(jnp.float32), smoothing, group_scale)
    fresh = jnp.stack([fresh_keys, fresh_values], axis=2).astype(jnp.bfloat16)
    group_size = QH // KVH
    smooth_query = jnp.repeat(smoothing.reshape(KVH, HD), group_size, axis=0).reshape(-1)
    queries = (decode_query.astype(jnp.float32) * smooth_query).astype(jnp.bfloat16)
    context = MAXPAGES * PAGE
    offsets = jnp.arange(PAGE, dtype=jnp.int32)
    score_scale = HD ** (-0.5)
    causal = jnp.arange(STEPS)[None, :] <= jnp.arange(STEPS)[:, None]

    def per_request(request_item):
        table_row, length, query_row, fresh_row = request_item
        row_ids = (table_row[:, None] * PAGE + offsets[None, :]).reshape(-1).astype(jnp.int32)
        cache_rows = jnp.take(kv_cache, row_ids, axis=0)
        keys_all = jnp.concatenate([cache_rows[:, 0], fresh_row[:, 0]], axis=0).astype(jnp.float32).reshape(context + STEPS, KVH, HD)
        values_all = jnp.concatenate([cache_rows[:, 1], fresh_row[:, 1]], axis=0).astype(jnp.float32).reshape(context + STEPS, KVH, HD)
        valid_cache = jnp.broadcast_to(jnp.arange(context)[None, :] < length, (STEPS, context))
        valid_keys = jnp.concatenate([valid_cache, causal], axis=1)
        query_heads = query_row.astype(jnp.float32).reshape(STEPS, KVH, group_size, HD)
        scores = jnp.einsum('tkgd,nkd->tkgn', query_heads, keys_all) * score_scale
        key_mask = valid_keys[:, None, None, :]
        scores = jnp.where(key_mask, scores, NEGATIVE)
        row_max = lax.optimization_barrier(jnp.max(scores, axis=-1, keepdims=True))
        expd = jnp.where(key_mask, jnp.exp(scores - row_max), 0.0)
        totals = lax.optimization_barrier(jnp.sum(expd, axis=-1))
        rounded = lax.optimization_barrier(expd.astype(jnp.bfloat16)).astype(jnp.float32)
        summed = jnp.einsum('tkgn,nkd->tkgd', rounded, values_all)
        return (summed / totals[..., None]).reshape(STEPS, QH * HD).astype(jnp.bfloat16)
    per_batch = lax.map(per_request, (page_table, lengths, jnp.swapaxes(queries, 0, 1), jnp.swapaxes(fresh, 0, 1)))
    attention = jnp.swapaxes(per_batch, 0, 1)
    return (kv_cache, smoothing, attention)
```

```python
import functools

import jax
import jax.numpy as jnp
from jax import lax
from jax.experimental import pallas as pl
from jax.experimental.pallas import tpu as pltpu
from jax.sharding import PartitionSpec as P

KVH = 8
HD = 128
QH = 64
PAGE = 32


EPSILON = 1e-05
NEGATIVE = -1e30
SHORT = 8


def shifted(x, axis, k):
    n = lax.axis_size(axis)
    return lax.ppermute(x, axis, [(i, (i + k) % n) for i in range(n)])


def from_all(x, axis):
    n = lax.axis_size(axis)
    if n > SHORT:
        order = (lax.axis_index(axis) - jnp.arange(n)) % n
        return list(lax.all_gather(x, axis)[order])
    return [x] + [shifted(x, axis, k) for k in range(1, n)]


def to_groups(x):
    n = lax.axis_size("seq")
    if n > SHORT:
        me, k = lax.axis_index("seq"), jnp.arange(n)
        back = lax.all_to_all(x[(me - k) % n], "seq", split_axis=0, concat_axis=0)
        return list(back[(me + k) % n])
    return [x[0]] + [shifted(x[k], "seq", -k) for k in range(1, n)]


def project_kernel(count, has_total, info, *refs):
    lefts, weights = refs[:count], refs[count : 2 * count]
    out = refs[-1]
    out[...] = refs[2 * count][...] if has_total else jnp.zeros_like(out)
    for j in range(count):

        @pl.when(info[count + j] == 1)
        def _(j=j):
            out[...] += jnp.dot(
                lefts[j][...], weights[j][...], preferred_element_type=jnp.float32
            )


def project(hidden, total, weights, where, live):
    tokens = hidden.shape[0]
    depth, columns = weights[0].shape
    count = len(weights)
    tile = min(tokens, 256)
    info = jnp.stack([jnp.asarray(v, jnp.int32) for v in list(where) + list(live)])

    def left_spec(j):
        return pl.BlockSpec((tile, depth), lambda i, info: (i * info[count + j], info[j]))

    total_spec = pl.BlockSpec((tile, columns), lambda i, info: (i, 0))
    has_total = total is not None
    return pl.pallas_call(
        functools.partial(project_kernel, count, has_total),
        out_shape=jax.ShapeDtypeStruct((tokens, columns), jnp.float32),
        grid_spec=pltpu.PrefetchScalarGridSpec(
            num_scalar_prefetch=1,
            grid=(tokens // tile,),
            in_specs=[left_spec(j) for j in range(count)]
            + [pl.BlockSpec((depth, columns), lambda i, info: (0, 0))] * count
            + [total_spec] * has_total,
            out_specs=total_spec,
        ),
        cost_estimate=pl.CostEstimate(
            flops=2 * tokens * depth * columns * count,
            bytes_accessed=2 * count * depth * (tokens + columns) + 8 * tokens * columns,
            transcendentals=0,
        ),
        input_output_aliases={1 + 2 * count: 0} if has_total else {},
        name="project",
    )(info, *([hidden] * count), *weights, *([total] if has_total else []))


def score_kernel(parts, steps, scale, group, query, smooth, count, *refs):
    keys, (probs, highest, total), scores = refs[:parts], refs[parts:-1], refs[-1]
    tokens = keys[0].shape[0]
    scaled = (query[0].astype(jnp.float32) * smooth[...]).astype(jnp.bfloat16)
    for p in range(parts):
        scores[:, p * tokens : (p + 1) * tokens] = lax.dot_general(
            scaled, keys[p][...], (((1,), (1,)), ((), ())), preferred_element_type=jnp.float32
        )
    requests = count.shape[1]
    rows = scores.shape[0]
    group_rows = rows // (steps * requests)
    pair = 2 if requests % 2 == 0 else 1
    for first in range(0, requests, pair):
        times = jnp.concatenate(
            [
                jnp.broadcast_to(count[0, first + a : first + a + 1, :], (group_rows, parts * tokens))
                for a in range(pair)
            ],
            axis=0,
        )
        for step in range(steps):
            start = (step * requests + first) * group_rows
            at = pl.ds(start, pair * group_rows)
            raw = jnp.where(times > 0.0, scores[at, :] * scale, NEGATIVE)
            top = jnp.max(raw, axis=1, keepdims=True)
            expd = jnp.exp(raw - top)
            highest[0, at, :] = top
            total[0, at, :] = jnp.sum(expd * times, axis=1, keepdims=True)
            probs[0, at, :] = (expd.astype(jnp.bfloat16).astype(jnp.float32) * times).astype(
                jnp.bfloat16
            )


def score(groups, query, smooth, count, keys, steps, scale):
    slots, rows, width = query.shape
    tokens = keys[0].shape[0]
    parts = len(keys)
    requests = count.shape[1]
    slot_spec = pl.BlockSpec((1, rows, 1), lambda k, group: (k, 0, 0))
    return pl.pallas_call(
        functools.partial(score_kernel, parts, steps, scale),
        out_shape=(
            jax.ShapeDtypeStruct((slots, rows, parts * tokens), jnp.bfloat16),
            jax.ShapeDtypeStruct((slots, rows, 1), jnp.float32),
            jax.ShapeDtypeStruct((slots, rows, 1), jnp.float32),
        ),
        grid_spec=pltpu.PrefetchScalarGridSpec(
            num_scalar_prefetch=1,
            grid=(slots,),
            in_specs=[
                pl.BlockSpec((1, rows, width), lambda k, group: (k, 0, 0)),
                pl.BlockSpec((1, width), lambda k, group: (0, 0)),
                pl.BlockSpec((1, requests, parts * tokens), lambda k, group: (group[k], 0, 0)),
            ]
            + [pl.BlockSpec((tokens, width), lambda k, group: (0, 0))] * parts,
            out_specs=(
                pl.BlockSpec((1, rows, parts * tokens), lambda k, group: (k, 0, 0)),
                slot_spec,
                slot_spec,
            ),
            scratch_shapes=[pltpu.VMEM((rows, parts * tokens), jnp.float32)],
        ),
        cost_estimate=pl.CostEstimate(
            flops=2 * slots * rows * width * parts * tokens,
            bytes_accessed=2 * slots * rows * parts * tokens,
            transcendentals=slots * rows * parts * tokens,
        ),
        name="score",
    )(groups, query, smooth, count, *keys)


def weigh_kernel(parts, probs, *refs):
    values, out = refs[:parts], refs[-1]
    tokens = values[0].shape[0]
    out[0] = sum(
        jnp.dot(
            probs[0, :, p * tokens : (p + 1) * tokens],
            values[p][...],
            preferred_element_type=jnp.float32,
        )
        for p in range(parts)
    ).astype(jnp.bfloat16)


def weigh(probs, values):
    slots, rows, _ = probs.shape
    tokens, width = values[0].shape
    parts = len(values)
    return pl.pallas_call(
        functools.partial(weigh_kernel, parts),
        out_shape=jax.ShapeDtypeStruct((slots, rows, width), jnp.bfloat16),
        grid=(slots,),
        in_specs=[pl.BlockSpec((1, rows, parts * tokens), lambda k: (k, 0, 0))]
        + [pl.BlockSpec((tokens, width), lambda k: (0, 0))] * parts,
        out_specs=pl.BlockSpec((1, rows, width), lambda k: (k, 0, 0)),
        cost_estimate=pl.CostEstimate(
            flops=2 * slots * rows * width * parts * tokens,
            bytes_accessed=2 * slots * rows * parts * tokens,
            transcendentals=0,
        ),
        name="weigh",
    )(probs, *values)


def token_counts(page_table, lengths, first_pages, pages_dev):
    slots = page_table.shape[1]
    slot_ids = jnp.arange(slots, dtype=jnp.int32)
    whole_slots, rest = lengths // PAGE, lengths % PAGE
    pages = jnp.concatenate(
        [first + jnp.arange(pages_dev, dtype=jnp.int32) for first in first_pages]
    )
    same = page_table[:, :, None] == pages[None, None, :]
    whole = jnp.sum(same & (slot_ids[None, :] < whole_slots[:, None])[:, :, None], axis=1)
    last = jnp.sum(same & (slot_ids[None, :] == whole_slots[:, None])[:, :, None], axis=1)
    token = jnp.arange(pages.shape[0] * PAGE, dtype=jnp.int32)
    spread = token[None, :] // PAGE == jnp.arange(pages.shape[0], dtype=jnp.int32)[:, None]
    spread = spread.astype(jnp.bfloat16)
    whole = jnp.dot(whole.astype(jnp.bfloat16), spread, preferred_element_type=jnp.float32)
    last = jnp.dot(last.astype(jnp.bfloat16), spread, preferred_element_type=jnp.float32)
    return whole + jnp.where((token % PAGE)[None, :] < rest[:, None], last, 0.0)


def clip_keys(raw, smooth, scale):
    return jnp.clip(raw / smooth, -8.0 * scale[0], 7.0 * scale[0]).astype(jnp.bfloat16)


def clip_values(raw, scale):
    return jnp.clip(raw, -8.0 * scale[1], 7.0 * scale[1]).astype(jnp.bfloat16)


def my_part(x, parts, index, axis):
    size = x.shape[axis] // parts
    pieces = [lax.slice_in_dim(x, p * size, (p + 1) * size, axis=axis) for p in range(parts)]
    out = pieces[0]
    for p in range(1, parts):
        out = jnp.where(index == p, pieces[p], out)
    return out


def line_project(hidden, key_weight, value_weight):
    groups, owners = lax.axis_size("seq"), lax.axis_size("rep")
    my_group, my_owner = lax.axis_index("seq"), lax.axis_index("rep")

    def block_of(group):
        group = jnp.clip(group, 0, groups - 1)
        return [group * owners + (my_owner - k) % owners for k in range(owners)]

    weights = (key_weight, value_weight)
    moving = [(weight, weight) for weight in weights]
    totals = [
        project(hidden, None, from_all(w, "rep"), block_of(my_group), [jnp.int32(1)] * owners)
        for w in weights
    ]
    for hop in range(1, groups):
        here_left = (my_group - hop >= 0).astype(jnp.int32)
        here_right = (my_group + hop < groups).astype(jnp.int32)
        for j in range(len(weights)):
            left, right = moving[j]
            left = lax.ppermute(left, "seq", [(i, i + 1) for i in range(hop - 1, groups - 1)])
            right = lax.ppermute(right, "seq", [(i, i - 1) for i in range(1, groups - hop + 1)])
            moving[j] = (left, right)
            totals[j] = project(
                hidden,
                totals[j],
                from_all(left, "rep") + from_all(right, "rep"),
                block_of(my_group - hop) + block_of(my_group + hop),
                [here_left] * owners + [here_right] * owners,
            )
    return totals


def on_device(
    hidden, key_weight, value_weight, group_scale, new_kv, decode_query, page_table, lengths
):
    tokens = hidden.shape[0]
    columns = key_weight.shape[1]
    group_size = QH // KVH
    groups, owners = lax.axis_size("seq"), lax.axis_size("rep")
    my_group, my_owner = lax.axis_index("seq"), lax.axis_index("rep")
    assert columns // HD == owners
    pages_dev = tokens // PAGE
    step_count, per_group = decode_query.shape[:2]

    raw_query = my_part(decode_query, owners, my_owner, 2).reshape(-1, HD)

    owner_at = [(my_owner - k) % owners for k in range(owners)]
    yes = jnp.int32(1)

    if groups > SHORT:
        raw_keys, raw_values = (
            project(
                hidden,
                None,
                [lax.all_gather(weight, ("seq", "rep"), axis=0, tiled=True)],
                [0],
                [yes],
            )
            for weight in (key_weight, value_weight)
        )
    else:
        raw_keys, raw_values = line_project(hidden, key_weight, value_weight)
    queries = jnp.stack(from_all(raw_query, "seq"))

    local_max = jnp.max(jnp.abs(raw_keys), axis=0, keepdims=True)
    local_max = functools.reduce(jnp.maximum, from_all(local_max, "rep"))
    local_max = functools.reduce(jnp.maximum, from_all(local_max, "seq"))
    smooth = jnp.sqrt(local_max + EPSILON)
    smoothing = smooth.reshape(-1)
    keys = clip_keys(raw_keys, smooth, group_scale)
    values = clip_values(raw_values, group_scale)
    kv_cache = jnp.stack([keys, values], axis=1)

    def by_head(x):
        return [my_part(x, owners, my_owner, 1)] + [
            shifted(my_part(x, owners, (my_owner + k) % owners, 1), "rep", k)
            for k in range(1, owners)
        ]

    my_smooth = my_part(smooth, owners, my_owner, 1)
    first_pages = [(my_group * owners + owner) * pages_dev for owner in owner_at]
    counts = token_counts(page_table, lengths, first_pages, pages_dev)
    counts = counts.reshape(groups, per_group, -1)
    group_at = jnp.stack([(my_group - k) % groups for k in range(groups)])
    score_scale = HD ** (-0.5)
    probs, highest, total = score(
        group_at, queries, my_smooth, counts, by_head(keys), step_count, score_scale
    )
    summed = weigh(probs, by_head(values))
    stats = jnp.stack([highest[..., 0], total[..., 0]], axis=1)

    stats = jnp.stack(to_groups(stats))
    highest, total = stats[:, 0], stats[:, 1]

    shape = (step_count, per_group, group_size, HD)
    query = (raw_query.astype(jnp.float32) * my_smooth).astype(jnp.bfloat16).reshape(shape)
    my_kv = my_part(new_kv, owners, my_owner, 3).astype(jnp.float32)
    my_scale = my_part(group_scale, owners, my_owner, 1)
    fresh_keys = clip_keys(my_kv[:, :, 0], my_smooth, my_scale)
    fresh_values = clip_values(my_kv[:, :, 1], my_scale)
    fresh_scores = (
        jnp.einsum("trgd,urd->trgu", query, fresh_keys, preferred_element_type=jnp.float32)
        * score_scale
    )
    causal = jnp.arange(step_count)[None, :] <= jnp.arange(step_count)[:, None]
    causal = causal[:, None, None, :]
    fresh_scores = jnp.where(causal, fresh_scores, NEGATIVE)
    fresh_max = jnp.max(fresh_scores, axis=-1)
    fresh_weights = jnp.where(causal, jnp.exp(fresh_scores - fresh_max[..., None]), 0.0)
    fresh_total = jnp.sum(fresh_weights, axis=-1)
    fresh_summed = jnp.einsum(
        "trgu,urd->trgd",
        fresh_weights.astype(jnp.bfloat16),
        fresh_values,
        preferred_element_type=jnp.float32,
    )

    fresh_max, fresh_total = fresh_max.reshape(-1), fresh_total.reshape(-1)
    top = jnp.maximum(jnp.max(highest, axis=0), fresh_max)
    share = jnp.exp(highest - top[None])
    fresh_share = jnp.exp(fresh_max - top)
    norm = 1.0 / (jnp.sum(total * share, axis=0) + fresh_total * fresh_share)
    share, fresh_share = share * norm, fresh_share * norm
    attention = fresh_summed.reshape(-1, HD) * fresh_share[:, None]
    for k, part in enumerate(to_groups(summed)):
        attention = attention + part.astype(jnp.float32) * share[k][:, None]
    attention = attention.astype(jnp.bfloat16).reshape(step_count, per_group, group_size * HD)
    by_owner = from_all(attention, "rep")
    attention = jnp.concatenate(
        [
            functools.reduce(
                lambda out, k: jnp.where((my_owner - k) % owners == head, by_owner[k], out),
                range(1, owners),
                by_owner[0],
            )
            for head in range(owners)
        ],
        axis=2,
    )
    return (kv_cache, smoothing, attention)


def solution(mesh):
    placed = (
        P(("seq", "rep"), None),
        P(("seq", "rep"), "head"),
        P(("seq", "rep"), "head"),
        P(None, "head"),
        P(None, "seq", None, "head"),
        P(None, "seq", "head"),
        P(),
        P(),
    )
    return jax.shard_map(
        on_device,
        mesh=mesh,
        in_specs=placed,
        out_specs=(P(("seq", "rep"), None, "head"), P("head"), P(None, "seq", "head")),
        check_vma=False,
    )
```

```python
import functools

import jax
import jax.numpy as jnp
from jax import lax
from jax.experimental import pallas as pl
from jax.experimental.pallas import tpu as pltpu
from jax.sharding import PartitionSpec as P


KVH = 8
HD = 128
QH = 64
PAGE = 32


EPSILON = 1e-05
NEGATIVE = -1e30
SHORT = 8


def shifted(x, axis, k):
    n = lax.axis_size(axis)
    return lax.ppermute(x, axis, [(i, (i + k) % n) for i in range(n)])


def from_all(x, axis):
    n = lax.axis_size(axis)
    if n > SHORT:
        order = (lax.axis_index(axis) - jnp.arange(n)) % n
        return list(lax.all_gather(x, axis)[order])
    return [x] + [shifted(x, axis, k) for k in range(1, n)]


def to_groups(x):
    n = lax.axis_size("seq")
    if n > SHORT:
        me, k = lax.axis_index("seq"), jnp.arange(n)
        back = lax.all_to_all(x[(me - k) % n], "seq", split_axis=0, concat_axis=0)
        return list(back[(me + k) % n])
    return [x[0]] + [shifted(x[k], "seq", -k) for k in range(1, n)]


def project_kernel(count, has_total, info, left, *refs):
    weights, total = refs[:count], refs[count] if has_total else None
    out, held, arrived = refs[-3:]
    depth = held.shape[1]
    copies = [pltpu.make_async_copy(weights[j], held.at[j], arrived.at[j]) for j in range(count)]
    for copy in copies:
        copy.start()
    out[...] = total[...] if has_total else jnp.zeros_like(out)
    for j, copy in enumerate(copies):
        copy.wait()

        @pl.when(info[count + j] == 1)
        def _(j=j):
            block = pl.ds(pl.multiple_of(info[j] * depth, depth), depth)
            out[...] += jnp.dot(left[:, block], held[j], preferred_element_type=jnp.float32)


def project(hidden, total, weights, where, live):
    tokens = hidden.shape[0]
    depth, columns = weights[0].shape
    count = len(weights)
    info = jnp.stack([jnp.asarray(v, jnp.int32) for v in list(where) + list(live)])
    has_total = total is not None
    whole = pl.BlockSpec(memory_space=pltpu.VMEM)
    return pl.pallas_call(
        functools.partial(project_kernel, count, has_total),
        out_shape=jax.ShapeDtypeStruct((tokens, columns), jnp.float32),
        in_specs=[pl.BlockSpec(memory_space=pltpu.SMEM), whole]
        + [pl.BlockSpec(memory_space=pl.ANY)] * count
        + [whole] * has_total,
        out_specs=whole,
        scratch_shapes=[
            pltpu.VMEM((count, depth, columns), weights[0].dtype),
            pltpu.SemaphoreType.DMA((count,)),
        ],
        compiler_params=pltpu.CompilerParams(vmem_limit_bytes=12 * 2**20),
        cost_estimate=pl.CostEstimate(
            flops=2 * tokens * depth * columns * count,
            bytes_accessed=2 * count * depth * (tokens + columns) + 8 * tokens * columns,
            transcendentals=0,
        ),
        input_output_aliases={2 + count: 0} if has_total else {},
        name="project",
    )(info, hidden, *weights, *([total] if has_total else []))


def score_kernel(parts, steps, scale, group, query, smooth, count, *refs):
    keys, (probs, highest, total), scores = refs[:parts], refs[parts:-1], refs[-1]
    tokens = keys[0].shape[0]
    scaled = (query[0].astype(jnp.float32) * smooth[...]).astype(jnp.bfloat16)
    for p in range(parts):
        scores[:, p * tokens : (p + 1) * tokens] = lax.dot_general(
            scaled, keys[p][...], (((1,), (1,)), ((), ())), preferred_element_type=jnp.float32
        )
    requests = count.shape[1]
    rows = scores.shape[0]
    group_rows = rows // (steps * requests)
    pair = 2 if requests % 2 == 0 else 1
    for first in range(0, requests, pair):
        times = jnp.concatenate(
            [
                jnp.broadcast_to(count[0, first + a : first + a + 1, :], (group_rows, parts * tokens))
                for a in range(pair)
            ],
            axis=0,
        )
        for step in range(steps):
            start = (step * requests + first) * group_rows
            at = pl.ds(start, pair * group_rows)
            raw = jnp.where(times > 0.0, scores[at, :] * scale, NEGATIVE)
            top = jnp.max(raw, axis=1, keepdims=True)
            expd = jnp.exp(raw - top)
            highest[0, at, :] = top
            total[0, at, :] = jnp.sum(expd * times, axis=1, keepdims=True)
            probs[0, at, :] = (expd.astype(jnp.bfloat16).astype(jnp.float32) * times).astype(
                jnp.bfloat16
            )


def score(groups, query, smooth, count, keys, steps, scale):
    slots, rows, width = query.shape
    tokens = keys[0].shape[0]
    parts = len(keys)
    requests = count.shape[1]
    slot_spec = pl.BlockSpec((1, rows, 1), lambda k, group: (k, 0, 0))
    return pl.pallas_call(
        functools.partial(score_kernel, parts, steps, scale),
        out_shape=(
            jax.ShapeDtypeStruct((slots, rows, parts * tokens), jnp.bfloat16),
            jax.ShapeDtypeStruct((slots, rows, 1), jnp.float32),
            jax.ShapeDtypeStruct((slots, rows, 1), jnp.float32),
        ),
        grid_spec=pltpu.PrefetchScalarGridSpec(
            num_scalar_prefetch=1,
            grid=(slots,),
            in_specs=[
                pl.BlockSpec((1, rows, width), lambda k, group: (k, 0, 0)),
                pl.BlockSpec((1, width), lambda k, group: (0, 0)),
                pl.BlockSpec((1, requests, parts * tokens), lambda k, group: (group[k], 0, 0)),
            ]
            + [pl.BlockSpec((tokens, width), lambda k, group: (0, 0))] * parts,
            out_specs=(
                pl.BlockSpec((1, rows, parts * tokens), lambda k, group: (k, 0, 0)),
                slot_spec,
                slot_spec,
            ),
            scratch_shapes=[pltpu.VMEM((rows, parts * tokens), jnp.float32)],
        ),
        cost_estimate=pl.CostEstimate(
            flops=2 * slots * rows * width * parts * tokens,
            bytes_accessed=2 * slots * rows * parts * tokens,
            transcendentals=slots * rows * parts * tokens,
        ),
        name="score",
    )(groups, query, smooth, count, *keys)


def weigh_kernel(parts, probs, *refs):
    values, out = refs[:parts], refs[-1]
    tokens = values[0].shape[0]
    out[0] = sum(
        jnp.dot(
            probs[0, :, p * tokens : (p + 1) * tokens],
            values[p][...],
            preferred_element_type=jnp.float32,
        )
        for p in range(parts)
    ).astype(jnp.bfloat16)


def weigh(probs, values):
    slots, rows, _ = probs.shape
    tokens, width = values[0].shape
    parts = len(values)
    return pl.pallas_call(
        functools.partial(weigh_kernel, parts),
        out_shape=jax.ShapeDtypeStruct((slots, rows, width), jnp.bfloat16),
        grid=(slots,),
        in_specs=[pl.BlockSpec((1, rows, parts * tokens), lambda k: (k, 0, 0))]
        + [pl.BlockSpec((tokens, width), lambda k: (0, 0))] * parts,
        out_specs=pl.BlockSpec((1, rows, width), lambda k: (k, 0, 0)),
        cost_estimate=pl.CostEstimate(
            flops=2 * slots * rows * width * parts * tokens,
            bytes_accessed=2 * slots * rows * parts * tokens,
            transcendentals=0,
        ),
        name="weigh",
    )(probs, *values)


def token_counts(page_table, lengths, first_pages, pages_dev):
    slots = page_table.shape[1]
    slot_ids = jnp.arange(slots, dtype=jnp.int32)
    whole_slots, rest = lengths // PAGE, lengths % PAGE
    pages = jnp.concatenate(
        [first + jnp.arange(pages_dev, dtype=jnp.int32) for first in first_pages]
    )
    same = page_table[:, :, None] == pages[None, None, :]
    whole = jnp.sum(same & (slot_ids[None, :] < whole_slots[:, None])[:, :, None], axis=1)
    last = jnp.sum(same & (slot_ids[None, :] == whole_slots[:, None])[:, :, None], axis=1)
    token = jnp.arange(pages.shape[0] * PAGE, dtype=jnp.int32)
    spread = token[None, :] // PAGE == jnp.arange(pages.shape[0], dtype=jnp.int32)[:, None]
    spread = spread.astype(jnp.bfloat16)
    whole = jnp.dot(whole.astype(jnp.bfloat16), spread, preferred_element_type=jnp.float32)
    last = jnp.dot(last.astype(jnp.bfloat16), spread, preferred_element_type=jnp.float32)
    return whole + jnp.where((token % PAGE)[None, :] < rest[:, None], last, 0.0)


def clip_keys(raw, smooth, scale):
    return jnp.clip(raw / smooth, -8.0 * scale[0], 7.0 * scale[0]).astype(jnp.bfloat16)


def clip_values(raw, scale):
    return jnp.clip(raw, -8.0 * scale[1], 7.0 * scale[1]).astype(jnp.bfloat16)


def my_part(x, parts, index, axis):
    size = x.shape[axis] // parts
    pieces = [lax.slice_in_dim(x, p * size, (p + 1) * size, axis=axis) for p in range(parts)]
    out = pieces[0]
    for p in range(1, parts):
        out = jnp.where(index == p, pieces[p], out)
    return out


def line_project(hidden, key_weight, value_weight, raw_query):
    groups, owners = lax.axis_size("seq"), lax.axis_size("rep")
    my_group, my_owner = lax.axis_index("seq"), lax.axis_index("rep")

    def block_of(group, k):
        return jnp.clip(group, 0, groups - 1) * owners + (my_owner - k) % owners

    yes = jnp.int32(1)
    names = ("k", "v")
    moving, arrived, totals = {}, {}, {}

    def send(name, hop):
        left, right = moving[name]
        left = lax.ppermute(left, "seq", [(i, i + 1) for i in range(hop - 1, groups - 1)])
        right = lax.ppermute(right, "seq", [(i, i - 1) for i in range(1, groups - hop + 1)])
        arrived[name] = (left, right)

    def absorb(name, hop):
        left, right = moving[name]
        here = [(my_group - hop, (my_group >= hop).astype(jnp.int32), left)]
        here.append((my_group + hop, (my_group + hop < groups).astype(jnp.int32), right))
        if hop == 0:
            here = [(my_group, yes, left)]
        elif 2 * hop >= groups:
            is_left = my_group >= hop
            here = [
                (
                    jnp.where(is_left, my_group - hop, my_group + hop),
                    here[0][1] + here[1][1],
                    jnp.where(is_left, left, right),
                )
            ]
        passed = [[shifted(block, "rep", k) for _, _, block in here] for k in range(1, owners)]
        for k, blocks in enumerate([[block for _, _, block in here]] + passed):
            totals[name] = project(
                hidden,
                totals.get(name),
                blocks,
                [block_of(group, k) for group, _, _ in here],
                [live for _, live, _ in here],
            )

    moving["k"], moving["v"] = (key_weight,) * 2, (value_weight,) * 2
    for name in names:
        send(name, 1)
        absorb(name, 0)
    queries = None
    for hop in range(1, groups):
        for name in names:
            other = names[1 - names.index(name)]
            moving[name], totals[other] = lax.optimization_barrier((arrived[name], totals[other]))
            if hop < groups - 1:
                send(name, hop + 1)
            if name == "k" and hop == max(1, groups - 2):
                raw_query, moving[name] = lax.optimization_barrier((raw_query, moving[name]))
                queries = jnp.stack(from_all(raw_query, "seq"))
            absorb(name, hop)
    return totals["k"], totals["v"], queries


def on_device(
    hidden, key_weight, value_weight, group_scale, new_kv, decode_query, page_table, lengths
):
    tokens = hidden.shape[0]
    columns = key_weight.shape[1]
    group_size = QH // KVH
    groups, owners = lax.axis_size("seq"), lax.axis_size("rep")
    my_group, my_owner = lax.axis_index("seq"), lax.axis_index("rep")
    assert columns // HD == owners
    pages_dev = tokens // PAGE
    step_count, per_group = decode_query.shape[:2]

    raw_query = my_part(decode_query, owners, my_owner, 2).reshape(-1, HD)

    owner_at = [(my_owner - k) % owners for k in range(owners)]
    if groups > SHORT:
        raw_keys, raw_values = (
            jnp.dot(
                hidden,
                lax.all_gather(weight, ("seq", "rep"), axis=0, tiled=True),
                preferred_element_type=jnp.float32,
            )
            for weight in (key_weight, value_weight)
        )
        queries = jnp.stack(from_all(raw_query, "seq"))
    else:
        raw_keys, raw_values, queries = line_project(hidden, key_weight, value_weight, raw_query)

    local_max = jnp.max(jnp.abs(raw_keys), axis=0, keepdims=True)
    local_max = functools.reduce(jnp.maximum, from_all(local_max, "rep"))
    local_max = functools.reduce(jnp.maximum, from_all(local_max, "seq"))
    smooth = jnp.sqrt(local_max + EPSILON)
    smoothing = smooth.reshape(-1)
    keys = clip_keys(raw_keys, smooth, group_scale)
    values = clip_values(raw_values, group_scale)
    kv_cache = jnp.stack([keys, values], axis=1)

    def by_head(x):
        return [my_part(x, owners, my_owner, 1)] + [
            shifted(my_part(x, owners, (my_owner + k) % owners, 1), "rep", k)
            for k in range(1, owners)
        ]

    my_smooth = my_part(smooth, owners, my_owner, 1)
    first_pages = [(my_group * owners + owner) * pages_dev for owner in owner_at]
    counts = token_counts(page_table, lengths, first_pages, pages_dev)
    counts = counts.reshape(groups, per_group, -1)
    group_at = jnp.stack([(my_group - k) % groups for k in range(groups)])
    score_scale = HD ** (-0.5)
    probs, highest, total = score(
        group_at, queries, my_smooth, counts, by_head(keys), step_count, score_scale
    )
    summed = weigh(probs, by_head(values))
    stats = jnp.stack([highest[..., 0], total[..., 0]], axis=1)

    stats = jnp.stack(to_groups(stats))
    highest, total = stats[:, 0], stats[:, 1]

    shape = (step_count, per_group, group_size, HD)
    query = (raw_query.astype(jnp.float32) * my_smooth).astype(jnp.bfloat16).reshape(shape)
    my_kv = my_part(new_kv, owners, my_owner, 3).astype(jnp.float32)
    my_scale = my_part(group_scale, owners, my_owner, 1)
    fresh_keys = clip_keys(my_kv[:, :, 0], my_smooth, my_scale)
    fresh_values = clip_values(my_kv[:, :, 1], my_scale)
    fresh_scores = (
        jnp.einsum("trgd,urd->trgu", query, fresh_keys, preferred_element_type=jnp.float32)
        * score_scale
    )
    causal = jnp.arange(step_count)[None, :] <= jnp.arange(step_count)[:, None]
    causal = causal[:, None, None, :]
    fresh_scores = jnp.where(causal, fresh_scores, NEGATIVE)
    fresh_max = jnp.max(fresh_scores, axis=-1)
    fresh_weights = jnp.where(causal, jnp.exp(fresh_scores - fresh_max[..., None]), 0.0)
    fresh_total = jnp.sum(fresh_weights, axis=-1)
    fresh_summed = jnp.einsum(
        "trgu,urd->trgd",
        fresh_weights.astype(jnp.bfloat16),
        fresh_values,
        preferred_element_type=jnp.float32,
    )

    fresh_max, fresh_total = fresh_max.reshape(-1), fresh_total.reshape(-1)
    top = jnp.maximum(jnp.max(highest, axis=0), fresh_max)
    share = jnp.exp(highest - top[None])
    fresh_share = jnp.exp(fresh_max - top)
    norm = 1.0 / (jnp.sum(total * share, axis=0) + fresh_total * fresh_share)
    share, fresh_share = share * norm, fresh_share * norm
    attention = fresh_summed.reshape(-1, HD) * fresh_share[:, None]
    for k, part in enumerate(to_groups(summed)):
        attention = attention + part.astype(jnp.float32) * share[k][:, None]
    attention = attention.astype(jnp.bfloat16).reshape(step_count, per_group, group_size * HD)
    by_owner = from_all(attention, "rep")
    attention = jnp.concatenate(
        [
            functools.reduce(
                lambda out, k: jnp.where((my_owner - k) % owners == head, by_owner[k], out),
                range(1, owners),
                by_owner[0],
            )
            for head in range(owners)
        ],
        axis=2,
    )
    return (kv_cache, smoothing, attention)


def solution(mesh):
    placed = (
        P(("seq", "rep"), None),
        P(("seq", "rep"), "head"),
        P(("seq", "rep"), "head"),
        P(None, "head"),
        P(None, "seq", None, "head"),
        P(None, "seq", "head"),
        P(),
        P(),
    )

    return jax.shard_map(
        on_device,
        mesh=mesh,
        in_specs=placed,
        out_specs=(P(("seq", "rep"), None, "head"), P("head"), P(None, "seq", "head")),
        check_vma=False,
    )
```

```python
import functools

import jax
import jax.numpy as jnp
from jax import lax
from jax.experimental import pallas as pl
from jax.experimental.pallas import tpu as pltpu
from jax.sharding import PartitionSpec as P


KVH = 8
HD = 128
QH = 64
PAGE = 32


EPSILON = 1e-05
NEGATIVE = -1e30
SHORT = 8


def shifted(x, axis, k):
    n = lax.axis_size(axis)
    return lax.ppermute(x, axis, [(i, (i + k) % n) for i in range(n)])


def from_all(x, axis):
    n = lax.axis_size(axis)
    if n > SHORT:
        order = (lax.axis_index(axis) - jnp.arange(n)) % n
        return list(lax.all_gather(x, axis)[order])
    return [x] + [shifted(x, axis, k) for k in range(1, n)]


def to_groups(x):
    n = lax.axis_size("seq")
    if n > SHORT:
        me, k = lax.axis_index("seq"), jnp.arange(n)
        back = lax.all_to_all(jnp.stack(x)[(me - k) % n], "seq", split_axis=0, concat_axis=0)
        return list(back[(me + k) % n])
    return [x[0]] + [shifted(x[k], "seq", -k) for k in range(1, n)]


def project_kernel(count, pieces, has_total, info, hidden, *refs):
    weights, total = refs[:count], refs[count] if has_total else None
    out, lefts, rights, left_here, right_here = refs[-5:]
    tokens, depth = lefts.shape[1:]
    tile = tokens // pieces

    def right_copy(j):
        return pltpu.make_async_copy(weights[j], rights.at[j], right_here.at[j])

    def left_copy(j, p):
        rows = pl.ds(p * tile, tile)
        block = pl.ds(pl.multiple_of(info[j] * depth, depth), depth)
        return pltpu.make_async_copy(
            hidden.at[rows, block], lefts.at[j, rows, :], left_here.at[j, p]
        )

    for j in range(count):

        @pl.when(info[count + j] == 1)
        def _(j=j):
            right_copy(j).start()
            for p in range(pieces):
                left_copy(j, p).start()

    out[...] = total[...] if has_total else jnp.zeros_like(out)
    for j in range(count):

        @pl.when(info[count + j] == 1)
        def _(j=j):
            right_copy(j).wait()
            for p in range(pieces):
                rows = pl.ds(p * tile, tile)
                left_copy(j, p).wait()
                out[rows, :] += jnp.dot(
                    lefts[j, rows, :], rights[j], preferred_element_type=jnp.float32
                )


def project(hidden, total, weights, where, live):
    tokens = hidden.shape[0]
    depth, columns = weights[0].shape
    count = len(weights)
    pieces = 4 if tokens % 64 == 0 else 1
    info = jnp.stack([jnp.asarray(v, jnp.int32) for v in list(where) + list(live)])
    has_total = total is not None
    whole = pl.BlockSpec(memory_space=pltpu.VMEM)
    return pl.pallas_call(
        functools.partial(project_kernel, count, pieces, has_total),
        out_shape=jax.ShapeDtypeStruct((tokens, columns), jnp.float32),
        in_specs=[pl.BlockSpec(memory_space=pltpu.SMEM)]
        + [pl.BlockSpec(memory_space=pltpu.HBM)]
        + [pl.BlockSpec(memory_space=pl.ANY)] * count
        + [whole] * has_total,
        out_specs=whole,
        scratch_shapes=[
            pltpu.VMEM((count, tokens, depth), hidden.dtype),
            pltpu.VMEM((count, depth, columns), weights[0].dtype),
            pltpu.SemaphoreType.DMA((count, pieces)),
            pltpu.SemaphoreType.DMA((count,)),
        ],
        compiler_params=pltpu.CompilerParams(vmem_limit_bytes=50 * 2**20),
        cost_estimate=pl.CostEstimate(
            flops=2 * tokens * depth * columns * count,
            bytes_accessed=2 * count * depth * (tokens + columns) + 8 * tokens * columns,
            transcendentals=0,
        ),
        input_output_aliases={2 + count: 0} if has_total else {},
        name="project",
    )(info, hidden, *weights, *([total] if has_total else []))


def score_kernel(slots, parts, steps, scale, group, query, smooth, count, *refs):
    keys, probs, stats = refs[:parts], refs[parts], refs[parts + 1 : parts + 1 + slots]
    scores, tops, sums = refs[-3:]
    tokens = keys[0].shape[0]
    scaled = (query[0].astype(jnp.float32) * smooth[...]).astype(jnp.bfloat16)
    for p in range(parts):
        scores[:, p * tokens : (p + 1) * tokens] = lax.dot_general(
            scaled, keys[p][...], (((1,), (1,)), ((), ())), preferred_element_type=jnp.float32
        )
    requests = count.shape[1]
    rows = scores.shape[0]
    group_rows = rows // (steps * requests)
    pair = 2 if requests % 2 == 0 else 1
    for first in range(0, requests, pair):
        times = jnp.concatenate(
            [
                jnp.broadcast_to(count[0, first + a : first + a + 1, :], (group_rows, parts * tokens))
                for a in range(pair)
            ],
            axis=0,
        )
        bias = jnp.where(times > 0.0, 0.0, NEGATIVE)
        for step in range(steps):
            start = (step * requests + first) * group_rows
            at = pl.ds(start, pair * group_rows)
            raw = scores[at, :] * scale + bias
            top = jnp.max(raw, axis=1, keepdims=True)
            counted = jnp.exp(raw - top) * times
            probs[0, at, :] = counted.astype(jnp.bfloat16)
            tops[at, :] = jnp.broadcast_to(top, (pair * group_rows, 128))
            sums[at, :] = jnp.broadcast_to(
                jnp.sum(counted, axis=1, keepdims=True), (pair * group_rows, 128)
            )
    for slot in range(slots):

        @pl.when(pl.program_id(0) == slot)
        def _(slot=slot):
            stats[slot][0:1, :] = jnp.transpose(tops[...])[0:1, :]
            stats[slot][1:2, :] = jnp.transpose(sums[...])[0:1, :]


def score(groups, query, smooth, count, keys, steps, scale):
    slots, rows, width = query.shape
    tokens = keys[0].shape[0]
    parts = len(keys)
    requests = count.shape[1]
    probs, *stats = pl.pallas_call(
        functools.partial(score_kernel, slots, parts, steps, scale),
        out_shape=[jax.ShapeDtypeStruct((slots, rows, parts * tokens), jnp.bfloat16)]
        + [jax.ShapeDtypeStruct((2, rows), jnp.float32)] * slots,
        grid_spec=pltpu.PrefetchScalarGridSpec(
            num_scalar_prefetch=1,
            grid=(slots,),
            in_specs=[
                pl.BlockSpec((1, rows, width), lambda k, group: (k, 0, 0)),
                pl.BlockSpec((1, width), lambda k, group: (0, 0)),
                pl.BlockSpec((1, requests, parts * tokens), lambda k, group: (group[k], 0, 0)),
            ]
            + [pl.BlockSpec((tokens, width), lambda k, group: (0, 0))] * parts,
            out_specs=[pl.BlockSpec((1, rows, parts * tokens), lambda k, group: (k, 0, 0))]
            + [pl.BlockSpec((2, rows), lambda k, group: (0, 0))] * slots,
            scratch_shapes=[
                pltpu.VMEM((rows, parts * tokens), jnp.float32),
                pltpu.VMEM((rows, 128), jnp.float32),
                pltpu.VMEM((rows, 128), jnp.float32),
            ],
        ),
        compiler_params=pltpu.CompilerParams(vmem_limit_bytes=16 * 2**20),
        cost_estimate=pl.CostEstimate(
            flops=2 * slots * rows * width * parts * tokens,
            bytes_accessed=2 * slots * rows * parts * tokens,
            transcendentals=slots * rows * parts * tokens,
        ),
        name="score",
    )(groups, query, smooth, count, *keys)
    return probs, stats


def weigh_kernel(slots, parts, probs, *refs):
    values, outs = refs[:parts], refs[parts:]
    tokens = values[0].shape[0]
    summed = sum(
        jnp.dot(
            probs[0, :, p * tokens : (p + 1) * tokens],
            values[p][...],
            preferred_element_type=jnp.float32,
        )
        for p in range(parts)
    ).astype(jnp.bfloat16)
    for slot in range(slots):

        @pl.when(pl.program_id(0) == slot)
        def _(slot=slot):
            outs[slot][...] = summed


def weigh(probs, values):
    slots, rows, _ = probs.shape
    tokens, width = values[0].shape
    parts = len(values)
    return pl.pallas_call(
        functools.partial(weigh_kernel, slots, parts),
        out_shape=[jax.ShapeDtypeStruct((rows, width), jnp.bfloat16)] * slots,
        grid=(slots,),
        in_specs=[pl.BlockSpec((1, rows, parts * tokens), lambda k: (k, 0, 0))]
        + [pl.BlockSpec((tokens, width), lambda k: (0, 0))] * parts,
        out_specs=[pl.BlockSpec((rows, width), lambda k: (0, 0))] * slots,
        compiler_params=pltpu.CompilerParams(vmem_limit_bytes=16 * 2**20),
        cost_estimate=pl.CostEstimate(
            flops=2 * slots * rows * width * parts * tokens,
            bytes_accessed=2 * slots * rows * parts * tokens,
            transcendentals=0,
        ),
        name="weigh",
    )(probs, *values)


def token_counts(page_table, lengths, first_pages, pages_dev):
    slots = page_table.shape[1]
    slot_ids = jnp.arange(slots, dtype=jnp.int32)
    whole_slots, rest = lengths // PAGE, lengths % PAGE
    pages = jnp.concatenate(
        [first + jnp.arange(pages_dev, dtype=jnp.int32) for first in first_pages]
    )
    same = page_table[:, :, None] == pages[None, None, :]
    whole = jnp.sum(same & (slot_ids[None, :] < whole_slots[:, None])[:, :, None], axis=1)
    last = jnp.sum(same & (slot_ids[None, :] == whole_slots[:, None])[:, :, None], axis=1)
    token = jnp.arange(pages.shape[0] * PAGE, dtype=jnp.int32)
    spread = token[None, :] // PAGE == jnp.arange(pages.shape[0], dtype=jnp.int32)[:, None]
    spread = spread.astype(jnp.bfloat16)
    whole = jnp.dot(whole.astype(jnp.bfloat16), spread, preferred_element_type=jnp.float32)
    last = jnp.dot(last.astype(jnp.bfloat16), spread, preferred_element_type=jnp.float32)
    return whole + jnp.where((token % PAGE)[None, :] < rest[:, None], last, 0.0)


def clip_keys(raw, smooth, scale):
    return jnp.clip(raw / smooth, -8.0 * scale[0], 7.0 * scale[0]).astype(jnp.bfloat16)


def clip_values(raw, scale):
    return jnp.clip(raw, -8.0 * scale[1], 7.0 * scale[1]).astype(jnp.bfloat16)


def my_part(x, parts, index, axis):
    size = x.shape[axis] // parts
    pieces = [lax.slice_in_dim(x, p * size, (p + 1) * size, axis=axis) for p in range(parts)]
    out = pieces[0]
    for p in range(1, parts):
        out = jnp.where(index == p, pieces[p], out)
    return out


def smooth_of(raw_keys):
    top = jnp.max(jnp.abs(raw_keys), axis=0, keepdims=True)
    top = functools.reduce(jnp.maximum, from_all(top, "rep"))
    top = functools.reduce(jnp.maximum, from_all(top, "seq"))
    return jnp.sqrt(top + EPSILON)


def line_project(hidden, key_weight, value_weight, raw_query):
    groups, owners = lax.axis_size("seq"), lax.axis_size("rep")
    my_group, my_owner = lax.axis_index("seq"), lax.axis_index("rep")

    def block_of(group, k):
        return jnp.clip(group, 0, groups - 1) * owners + (my_owner - k) % owners

    yes = jnp.int32(1)
    names = ("k", "v")
    moving, arrived, totals = {}, {}, {}

    def send(name, hop):
        left, right = moving[name]
        left = lax.ppermute(left, "seq", [(i, i + 1) for i in range(hop - 1, groups - 1)])
        right = lax.ppermute(right, "seq", [(i, i - 1) for i in range(1, groups - hop + 1)])
        arrived[name] = (left, right)

    def absorb(name, hop):
        left, right = moving[name]
        here = [(my_group - hop, (my_group >= hop).astype(jnp.int32), left)]
        here.append((my_group + hop, (my_group + hop < groups).astype(jnp.int32), right))
        if hop == 0:
            here = [(my_group, yes, left)]
        elif 2 * hop >= groups:
            is_left = my_group >= hop
            here = [
                (
                    jnp.where(is_left, my_group - hop, my_group + hop),
                    here[0][1] + here[1][1],
                    jnp.where(is_left, left, right),
                )
            ]
        passed = [[shifted(block, "rep", k) for _, _, block in here] for k in range(1, owners)]
        for k, blocks in enumerate([[block for _, _, block in here]] + passed):
            totals[name] = project(
                hidden,
                totals.get(name),
                blocks,
                [block_of(group, k) for group, _, _ in here],
                [live for _, live, _ in here],
            )

    moving["k"], moving["v"] = (key_weight,) * 2, (value_weight,) * 2
    for name in names:
        send(name, 1)
    queries = from_all(raw_query, "seq")
    for name in names:
        absorb(name, 0)
    for hop in range(1, groups):
        for name in names:
            if name == names[-1] and hop == groups - 1:
                smooth = smooth_of(totals["k"])
                moving[name], smooth = lax.optimization_barrier((arrived[name], smooth))
            else:
                moving[name], totals = lax.optimization_barrier((arrived[name], totals))
            if hop < groups - 1:
                send(name, hop + 1)
            absorb(name, hop)
    return totals["k"], totals["v"], smooth, jnp.stack(queries)


def on_device(
    hidden, key_weight, value_weight, group_scale, new_kv, decode_query, page_table, lengths
):
    tokens = hidden.shape[0]
    columns = key_weight.shape[1]
    group_size = QH // KVH
    groups, owners = lax.axis_size("seq"), lax.axis_size("rep")
    my_group, my_owner = lax.axis_index("seq"), lax.axis_index("rep")
    assert columns // HD == owners
    pages_dev = tokens // PAGE
    step_count, per_group = decode_query.shape[:2]

    raw_query = my_part(decode_query, owners, my_owner, 2).reshape(-1, HD)

    owner_at = [(my_owner - k) % owners for k in range(owners)]
    if groups > SHORT:
        raw_keys, raw_values = (
            jnp.dot(
                hidden,
                lax.all_gather(weight, ("seq", "rep"), axis=0, tiled=True),
                preferred_element_type=jnp.float32,
            )
            for weight in (key_weight, value_weight)
        )
        queries = jnp.stack(from_all(raw_query, "seq"))
        smooth = smooth_of(raw_keys)
    else:
        raw_keys, raw_values, smooth, queries = line_project(hidden, key_weight, value_weight, raw_query)

    def by_head(x):
        return [my_part(x, owners, my_owner, 1)] + [
            shifted(my_part(x, owners, (my_owner + k) % owners, 1), "rep", k)
            for k in range(1, owners)
        ]

    smoothing = smooth.reshape(-1)
    keys = clip_keys(raw_keys, smooth, group_scale)
    head_keys = by_head(keys)
    head_keys, raw_values = lax.optimization_barrier((head_keys, raw_values))
    values = clip_values(raw_values, group_scale)
    kv_cache = jnp.stack([keys, values], axis=1)

    my_smooth = my_part(smooth, owners, my_owner, 1)
    first_pages = [(my_group * owners + owner) * pages_dev for owner in owner_at]
    counts = token_counts(page_table, lengths, first_pages, pages_dev)
    counts = counts.reshape(groups, per_group, -1)
    group_at = jnp.stack([(my_group - k) % groups for k in range(groups)])
    score_scale = HD ** (-0.5)
    probs, stats = score(
        group_at, queries, my_smooth, counts, head_keys, step_count, score_scale
    )
    summed = weigh(probs, by_head(values))
    stats = jnp.stack(to_groups(stats))
    highest, total = stats[:, 0], stats[:, 1]

    shape = (step_count, per_group, group_size, HD)
    query = (raw_query.astype(jnp.float32) * my_smooth).astype(jnp.bfloat16).reshape(shape)
    my_kv = my_part(new_kv, owners, my_owner, 3).astype(jnp.float32)
    my_scale = my_part(group_scale, owners, my_owner, 1)
    fresh_keys = clip_keys(my_kv[:, :, 0], my_smooth, my_scale)
    fresh_values = clip_values(my_kv[:, :, 1], my_scale)
    fresh_scores = (
        jnp.einsum("trgd,urd->trgu", query, fresh_keys, preferred_element_type=jnp.float32)
        * score_scale
    )
    causal = jnp.arange(step_count)[None, :] <= jnp.arange(step_count)[:, None]
    causal = causal[:, None, None, :]
    fresh_scores = jnp.where(causal, fresh_scores, NEGATIVE)
    fresh_max = jnp.max(fresh_scores, axis=-1)
    fresh_weights = jnp.where(causal, jnp.exp(fresh_scores - fresh_max[..., None]), 0.0)
    fresh_total = jnp.sum(fresh_weights, axis=-1)
    fresh_summed = jnp.einsum(
        "trgu,urd->trgd",
        fresh_weights.astype(jnp.bfloat16),
        fresh_values,
        preferred_element_type=jnp.float32,
    )

    fresh_max, fresh_total = fresh_max.reshape(-1), fresh_total.reshape(-1)
    top = jnp.maximum(jnp.max(highest, axis=0), fresh_max)
    share = jnp.exp(highest - top[None])
    fresh_share = jnp.exp(fresh_max - top)
    norm = 1.0 / (jnp.sum(total * share, axis=0) + fresh_total * fresh_share)
    share, fresh_share = share * norm, fresh_share * norm
    attention = fresh_summed.reshape(-1, HD) * fresh_share[:, None]
    summed, kv_cache = lax.optimization_barrier((to_groups(summed), kv_cache))
    for k, part in enumerate(summed):
        attention = attention + part.astype(jnp.float32) * share[k][:, None]
    attention = attention.astype(jnp.bfloat16).reshape(step_count, per_group, group_size * HD)
    by_owner = from_all(attention, "rep")
    attention = jnp.concatenate(
        [
            functools.reduce(
                lambda out, k: jnp.where((my_owner - k) % owners == head, by_owner[k], out),
                range(1, owners),
                by_owner[0],
            )
            for head in range(owners)
        ],
        axis=2,
    )
    return (kv_cache, smoothing, attention)


def solution(mesh):
    placed = (
        P(("seq", "rep"), None),
        P(("seq", "rep"), "head"),
        P(("seq", "rep"), "head"),
        P(None, "head"),
        P(None, "seq", None, "head"),
        P(None, "seq", "head"),
        P(),
        P(),
    )

    return jax.shard_map(
        on_device,
        mesh=mesh,
        in_specs=placed,
        out_specs=(P(("seq", "rep"), None, "head"), P("head"), P(None, "seq", "head")),
        check_vma=False,
    )
```

```python
import functools

import jax
import jax.numpy as jnp
from jax import lax
from jax.experimental import pallas as pl
from jax.experimental.pallas import tpu as pltpu
from jax.sharding import PartitionSpec as P


KVH = 8
HD = 128
QH = 64
PAGE = 32


EPSILON = 1e-05
NEGATIVE = -1e30
SHORT = 8


def shifted(x, axis, k):
    n = lax.axis_size(axis)
    return lax.ppermute(x, axis, [(i, (i + k) % n) for i in range(n)])


def from_all(x, axis):
    n = lax.axis_size(axis)
    if n > SHORT:
        order = (lax.axis_index(axis) - jnp.arange(n)) % n
        return list(lax.all_gather(x, axis)[order])
    return [x] + [shifted(x, axis, k) for k in range(1, n)]


def to_groups(x):
    n = lax.axis_size("seq")
    if n > SHORT:
        me, k = lax.axis_index("seq"), jnp.arange(n)
        back = lax.all_to_all(jnp.stack(x)[(me - k) % n], "seq", split_axis=0, concat_axis=0)
        return list(back[(me + k) % n])
    return [x[0]] + [shifted(x[k], "seq", -k) for k in range(1, n)]


def load_kernel(owners, place, hidden, key_weight, value_weight, held, keys, values, arrived):
    depth = key_weight.shape[0]
    blocks = held.shape[1] // depth

    def block(j):
        index = lax.rem(place[0] * owners + place[1] + j, blocks)
        return pl.ds(pl.multiple_of(index * depth, depth), depth)

    def copy(j):
        return pltpu.make_async_copy(hidden.at[:, block(j)], held.at[:, block(j)], arrived.at[j])

    for j in range(blocks):
        copy(j).start()
    copy(0).wait()
    for weight, out in ((key_weight, keys), (value_weight, values)):
        out[...] = jnp.dot(held[:, block(0)], weight[...], preferred_element_type=jnp.float32)
    for j in range(1, blocks):
        copy(j).wait()


def load(hidden, key_weight, value_weight, place, owners):
    tokens, width = hidden.shape
    depth, columns = key_weight.shape
    whole = pl.BlockSpec(memory_space=pltpu.VMEM)
    total = jax.ShapeDtypeStruct((tokens, columns), jnp.float32)
    return pl.pallas_call(
        functools.partial(load_kernel, owners),
        out_shape=(jax.ShapeDtypeStruct(hidden.shape, hidden.dtype), total, total),
        in_specs=[
            pl.BlockSpec(memory_space=pltpu.SMEM),
            pl.BlockSpec(memory_space=pltpu.HBM),
            whole,
            whole,
        ],
        out_specs=(whole,) * 3,
        scratch_shapes=[pltpu.SemaphoreType.DMA((width // depth,))],
        compiler_params=pltpu.CompilerParams(vmem_limit_bytes=36 * 2**20),
        cost_estimate=pl.CostEstimate(
            flops=4 * tokens * depth * columns,
            bytes_accessed=2 * tokens * width,
            transcendentals=0,
        ),
        name="load",
    )(place, hidden, key_weight, value_weight)


def project_kernel(hops, back, groups, owners, place, left, *refs):
    count = len(hops)
    weights, total = refs[:count], refs[count]
    out, held, arrived = refs[-3:]
    depth = held.shape[1]
    copies = [pltpu.make_async_copy(weights[j], held.at[j], arrived.at[j]) for j in range(count)]
    for copy in copies:
        copy.start()
    out[...] = total[...]
    owner = lax.rem(place[1] + owners - back, owners)
    for j, copy in enumerate(copies):
        copy.wait()
        group = place[0] + hops[j][0]
        for hop in hops[j][1:]:
            group = jnp.where((group >= 0) & (group < groups), group, place[0] + hop)

        @pl.when((group >= 0) & (group < groups))
        def _(j=j, group=group):
            block = pl.ds(pl.multiple_of((group * owners + owner) * depth, depth), depth)
            out[...] += jnp.dot(left[:, block], held[j], preferred_element_type=jnp.float32)


def project(hidden, total, weights, place, hops, back, groups, owners):
    tokens = hidden.shape[0]
    depth, columns = weights[0].shape
    count = len(weights)
    whole = pl.BlockSpec(memory_space=pltpu.VMEM)
    return pl.pallas_call(
        functools.partial(project_kernel, hops, back, groups, owners),
        out_shape=jax.ShapeDtypeStruct((tokens, columns), jnp.float32),
        in_specs=[pl.BlockSpec(memory_space=pltpu.SMEM), whole]
        + [pl.BlockSpec(memory_space=pl.ANY)] * count
        + [whole],
        out_specs=whole,
        scratch_shapes=[
            pltpu.VMEM((count, depth, columns), weights[0].dtype),
            pltpu.SemaphoreType.DMA((count,)),
        ],
        compiler_params=pltpu.CompilerParams(vmem_limit_bytes=12 * 2**20),
        cost_estimate=pl.CostEstimate(
            flops=2 * tokens * depth * columns * count,
            bytes_accessed=2 * count * depth * (tokens + columns) + 8 * tokens * columns,
            transcendentals=0,
        ),
        input_output_aliases={2 + count: 0},
        name="project",
    )(place, hidden, *weights, total)


def score_kernel(slots, parts, steps, scale, group, query, smooth, count, *refs):
    keys, probs, stats = refs[:parts], refs[parts], refs[parts + 1 : parts + 1 + slots]
    scores, tops, sums = refs[-3:]
    tokens = keys[0].shape[0]
    scaled = (query[0].astype(jnp.float32) * smooth[...]).astype(jnp.bfloat16)
    for p in range(parts):
        scores[:, p * tokens : (p + 1) * tokens] = lax.dot_general(
            scaled, keys[p][...], (((1,), (1,)), ((), ())), preferred_element_type=jnp.float32
        )
    requests = count.shape[1]
    rows = scores.shape[0]
    group_rows = rows // (steps * requests)
    pair = 2 if requests % 2 == 0 else 1
    for first in range(0, requests, pair):
        times = jnp.concatenate(
            [
                jnp.broadcast_to(count[0, first + a : first + a + 1, :], (group_rows, parts * tokens))
                for a in range(pair)
            ],
            axis=0,
        )
        bias = jnp.where(times > 0.0, 0.0, NEGATIVE)
        for step in range(steps):
            start = (step * requests + first) * group_rows
            at = pl.ds(start, pair * group_rows)
            raw = scores[at, :] * scale + bias
            top = jnp.max(raw, axis=1, keepdims=True)
            counted = jnp.exp(raw - top) * times
            probs[0, at, :] = counted.astype(jnp.bfloat16)
            tops[at, :] = jnp.broadcast_to(top, (pair * group_rows, 128))
            sums[at, :] = jnp.broadcast_to(
                jnp.sum(counted, axis=1, keepdims=True), (pair * group_rows, 128)
            )
    for slot in range(slots):

        @pl.when(pl.program_id(0) == slot)
        def _(slot=slot):
            stats[slot][0:1, :] = jnp.transpose(tops[...])[0:1, :]
            stats[slot][1:2, :] = jnp.transpose(sums[...])[0:1, :]


def score(groups, query, smooth, count, keys, steps, scale):
    slots, rows, width = query.shape
    tokens = keys[0].shape[0]
    parts = len(keys)
    requests = count.shape[1]
    probs, *stats = pl.pallas_call(
        functools.partial(score_kernel, slots, parts, steps, scale),
        out_shape=[jax.ShapeDtypeStruct((slots, rows, parts * tokens), jnp.bfloat16)]
        + [jax.ShapeDtypeStruct((2, rows), jnp.float32)] * slots,
        grid_spec=pltpu.PrefetchScalarGridSpec(
            num_scalar_prefetch=1,
            grid=(slots,),
            in_specs=[
                pl.BlockSpec((1, rows, width), lambda k, group: (k, 0, 0)),
                pl.BlockSpec((1, width), lambda k, group: (0, 0)),
                pl.BlockSpec((1, requests, parts * tokens), lambda k, group: (group[k], 0, 0)),
            ]
            + [pl.BlockSpec((tokens, width), lambda k, group: (0, 0))] * parts,
            out_specs=[pl.BlockSpec((1, rows, parts * tokens), lambda k, group: (k, 0, 0))]
            + [pl.BlockSpec((2, rows), lambda k, group: (0, 0))] * slots,
            scratch_shapes=[
                pltpu.VMEM((rows, parts * tokens), jnp.float32),
                pltpu.VMEM((rows, 128), jnp.float32),
                pltpu.VMEM((rows, 128), jnp.float32),
            ],
        ),
        compiler_params=pltpu.CompilerParams(vmem_limit_bytes=16 * 2**20),
        cost_estimate=pl.CostEstimate(
            flops=2 * slots * rows * width * parts * tokens,
            bytes_accessed=2 * slots * rows * parts * tokens,
            transcendentals=slots * rows * parts * tokens,
        ),
        name="score",
    )(groups, query, smooth, count, *keys)
    return probs, stats


def thirds(x):
    out = []
    for _ in range(3):
        out.append(x.astype(jnp.bfloat16))
        x = x - out[-1].astype(jnp.float32)
    return out


def weigh_kernel(slots, parts, probs, *refs):
    values, stats, outs = refs[:parts], refs[parts : parts + slots], refs[parts + slots :]
    tokens, width = values[0].shape
    rows = probs.shape[1]
    summed = sum(
        jnp.dot(
            probs[0, :, p * tokens : (p + 1) * tokens],
            values[p][...],
            preferred_element_type=jnp.float32,
        )
        for p in range(parts)
    ).astype(jnp.bfloat16)
    for slot in range(slots):

        @pl.when(pl.program_id(0) == slot)
        def _(slot=slot):
            outs[slot][0:rows, :] = summed
            lines = []
            for third in thirds(stats[slot][...]):
                third = third.astype(jnp.float32)
                lines += [third[:, c : c + width] for c in range(0, rows, width)]
            tail = outs[slot].shape[0] - rows
            lines.append(jnp.zeros((tail - 2 * len(lines), width), jnp.float32))
            outs[slot][rows:, :] = jnp.concatenate(lines, axis=0).astype(jnp.bfloat16)


def packed_rows(rows, width):
    return rows + (6 * (rows // width) // 16 + 1) * 16


def weigh(probs, values, stats):
    slots, rows, _ = probs.shape
    tokens, width = values[0].shape
    parts = len(values)
    total_rows = packed_rows(rows, width)
    return pl.pallas_call(
        functools.partial(weigh_kernel, slots, parts),
        out_shape=[jax.ShapeDtypeStruct((total_rows, width), jnp.bfloat16)] * slots,
        grid=(slots,),
        in_specs=[pl.BlockSpec((1, rows, parts * tokens), lambda k: (k, 0, 0))]
        + [pl.BlockSpec((tokens, width), lambda k: (0, 0))] * parts
        + [pl.BlockSpec((2, rows), lambda k: (0, 0))] * slots,
        out_specs=[pl.BlockSpec((total_rows, width), lambda k: (0, 0))] * slots,
        compiler_params=pltpu.CompilerParams(vmem_limit_bytes=16 * 2**20),
        cost_estimate=pl.CostEstimate(
            flops=2 * slots * rows * width * parts * tokens,
            bytes_accessed=2 * slots * rows * parts * tokens,
            transcendentals=0,
        ),
        name="weigh",
    )(probs, *values, *stats)


def fresh_kernel(scale, query, smooth, new_keys, new_values, group_scale, summed, highest, total):
    steps, requests, width = new_keys.shape
    group_rows = query.shape[0] // (steps * requests)
    rows = requests * group_rows
    scaled = (query[...].astype(jnp.float32) * smooth[...]).astype(jnp.bfloat16)
    scaled = scaled.astype(jnp.float32)

    def by_row(x):
        x = x.astype(jnp.bfloat16).astype(jnp.float32)
        spread = [jnp.broadcast_to(x[r : r + 1], (group_rows, width)) for r in range(requests)]
        return jnp.concatenate(spread, axis=0)

    def clip(x, row):
        limit = group_scale[row : row + 1, :]
        return jnp.clip(x, -8.0 * limit, 7.0 * limit)

    keys = [by_row(clip(new_keys[u] / smooth[...], 0)) for u in range(steps)]
    values = [by_row(clip(new_values[u], 1)) for u in range(steps)]
    for step in range(steps):
        at = pl.ds(step * rows, rows)
        mine = scaled[step * rows : (step + 1) * rows]
        scores = [
            jnp.sum(mine * keys[u], axis=1, keepdims=True) * scale for u in range(step + 1)
        ]
        top = functools.reduce(jnp.maximum, scores)
        expd = [jnp.exp(score - top) for score in scores]
        highest[at, :] = jnp.broadcast_to(top, (rows, width))
        total[at, :] = jnp.broadcast_to(sum(expd), (rows, width))
        summed[at, :] = sum(
            e.astype(jnp.bfloat16).astype(jnp.float32) * value for e, value in zip(expd, values)
        )


def fresh(query, smooth, new_keys, new_values, group_scale, scale):
    return pl.pallas_call(
        functools.partial(fresh_kernel, scale),
        out_shape=(jax.ShapeDtypeStruct(query.shape, jnp.float32),) * 3,
        compiler_params=pltpu.CompilerParams(vmem_limit_bytes=16 * 2**20),
        name="fresh",
    )(query, smooth, new_keys, new_values, group_scale)


def finish_kernel(slots, *refs):
    messages, (summed, highest, total, out) = refs[:slots], refs[slots:]
    rows, width = out.shape
    pieces = rows // width
    tails = [message[rows:, :].astype(jnp.float32) for message in messages]

    def column(slot, piece, which):
        lines = [tails[slot][2 * (j * pieces + piece) + which :][:1] for j in range(3)]
        return jnp.transpose(jnp.broadcast_to(lines[0] + lines[1] + lines[2], (width, width)))

    for piece in range(pieces):
        at = pl.ds(piece * width, width)
        parts = [
            (messages[k][at, :].astype(jnp.float32), column(k, piece, 0), column(k, piece, 1))
            for k in range(slots)
        ]
        parts.append((summed[at, :], highest[at, :], total[at, :]))
        top = functools.reduce(jnp.maximum, [part[1] for part in parts])
        shares = [jnp.exp(part[1] - top) for part in parts]
        norm = sum(share * part[2] for share, part in zip(shares, parts))
        out[at, :] = (sum(share * part[0] for share, part in zip(shares, parts)) / norm).astype(
            out.dtype
        )


def finish(messages, own):
    return pl.pallas_call(
        functools.partial(finish_kernel, len(messages)),
        out_shape=jax.ShapeDtypeStruct(own[0].shape, jnp.bfloat16),
        compiler_params=pltpu.CompilerParams(vmem_limit_bytes=16 * 2**20),
        name="finish",
    )(*messages, *own)


def token_counts(page_table, lengths, first_pages, pages_dev):
    slots = page_table.shape[1]
    slot_ids = jnp.arange(slots, dtype=jnp.int32)
    whole_slots, rest = lengths // PAGE, lengths % PAGE
    pages = jnp.concatenate(
        [first + jnp.arange(pages_dev, dtype=jnp.int32) for first in first_pages]
    )
    same = page_table[:, :, None] == pages[None, None, :]
    whole = jnp.sum(same & (slot_ids[None, :] < whole_slots[:, None])[:, :, None], axis=1)
    last = jnp.sum(same & (slot_ids[None, :] == whole_slots[:, None])[:, :, None], axis=1)
    token = jnp.arange(pages.shape[0] * PAGE, dtype=jnp.int32)
    spread = token[None, :] // PAGE == jnp.arange(pages.shape[0], dtype=jnp.int32)[:, None]
    spread = spread.astype(jnp.bfloat16)
    whole = jnp.dot(whole.astype(jnp.bfloat16), spread, preferred_element_type=jnp.float32)
    last = jnp.dot(last.astype(jnp.bfloat16), spread, preferred_element_type=jnp.float32)
    return whole + jnp.where((token % PAGE)[None, :] < rest[:, None], last, 0.0)


def clip_keys(raw, smooth, scale):
    return jnp.clip(raw / smooth, -8.0 * scale[0], 7.0 * scale[0]).astype(jnp.bfloat16)


def clip_values(raw, scale):
    return jnp.clip(raw, -8.0 * scale[1], 7.0 * scale[1]).astype(jnp.bfloat16)


def my_part(x, axis, owner_is, ahead=0):
    owners = len(owner_is)
    size = x.shape[axis] // owners
    pieces = [lax.slice_in_dim(x, p * size, (p + 1) * size, axis=axis) for p in range(owners)]
    out = pieces[0]
    for p in range(1, owners):
        out = jnp.where(owner_is[(p - ahead) % owners], pieces[p], out)
    return out


def smooth_of(raw_keys):
    top = jnp.max(jnp.abs(raw_keys), axis=0, keepdims=True)
    top = functools.reduce(jnp.maximum, from_all(top, "rep"))
    top = functools.reduce(jnp.maximum, from_all(top, "seq"))
    return jnp.sqrt(top + EPSILON)


def line_project(hidden, key_weight, value_weight, raw_query, early):
    groups, owners = lax.axis_size("seq"), lax.axis_size("rep")
    names = ("k", "v")
    moving, arrived, totals = {}, {}, {}

    def send(name, hop):
        left, right = moving[name]
        left = lax.ppermute(left, "seq", [(i, i + 1) for i in range(hop - 1, groups - 1)])
        right = lax.ppermute(right, "seq", [(i, i - 1) for i in range(1, groups - hop + 1)])
        arrived[name] = (left, right)

    def absorb(name, hop):
        left, right = moving[name]
        if hop == 0:
            here = [((0,), left)]
        elif 2 * hop >= groups:
            here = [((-hop, hop), left + right)]
        else:
            here = [((-hop,), left), ((hop,), right)]
        blocks = [block for _, block in here]
        passed = [[shifted(block, "rep", k) for block in blocks] for k in range(1, owners)]
        for k, ready in enumerate([blocks] + passed):
            if hop == 0 and k == 0:
                continue
            totals[name] = project(
                hidden,
                totals[name],
                ready,
                early[0],
                tuple(hops for hops, _ in here),
                k,
                groups,
                owners,
            )

    moving["k"], moving["v"] = (key_weight,) * 2, (value_weight,) * 2
    for name in names:
        send(name, 1)
    queries = from_all(raw_query, "seq")
    early, first = lax.optimization_barrier((early, (key_weight, value_weight)))
    hidden, totals["k"], totals["v"] = load(hidden, *first, early[0], owners)
    for name in names:
        absorb(name, 0)
    for hop in range(1, groups):
        for name in names:
            if name == names[-1] and hop == groups - 1:
                smooth = smooth_of(totals["k"])
                moving[name], smooth = lax.optimization_barrier((arrived[name], smooth))
            else:
                moving[name], totals = lax.optimization_barrier((arrived[name], totals))
            if hop < groups - 1:
                send(name, hop + 1)
            absorb(name, hop)
    return totals["k"], totals["v"], smooth, queries, early


def on_device(
    hidden, key_weight, value_weight, group_scale, new_kv, decode_query, page_table, lengths
):
    tokens = hidden.shape[0]
    columns = key_weight.shape[1]
    group_size = QH // KVH
    groups, owners = lax.axis_size("seq"), lax.axis_size("rep")
    my_group, my_owner = lax.axis_index("seq"), lax.axis_index("rep")
    assert columns // HD == owners
    pages_dev = tokens // PAGE
    step_count, per_group = decode_query.shape[:2]

    owner_is = [my_owner == owner for owner in range(owners)]
    raw_query = my_part(decode_query, 2, owner_is).reshape(1, -1, HD)

    first_pages = [
        (my_group * owners + (my_owner - k) % owners) * pages_dev for k in range(owners)
    ]
    counts = token_counts(page_table, lengths, first_pages, pages_dev)
    my_kv = my_part(new_kv, 3, owner_is).astype(jnp.float32)
    early = (
        jnp.stack([my_group, my_owner]),
        owner_is,
        counts.reshape(groups, per_group, -1),
        (my_group - jnp.arange(groups, dtype=jnp.int32)) % groups,
        (my_kv[:, :, 0], my_kv[:, :, 1], my_part(group_scale, 1, owner_is)),
    )
    if groups > SHORT:
        raw_keys, raw_values = (
            jnp.dot(
                hidden,
                lax.all_gather(weight, ("seq", "rep"), axis=0, tiled=True),
                preferred_element_type=jnp.float32,
            )
            for weight in (key_weight, value_weight)
        )
        queries = from_all(raw_query, "seq")
        smooth = smooth_of(raw_keys)
    else:
        raw_keys, raw_values, smooth, queries, early = line_project(
            hidden, key_weight, value_weight, raw_query, early
        )
    _, owner_is, counts, group_at, my_new = early

    def by_head(x):
        return [my_part(x, 1, owner_is)] + [
            shifted(my_part(x, 1, owner_is, k), "rep", k) for k in range(1, owners)
        ]

    smoothing = smooth.reshape(-1)
    my_smooth = my_part(smooth, 1, owner_is)
    keys = clip_keys(raw_keys, smooth, group_scale)
    head_keys, raw_values = lax.optimization_barrier((by_head(keys), raw_values))
    values = clip_values(raw_values, group_scale)
    score_scale = HD ** (-0.5)
    probs, stats = score(
        group_at,
        jnp.concatenate(queries),
        my_smooth,
        counts,
        head_keys,
        step_count,
        score_scale,
    )
    messages = weigh(probs, by_head(values), stats)

    messages, keys, values, late = lax.optimization_barrier(
        (messages, keys, values, (raw_query, my_smooth))
    )
    messages = to_groups(messages)
    kv_cache = jnp.stack([keys, values], axis=1)
    own = fresh(late[0].reshape(-1, HD), late[1], *my_new, score_scale)
    messages, kv_cache, own = lax.optimization_barrier((messages, kv_cache, own))
    attention = finish(messages, own).reshape(step_count, per_group, group_size * HD)
    by_owner = from_all(attention, "rep")
    attention = jnp.concatenate(
        [
            functools.reduce(
                lambda out, k: jnp.where(owner_is[(head + k) % owners], by_owner[k], out),
                range(1, owners),
                by_owner[0],
            )
            for head in range(owners)
        ],
        axis=2,
    )
    return (kv_cache, smoothing, attention)


def solution(mesh):
    placed = (
        P(("seq", "rep"), None),
        P(("seq", "rep"), "head"),
        P(("seq", "rep"), "head"),
        P(None, "head"),
        P(None, "seq", None, "head"),
        P(None, "seq", "head"),
        P(),
        P(),
    )

    return jax.shard_map(
        on_device,
        mesh=mesh,
        in_specs=placed,
        out_specs=(P(("seq", "rep"), None, "head"), P("head"), P(None, "seq", "head")),
        check_vma=False,
    )
```

```python
import functools

import jax
import jax.numpy as jnp
from jax import lax
from jax.experimental import pallas as pl
from jax.experimental.layout import Layout, with_layout_constraint
from jax.experimental.pallas import tpu as pltpu
from jax.sharding import PartitionSpec as P


HD = 128
PAGE = 32


EPSILON = 1e-05
NEGATIVE = -1e30
SHORT = 8


def shifted(x, axis, k):
    n = lax.axis_size(axis)
    return lax.ppermute(x, axis, [(i, (i + k) % n) for i in range(n)])


def from_all(x, axis):
    n = lax.axis_size(axis)
    if n > SHORT:
        order = (lax.axis_index(axis) - jnp.arange(n)) % n
        return list(lax.all_gather(x, axis)[order])
    return [x] + [shifted(x, axis, k) for k in range(1, n)]


def to_groups(x):
    n = lax.axis_size("seq")
    if n > SHORT:
        me, k = lax.axis_index("seq"), jnp.arange(n)
        back = lax.all_to_all(jnp.stack(x)[(me - k) % n], "seq", split_axis=0, concat_axis=0)
        return list(back[(me + k) % n])
    return [x[0]] + [shifted(x[k], "seq", -k) for k in range(1, n)]


def load_kernel(owners, place, hidden, *refs):
    weights, (held, keys, values, taken, arrived, taken_arrived) = refs[:2], refs[2:]
    depth = taken.shape[1]
    blocks = held.shape[1] // depth
    takes = [
        pltpu.make_async_copy(weight, taken.at[j], taken_arrived.at[j])
        for j, weight in enumerate(weights)
    ]

    def block(j):
        index = lax.rem(place[0] * owners + place[1] + j, blocks)
        return pl.ds(pl.multiple_of(index * depth, depth), depth)

    def copy(j):
        return pltpu.make_async_copy(hidden.at[:, block(j)], held.at[:, block(j)], arrived.at[j])

    copy(0).start()
    for take in takes:
        take.start()
    for j in range(1, blocks):
        copy(j).start()
    copy(0).wait()
    for j, out in enumerate((keys, values)):
        takes[j].wait()
        out[...] = jnp.dot(held[:, block(0)], taken[j], preferred_element_type=jnp.float32)
    for j in range(1, blocks):
        copy(j).wait()


def load(hidden, key_weight, value_weight, place, owners):
    tokens, width = hidden.shape
    depth, columns = key_weight.shape
    whole = pl.BlockSpec(memory_space=pltpu.VMEM)
    total = jax.ShapeDtypeStruct((tokens, columns), jnp.float32)
    return pl.pallas_call(
        functools.partial(load_kernel, owners),
        out_shape=(jax.ShapeDtypeStruct(hidden.shape, hidden.dtype), total, total),
        in_specs=[
            pl.BlockSpec(memory_space=pltpu.SMEM),
            pl.BlockSpec(memory_space=pltpu.HBM),
            pl.BlockSpec(memory_space=pl.ANY),
            pl.BlockSpec(memory_space=pl.ANY),
        ],
        out_specs=(whole,) * 3,
        scratch_shapes=[
            pltpu.VMEM((2, depth, columns), key_weight.dtype),
            pltpu.SemaphoreType.DMA((width // depth,)),
            pltpu.SemaphoreType.DMA((2,)),
        ],
        compiler_params=pltpu.CompilerParams(vmem_limit_bytes=30 * 2**20),
        cost_estimate=pl.CostEstimate(
            flops=4 * tokens * depth * columns,
            bytes_accessed=2 * tokens * width,
            transcendentals=0,
        ),
        name="load",
    )(place, hidden, key_weight, value_weight)


def project_kernel(hops, back, groups, owners, place, left, *refs):
    count = len(hops)
    weights, total = refs[:count], refs[count]
    out, held, arrived = refs[-3:]
    depth = held.shape[1]
    copies = [
        pltpu.make_async_copy(weights[j].at[pl.ds(0, depth)], held.at[j], arrived.at[j])
        for j in range(count)
    ]
    for copy in copies:
        copy.start()
    out[...] = total[...]
    owner = lax.rem(place[1] + owners - back, owners)
    for j, copy in enumerate(copies):
        copy.wait()
        group = place[0] + hops[j][0]
        for hop in hops[j][1:]:
            group = jnp.where((group >= 0) & (group < groups), group, place[0] + hop)

        @pl.when((group >= 0) & (group < groups))
        def _(j=j, group=group):
            block = pl.ds(pl.multiple_of((group * owners + owner) * depth, depth), depth)
            out[...] += jnp.dot(left[:, block], held[j], preferred_element_type=jnp.float32)


def project(hidden, total, weights, depth, place, hops, back, groups, owners):
    tokens = hidden.shape[0]
    columns = weights[0].shape[1]
    count = len(weights)
    whole = pl.BlockSpec(memory_space=pltpu.VMEM)
    return pl.pallas_call(
        functools.partial(project_kernel, hops, back, groups, owners),
        out_shape=jax.ShapeDtypeStruct((tokens, columns), jnp.float32),
        in_specs=[pl.BlockSpec(memory_space=pltpu.SMEM), whole]
        + [pl.BlockSpec(memory_space=pl.ANY)] * count
        + [whole],
        out_specs=whole,
        scratch_shapes=[
            pltpu.VMEM((count, depth, columns), weights[0].dtype),
            pltpu.SemaphoreType.DMA((count,)),
        ],
        compiler_params=pltpu.CompilerParams(vmem_limit_bytes=12 * 2**20),
        cost_estimate=pl.CostEstimate(
            flops=2 * tokens * depth * columns * count,
            bytes_accessed=2 * count * depth * (tokens + columns) + 8 * tokens * columns,
            transcendentals=0,
        ),
        input_output_aliases={2 + count: 0},
        name="project",
    )(place, hidden, *weights, total)


def score_kernel(slots, parts, steps, scale, group, query, smooth, count, *refs):
    keys, probs, stats = refs[:parts], refs[parts], refs[parts + 1 : parts + 1 + slots]
    scores, tops, sums = refs[-3:]
    tokens = keys[0].shape[0]
    width = keys[0].shape[1]
    requests = count.shape[1]
    rows = scores.shape[0]
    heads = query.shape[1] * query.shape[2] // (steps * requests * width)
    per_line = query.shape[2] // width
    raw = [
        query[0][
            (head // per_line) * steps * requests : (head // per_line + 1) * steps * requests,
            (head % per_line) * width : (head % per_line + 1) * width,
        ]
        for head in range(heads)
    ]
    raw = jnp.concatenate(raw, axis=0)
    scaled = (raw.astype(jnp.float32) * smooth[...]).astype(jnp.bfloat16)
    for p in range(parts):
        scores[:, p * tokens : (p + 1) * tokens] = lax.dot_general(
            scaled, keys[p][...], (((1,), (1,)), ((), ())), preferred_element_type=jnp.float32
        )
    again = 2 if (rows // requests) % 2 == 0 else 1
    times = jnp.concatenate([count[0]] * again, axis=0)
    bias = jnp.where(times > 0.0, 0.0, NEGATIVE)
    for start in range(0, rows, again * requests):
        at = pl.ds(start, again * requests)
        raw = scores[at, :] * scale + bias
        top = jnp.max(raw, axis=1, keepdims=True)
        counted = jnp.exp(raw - top) * times
        probs[0, at, :] = counted.astype(jnp.bfloat16)
        tops[at, :] = jnp.broadcast_to(top, (again * requests, 128))
        sums[at, :] = jnp.broadcast_to(
            jnp.sum(counted, axis=1, keepdims=True), (again * requests, 128)
        )
    for slot in range(slots):

        @pl.when(pl.program_id(0) == slot)
        def _(slot=slot):
            stats[slot][0:1, :] = jnp.transpose(tops[...])[0:1, :]
            stats[slot][1:2, :] = jnp.transpose(sums[...])[0:1, :]


def score(groups, query, smooth, count, keys, steps, scale):
    slots, packed, columns = query.shape
    tokens, width = keys[0].shape
    rows = packed * columns // width
    parts = len(keys)
    requests = count.shape[1]
    probs, *stats = pl.pallas_call(
        functools.partial(score_kernel, slots, parts, steps, scale),
        out_shape=[jax.ShapeDtypeStruct((slots, rows, parts * tokens), jnp.bfloat16)]
        + [jax.ShapeDtypeStruct((2, rows), jnp.float32)] * slots,
        grid_spec=pltpu.PrefetchScalarGridSpec(
            num_scalar_prefetch=1,
            grid=(slots,),
            in_specs=[
                pl.BlockSpec((1, packed, columns), lambda k, group: (k, 0, 0)),
                pl.BlockSpec((1, width), lambda k, group: (0, 0)),
                pl.BlockSpec((1, requests, parts * tokens), lambda k, group: (group[k], 0, 0)),
            ]
            + [pl.BlockSpec((tokens, width), lambda k, group: (0, 0))] * parts,
            out_specs=[pl.BlockSpec((1, rows, parts * tokens), lambda k, group: (k, 0, 0))]
            + [pl.BlockSpec((2, rows), lambda k, group: (0, 0))] * slots,
            scratch_shapes=[
                pltpu.VMEM((rows, parts * tokens), jnp.float32),
                pltpu.VMEM((rows, 128), jnp.float32),
                pltpu.VMEM((rows, 128), jnp.float32),
            ],
        ),
        compiler_params=pltpu.CompilerParams(vmem_limit_bytes=16 * 2**20),
        cost_estimate=pl.CostEstimate(
            flops=2 * slots * rows * width * parts * tokens,
            bytes_accessed=2 * slots * rows * parts * tokens,
            transcendentals=slots * rows * parts * tokens,
        ),
        name="score",
    )(groups, query, smooth, count, *keys)
    return probs, stats


def thirds(x):
    out = []
    for _ in range(3):
        out.append(x.astype(jnp.bfloat16))
        x = x - out[-1].astype(jnp.float32)
    return out


def weigh_kernel(slots, parts, probs, *refs):
    values, stats, outs = refs[:parts], refs[parts : parts + slots], refs[parts + slots :]
    tokens, width = values[0].shape
    rows = probs.shape[1]
    summed = sum(
        jnp.dot(
            probs[0, :, p * tokens : (p + 1) * tokens],
            values[p][...],
            preferred_element_type=jnp.float32,
        )
        for p in range(parts)
    ).astype(jnp.bfloat16)
    for slot in range(slots):

        @pl.when(pl.program_id(0) == slot)
        def _(slot=slot):
            outs[slot][0:rows, :] = summed
            lines = []
            for third in thirds(stats[slot][...]):
                third = third.astype(jnp.float32)
                lines += [third[:, c : c + width] for c in range(0, rows, width)]
            tail = outs[slot].shape[0] - rows
            lines.append(jnp.zeros((tail - 2 * len(lines), width), jnp.float32))
            outs[slot][rows:, :] = jnp.concatenate(lines, axis=0).astype(jnp.bfloat16)


def packed_rows(rows, width):
    return rows + (6 * (rows // width) // 16 + 1) * 16


def weigh(probs, values, stats):
    slots, rows, _ = probs.shape
    tokens, width = values[0].shape
    parts = len(values)
    total_rows = packed_rows(rows, width)
    return pl.pallas_call(
        functools.partial(weigh_kernel, slots, parts),
        out_shape=[jax.ShapeDtypeStruct((total_rows, width), jnp.bfloat16)] * slots,
        grid=(slots,),
        in_specs=[pl.BlockSpec((1, rows, parts * tokens), lambda k: (k, 0, 0))]
        + [pl.BlockSpec((tokens, width), lambda k: (0, 0))] * parts
        + [pl.BlockSpec((2, rows), lambda k: (0, 0))] * slots,
        out_specs=[pl.BlockSpec((total_rows, width), lambda k: (0, 0))] * slots,
        compiler_params=pltpu.CompilerParams(vmem_limit_bytes=16 * 2**20),
        cost_estimate=pl.CostEstimate(
            flops=2 * slots * rows * width * parts * tokens,
            bytes_accessed=2 * slots * rows * parts * tokens,
            transcendentals=0,
        ),
        name="weigh",
    )(probs, *values, *stats)


def fresh_kernel(scale, query, smooth, new_keys, new_values, group_scale, summed, highest, total):
    steps, requests, width = new_keys.shape
    lines = steps * requests

    def by_line(x):
        x = x.astype(jnp.bfloat16).astype(jnp.float32)
        return jnp.concatenate([x] * steps, axis=0)

    def clip(x, row):
        limit = group_scale[row : row + 1, :]
        return jnp.clip(x, -8.0 * limit, 7.0 * limit)

    keys = [by_line(clip(new_keys[u] / smooth[...], 0)) for u in range(steps)]
    values = [by_line(clip(new_values[u], 1)) for u in range(steps)]
    line = lax.broadcasted_iota(jnp.int32, (lines, 1), 0)
    seen = [line >= u * requests for u in range(steps)]
    for head in range(query.shape[1] // width):
        at = pl.ds(head * lines, lines)
        mine = query[:, head * width : (head + 1) * width].astype(jnp.float32) * smooth[...]
        mine = mine.astype(jnp.bfloat16).astype(jnp.float32)
        scores = [
            jnp.where(seen[u], jnp.sum(mine * keys[u], axis=1, keepdims=True) * scale, NEGATIVE)
            for u in range(steps)
        ]
        top = functools.reduce(jnp.maximum, scores)
        expd = [jnp.where(seen[u], jnp.exp(scores[u] - top), 0.0) for u in range(steps)]
        highest[at, :] = jnp.broadcast_to(top, (lines, width))
        total[at, :] = jnp.broadcast_to(sum(expd), (lines, width))
        summed[at, :] = sum(
            e.astype(jnp.bfloat16).astype(jnp.float32) * value for e, value in zip(expd, values)
        )


def fresh(query, smooth, new_keys, new_values, group_scale, scale):
    lines, columns = query.shape
    width = smooth.shape[1]
    part = jax.ShapeDtypeStruct((lines * columns // width, width), jnp.float32)
    return pl.pallas_call(
        functools.partial(fresh_kernel, scale),
        out_shape=(part,) * 3,
        compiler_params=pltpu.CompilerParams(vmem_limit_bytes=16 * 2**20),
        name="fresh",
    )(query, smooth, new_keys, new_values, group_scale)


def finish_kernel(slots, *refs):
    messages, (summed, highest, total, out) = refs[:slots], refs[slots:]
    rows, width = summed.shape
    lines = out.shape[0]
    tails = [message[rows:, :].astype(jnp.float32) for message in messages]
    pieces = rows // width

    def column(slot, piece, which):
        row = [tails[slot][2 * (j * pieces + piece) + which :][:1] for j in range(3)]
        return jnp.transpose(jnp.broadcast_to(row[0] + row[1] + row[2], (width, width)))

    for piece in range(pieces):
        at = pl.ds(piece * width, width)
        parts = [
            (messages[k][at, :].astype(jnp.float32), column(k, piece, 0), column(k, piece, 1))
            for k in range(slots)
        ]
        parts.append((summed[at, :], highest[at, :], total[at, :]))
        top = functools.reduce(jnp.maximum, [part[1] for part in parts])
        shares = [jnp.exp(part[1] - top) for part in parts]
        norm = sum(share * part[2] for share, part in zip(shares, parts))
        merged = sum(share * part[0] for share, part in zip(shares, parts)) / norm
        merged = merged.astype(out.dtype)
        for first in range(0, width, lines):
            head = (piece * width + first) // lines
            out[:, head * width : (head + 1) * width] = merged[first : first + lines]


def finish(messages, own, lines):
    rows, width = own[0].shape
    return pl.pallas_call(
        functools.partial(finish_kernel, len(messages)),
        out_shape=jax.ShapeDtypeStruct((lines, rows * width // lines), jnp.bfloat16),
        compiler_params=pltpu.CompilerParams(vmem_limit_bytes=16 * 2**20),
        name="finish",
    )(*messages, *own)


def token_counts(page_table, lengths, first_pages, pages_dev):
    slots = page_table.shape[1]
    slot_ids = jnp.arange(slots, dtype=jnp.int32)
    whole_slots, rest = lengths // PAGE, lengths % PAGE
    pages = jnp.concatenate(
        [first + jnp.arange(pages_dev, dtype=jnp.int32) for first in first_pages]
    )
    same = page_table[:, :, None] == pages[None, None, :]
    whole = jnp.sum(same & (slot_ids[None, :] < whole_slots[:, None])[:, :, None], axis=1)
    last = jnp.sum(same & (slot_ids[None, :] == whole_slots[:, None])[:, :, None], axis=1)
    token = jnp.arange(pages.shape[0] * PAGE, dtype=jnp.int32)
    spread = token[None, :] // PAGE == jnp.arange(pages.shape[0], dtype=jnp.int32)[:, None]
    spread = spread.astype(jnp.bfloat16)
    whole = jnp.dot(whole.astype(jnp.bfloat16), spread, preferred_element_type=jnp.float32)
    last = jnp.dot(last.astype(jnp.bfloat16), spread, preferred_element_type=jnp.float32)
    return whole + jnp.where((token % PAGE)[None, :] < rest[:, None], last, 0.0)


def clip_keys(raw, smooth, scale):
    return jnp.clip(raw / smooth, -8.0 * scale[0], 7.0 * scale[0]).astype(jnp.bfloat16)


def clip_values(raw, scale):
    return jnp.clip(raw, -8.0 * scale[1], 7.0 * scale[1]).astype(jnp.bfloat16)


def my_part(x, axis, owner_is, ahead=0):
    owners = len(owner_is)
    size = x.shape[axis] // owners
    pieces = [lax.slice_in_dim(x, p * size, (p + 1) * size, axis=axis) for p in range(owners)]
    out = pieces[0]
    for p in range(1, owners):
        out = jnp.where(owner_is[(p - ahead) % owners], pieces[p], out)
    return out


def smooth_of(raw_keys):
    top = jnp.max(jnp.abs(raw_keys), axis=0, keepdims=True)
    top = functools.reduce(jnp.maximum, from_all(top, "rep"))
    top = functools.reduce(jnp.maximum, from_all(top, "seq"))
    return jnp.sqrt(top + EPSILON)


def line_project(hidden, key_weight, value_weight, raw_query, early):
    groups, owners = lax.axis_size("seq"), lax.axis_size("rep")
    names = ("k", "v")
    moving, arrived, totals = {}, {}, {}

    def send(name, hop):
        left, right = moving[name]
        left = lax.ppermute(left, "seq", [(i, i + 1) for i in range(hop - 1, groups - 1)])
        right = lax.ppermute(right, "seq", [(i, i - 1) for i in range(1, groups - hop + 1)])
        arrived[name] = (left, right)

    def absorb(name, hop):
        left, right = moving[name]
        if hop == 0:
            here = [((0,), left)]
        elif 2 * hop >= groups:
            here = [((-hop, hop), left + right)]
        else:
            here = [((-hop,), left), ((hop,), right)]
        blocks = [block for _, block in here]
        passed = [[shifted(block, "rep", k) for block in blocks] for k in range(1, owners)]
        for k, ready in enumerate([blocks] + passed):
            if hop == 0 and k == 0:
                continue
            totals[name] = project(
                hidden,
                totals[name],
                ready,
                depth,
                early[0],
                tuple(hops for hops, _ in here),
                k,
                groups,
                owners,
            )

    depth = key_weight.shape[0]
    moving["k"], moving["v"] = (key_weight,) * 2, (jnp.concatenate([value_weight, raw_query]),) * 2
    lefts, rights = [None] * groups, [None] * groups
    for name in names:
        send(name, 1)
    early, first = lax.optimization_barrier((early, (key_weight, value_weight)))
    hidden, totals["k"], totals["v"] = load(hidden, *first, early[0], owners)
    moving["v"] = (value_weight,) * 2
    for name in names:
        absorb(name, 0)
    for hop in range(1, groups):
        for name in names:
            if name == names[-1] and hop == groups - 1:
                smooth = smooth_of(totals["k"])
                moving[name], smooth = lax.optimization_barrier((arrived[name], smooth))
            else:
                moving[name], totals = lax.optimization_barrier((arrived[name], totals))
            if hop < groups - 1:
                send(name, hop + 1)
            absorb(name, hop)
        lefts[hop], rights[groups - hop] = (block[depth:] for block in moving["v"])
    queries = [raw_query] + [lefts[k] + rights[k] for k in range(1, groups)]
    return totals["k"], totals["v"], smooth, queries, early


def on_device(
    hidden, key_weight, value_weight, group_scale, new_kv, decode_query, page_table, lengths
):
    tokens = hidden.shape[0]
    columns = key_weight.shape[1]
    groups, owners = lax.axis_size("seq"), lax.axis_size("rep")
    my_group, my_owner = lax.axis_index("seq"), lax.axis_index("rep")
    assert columns // HD == owners
    pages_dev = tokens // PAGE
    step_count, per_group = decode_query.shape[:2]

    owner_is = [my_owner == owner for owner in range(owners)]
    own_query = my_part(decode_query, 2, owner_is).reshape(step_count * per_group, -1)
    raw_query = jnp.concatenate(jnp.split(own_query, own_query.shape[1] // columns, axis=1))

    first_pages = [
        (my_group * owners + (my_owner - k) % owners) * pages_dev for k in range(owners)
    ]
    early = (
        jnp.stack([my_group, my_owner]),
        owner_is,
        first_pages,
        (my_group - jnp.arange(groups, dtype=jnp.int32)) % groups,
        own_query,
    )
    if groups > SHORT:
        raw_keys, raw_values = (
            jnp.dot(
                hidden,
                lax.all_gather(weight, ("seq", "rep"), axis=0, tiled=True),
                preferred_element_type=jnp.float32,
            )
            for weight in (key_weight, value_weight)
        )
        queries = from_all(raw_query, "seq")
        smooth = smooth_of(raw_keys)
    else:
        raw_keys, raw_values, smooth, queries, early = line_project(
            hidden, key_weight, value_weight, raw_query, early
        )
    _, owner_is, first_pages, group_at, own_query = early
    counts = token_counts(page_table, lengths, first_pages, pages_dev)
    counts = counts.reshape(groups, per_group, -1)
    my_kv = my_part(new_kv, 3, owner_is).astype(jnp.float32)
    my_new = (my_kv[:, :, 0], my_kv[:, :, 1], my_part(group_scale, 1, owner_is))

    def by_head(x):
        return [my_part(x, 1, owner_is)] + [
            shifted(my_part(x, 1, owner_is, k), "rep", k) for k in range(1, owners)
        ]

    smoothing = smooth.reshape(-1)
    my_smooth = my_part(smooth, 1, owner_is)
    keys = clip_keys(raw_keys, smooth, group_scale)
    head_keys, raw_values = lax.optimization_barrier((by_head(keys), raw_values))
    values = clip_values(raw_values, group_scale)
    score_scale = HD ** (-0.5)
    probs, stats = score(
        group_at,
        jnp.stack(queries),
        my_smooth,
        counts,
        head_keys,
        step_count,
        score_scale,
    )
    messages = weigh(probs, by_head(values), stats)

    messages, keys, values, late = lax.optimization_barrier(
        (messages, keys, values, (own_query, my_smooth))
    )
    messages = to_groups(messages)
    kv_cache = with_layout_constraint(jnp.stack([keys, values], axis=1), Layout((0, 1, 2)))
    own = fresh(late[0], late[1], *my_new, score_scale)
    messages, kv_cache, own = lax.optimization_barrier((messages, kv_cache, own))
    attention = finish(messages, own, step_count * per_group)
    by_owner = from_all(attention, "rep")
    attention = jnp.concatenate(
        [
            functools.reduce(
                lambda out, k: jnp.where(owner_is[(head + k) % owners], by_owner[k], out),
                range(1, owners),
                by_owner[0],
            )
            for head in range(owners)
        ],
        axis=1,
    ).reshape(decode_query.shape)
    return (kv_cache, smoothing, attention)


def solution(mesh):
    placed = (
        P(("seq", "rep"), None),
        P(("seq", "rep"), "head"),
        P(("seq", "rep"), "head"),
        P(None, "head"),
        P(None, "seq", None, "head"),
        P(None, "seq", "head"),
        P(),
        P(),
    )

    return jax.shard_map(
        on_device,
        mesh=mesh,
        in_specs=placed,
        out_specs=(P(("seq", "rep"), None, "head"), P("head"), P(None, "seq", "head")),
        check_vma=False,
    )
```

```python
import functools

import jax
import jax.numpy as jnp
from jax import lax
from jax.experimental import pallas as pl
from jax.experimental.layout import Layout, with_layout_constraint
from jax.experimental.pallas import tpu as pltpu
from jax.sharding import PartitionSpec as P


HD = 128
PAGE = 32


EPSILON = 1e-05
NEGATIVE = -1e30
LINE = 4


def shifted(x, axis, k):
    n = lax.axis_size(axis)
    return lax.ppermute(x, axis, [(i, (i + k) % n) for i in range(n)])


def partner(me, k, n):
    return me ^ k if n == LINE else (k - me) % n


def swapped(x, axis, k):
    n = lax.axis_size(axis)
    return lax.ppermute(x, axis, [(i, partner(i, k, n)) for i in range(n)])


def from_owners(x):
    return [x] + [shifted(x, "rep", k) for k in range(1, lax.axis_size("rep"))]


def from_groups(x):
    n = lax.axis_size("seq")
    if n != LINE:
        return list(lax.all_gather(x, "seq")[partner(lax.axis_index("seq"), jnp.arange(n), n)])
    return [x] + [swapped(x, "seq", k) for k in range(1, n)]


def to_groups(x):
    n = lax.axis_size("seq")
    if n != LINE:
        order = partner(lax.axis_index("seq"), jnp.arange(n), n)
        back = lax.all_to_all(jnp.stack(x)[order], "seq", split_axis=0, concat_axis=0)
        return list(back[order])
    return [x[0]] + [swapped(x[k], "seq", k) for k in range(1, n)]


def pack_kernel(weight, query, out, sem):
    depth, columns = weight.shape
    copy = pltpu.make_async_copy(weight, out.at[pl.ds(0, depth)], sem)
    copy.start()
    lines = query.shape[0]
    for k in range(query.shape[1] // columns):
        at = pl.ds(depth + k * lines, lines)
        out[at, :] = query[:, k * columns : (k + 1) * columns]
    copy.wait()


def pack(weight, query):
    depth, columns = weight.shape
    whole = pl.BlockSpec(memory_space=pltpu.VMEM)
    return pl.pallas_call(
        pack_kernel,
        out_shape=jax.ShapeDtypeStruct((depth + query.size // columns, columns), weight.dtype),
        in_specs=[pl.BlockSpec(memory_space=pl.ANY), whole],
        out_specs=whole,
        scratch_shapes=[pltpu.SemaphoreType.DMA],
        compiler_params=pltpu.CompilerParams(vmem_limit_bytes=8 * 2**20),
        name="pack",
    )(weight, query)


def load_kernel(owners, place, hidden, *refs):
    weights, (held, keys, values, taken, arrived, taken_arrived) = refs[:2], refs[2:]
    depth = taken.shape[1]
    blocks = held.shape[1] // depth
    takes = [
        pltpu.make_async_copy(weight, taken.at[j], taken_arrived.at[j])
        for j, weight in enumerate(weights)
    ]

    def block(j):
        index = lax.rem(place[0] * owners + place[1] + j, blocks)
        return pl.ds(pl.multiple_of(index * depth, depth), depth)

    def copy(j):
        return pltpu.make_async_copy(hidden.at[:, block(j)], held.at[:, block(j)], arrived.at[j])

    copy(0).start()
    for take in takes:
        take.start()
    for j in range(1, blocks):
        copy(j).start()
    copy(0).wait()
    for j, out in enumerate((keys, values)):
        takes[j].wait()
        out[...] = jnp.dot(held[:, block(0)], taken[j], preferred_element_type=jnp.float32)
    for j in range(1, blocks):
        copy(j).wait()


def load(hidden, key_weight, value_weight, place, owners):
    tokens, width = hidden.shape
    depth, columns = key_weight.shape
    whole = pl.BlockSpec(memory_space=pltpu.VMEM)
    total = jax.ShapeDtypeStruct((tokens, columns), jnp.float32)
    return pl.pallas_call(
        functools.partial(load_kernel, owners),
        out_shape=(jax.ShapeDtypeStruct(hidden.shape, hidden.dtype), total, total),
        in_specs=[
            pl.BlockSpec(memory_space=pltpu.SMEM),
            pl.BlockSpec(memory_space=pltpu.HBM),
            pl.BlockSpec(memory_space=pl.ANY),
            pl.BlockSpec(memory_space=pl.ANY),
        ],
        out_specs=(whole,) * 3,
        scratch_shapes=[
            pltpu.VMEM((2, depth, columns), key_weight.dtype),
            pltpu.SemaphoreType.DMA((width // depth,)),
            pltpu.SemaphoreType.DMA((2,)),
        ],
        compiler_params=pltpu.CompilerParams(vmem_limit_bytes=30 * 2**20),
        cost_estimate=pl.CostEstimate(
            flops=4 * tokens * depth * columns,
            bytes_accessed=2 * tokens * width,
            transcendentals=0,
        ),
        name="load",
    )(place, hidden, key_weight, value_weight)


def project_kernel(hops, back, groups, owners, place, left, *refs):
    count = len(hops)
    weights, total = refs[:count], refs[count]
    out, held, arrived = refs[-3:]
    depth = held.shape[1]
    copies = [
        pltpu.make_async_copy(weights[j].at[pl.ds(0, depth)], held.at[j], arrived.at[j])
        for j in range(count)
    ]
    for copy in copies:
        copy.start()
    out[...] = total[...]
    owner = lax.rem(place[1] + owners - back, owners)
    for j, copy in enumerate(copies):
        copy.wait()
        group = jnp.int32(-1)
        for parity, hop in hops[j]:
            there = place[0] + jnp.where(lax.rem(place[0], 2) == parity, hop, -hop)
            group = jnp.where((there >= 0) & (there < groups), there, group)

        @pl.when((group >= 0) & (group < groups))
        def _(j=j, group=group):
            block = pl.ds(pl.multiple_of((group * owners + owner) * depth, depth), depth)
            out[...] += jnp.dot(left[:, block], held[j], preferred_element_type=jnp.float32)


def project(hidden, total, weights, depth, place, hops, back, groups, owners):
    tokens = hidden.shape[0]
    columns = weights[0].shape[1]
    count = len(weights)
    whole = pl.BlockSpec(memory_space=pltpu.VMEM)
    return pl.pallas_call(
        functools.partial(project_kernel, hops, back, groups, owners),
        out_shape=jax.ShapeDtypeStruct((tokens, columns), jnp.float32),
        in_specs=[pl.BlockSpec(memory_space=pltpu.SMEM), whole]
        + [pl.BlockSpec(memory_space=pl.ANY)] * count
        + [whole],
        out_specs=whole,
        scratch_shapes=[
            pltpu.VMEM((count, depth, columns), weights[0].dtype),
            pltpu.SemaphoreType.DMA((count,)),
        ],
        compiler_params=pltpu.CompilerParams(vmem_limit_bytes=12 * 2**20),
        cost_estimate=pl.CostEstimate(
            flops=2 * tokens * depth * columns * count,
            bytes_accessed=2 * count * depth * (tokens + columns) + 8 * tokens * columns,
            transcendentals=0,
        ),
        input_output_aliases={2 + count: 0},
        name="project",
    )(place, hidden, *weights, total)


def score_kernel(slots, parts, steps, scale, group, query, smooth, count, *refs):
    keys, probs, stats = refs[:parts], refs[parts], refs[parts + 1 : parts + 1 + slots]
    scores, tops, sums = refs[-3:]
    tokens = keys[0].shape[0]
    width = keys[0].shape[1]
    requests = count.shape[1]
    rows = scores.shape[0]
    heads = query.shape[1] * query.shape[2] // (steps * requests * width)
    per_line = query.shape[2] // width
    raw = [
        query[0][
            (head // per_line) * steps * requests : (head // per_line + 1) * steps * requests,
            (head % per_line) * width : (head % per_line + 1) * width,
        ]
        for head in range(heads)
    ]
    raw = jnp.concatenate(raw, axis=0)
    scaled = (raw.astype(jnp.float32) * smooth[...]).astype(jnp.bfloat16)
    for p in range(parts):
        scores[:, p * tokens : (p + 1) * tokens] = lax.dot_general(
            scaled, keys[p][...], (((1,), (1,)), ((), ())), preferred_element_type=jnp.float32
        )
    again = 2 if (rows // requests) % 2 == 0 else 1
    times = jnp.concatenate([count[0]] * again, axis=0)
    bias = jnp.where(times > 0.0, 0.0, NEGATIVE)
    for start in range(0, rows, again * requests):
        at = pl.ds(start, again * requests)
        raw = scores[at, :] * scale + bias
        top = jnp.max(raw, axis=1, keepdims=True)
        counted = jnp.exp(raw - top) * times
        probs[0, at, :] = counted.astype(jnp.bfloat16)
        tops[at, :] = jnp.broadcast_to(top, (again * requests, 128))
        sums[at, :] = jnp.broadcast_to(
            jnp.sum(counted, axis=1, keepdims=True), (again * requests, 128)
        )
    for slot in range(slots):

        @pl.when(pl.program_id(0) == slot)
        def _(slot=slot):
            stats[slot][0:1, :] = jnp.transpose(tops[...])[0:1, :]
            stats[slot][1:2, :] = jnp.transpose(sums[...])[0:1, :]


def score(groups, query, smooth, count, keys, steps, scale):
    slots, packed, columns = query.shape
    tokens, width = keys[0].shape
    rows = packed * columns // width
    parts = len(keys)
    requests = count.shape[1]
    probs, *stats = pl.pallas_call(
        functools.partial(score_kernel, slots, parts, steps, scale),
        out_shape=[jax.ShapeDtypeStruct((slots, rows, parts * tokens), jnp.bfloat16)]
        + [jax.ShapeDtypeStruct((2, rows), jnp.float32)] * slots,
        grid_spec=pltpu.PrefetchScalarGridSpec(
            num_scalar_prefetch=1,
            grid=(slots,),
            in_specs=[
                pl.BlockSpec((1, packed, columns), lambda k, group: (k, 0, 0)),
                pl.BlockSpec((1, width), lambda k, group: (0, 0)),
                pl.BlockSpec((1, requests, parts * tokens), lambda k, group: (group[k], 0, 0)),
            ]
            + [pl.BlockSpec((tokens, width), lambda k, group: (0, 0))] * parts,
            out_specs=[pl.BlockSpec((1, rows, parts * tokens), lambda k, group: (k, 0, 0))]
            + [pl.BlockSpec((2, rows), lambda k, group: (0, 0))] * slots,
            scratch_shapes=[
                pltpu.VMEM((rows, parts * tokens), jnp.float32),
                pltpu.VMEM((rows, 128), jnp.float32),
                pltpu.VMEM((rows, 128), jnp.float32),
            ],
        ),
        compiler_params=pltpu.CompilerParams(vmem_limit_bytes=16 * 2**20),
        cost_estimate=pl.CostEstimate(
            flops=2 * slots * rows * width * parts * tokens,
            bytes_accessed=2 * slots * rows * parts * tokens,
            transcendentals=slots * rows * parts * tokens,
        ),
        name="score",
    )(groups, query, smooth, count, *keys)
    return probs, stats


def thirds(x):
    out = []
    for _ in range(3):
        out.append(x.astype(jnp.bfloat16))
        x = x - out[-1].astype(jnp.float32)
    return out


def weigh_kernel(slots, parts, probs, *refs):
    values, stats, outs = refs[:parts], refs[parts : parts + slots], refs[parts + slots :]
    tokens, width = values[0].shape
    rows = probs.shape[1]
    summed = sum(
        jnp.dot(
            probs[0, :, p * tokens : (p + 1) * tokens],
            values[p][...],
            preferred_element_type=jnp.float32,
        )
        for p in range(parts)
    ).astype(jnp.bfloat16)
    for slot in range(slots):

        @pl.when(pl.program_id(0) == slot)
        def _(slot=slot):
            outs[slot][0:rows, :] = summed
            lines = []
            for third in thirds(stats[slot][...]):
                third = third.astype(jnp.float32)
                lines += [third[:, c : c + width] for c in range(0, rows, width)]
            tail = outs[slot].shape[0] - rows
            lines.append(jnp.zeros((tail - 2 * len(lines), width), jnp.float32))
            outs[slot][rows:, :] = jnp.concatenate(lines, axis=0).astype(jnp.bfloat16)


def packed_rows(rows, width):
    return rows + (6 * (rows // width) // 16 + 1) * 16


def weigh(probs, values, stats):
    slots, rows, _ = probs.shape
    tokens, width = values[0].shape
    parts = len(values)
    total_rows = packed_rows(rows, width)
    return pl.pallas_call(
        functools.partial(weigh_kernel, slots, parts),
        out_shape=[jax.ShapeDtypeStruct((total_rows, width), jnp.bfloat16)] * slots,
        grid=(slots,),
        in_specs=[pl.BlockSpec((1, rows, parts * tokens), lambda k: (k, 0, 0))]
        + [pl.BlockSpec((tokens, width), lambda k: (0, 0))] * parts
        + [pl.BlockSpec((2, rows), lambda k: (0, 0))] * slots,
        out_specs=[pl.BlockSpec((total_rows, width), lambda k: (0, 0))] * slots,
        compiler_params=pltpu.CompilerParams(vmem_limit_bytes=16 * 2**20),
        cost_estimate=pl.CostEstimate(
            flops=2 * slots * rows * width * parts * tokens,
            bytes_accessed=2 * slots * rows * parts * tokens,
            transcendentals=0,
        ),
        name="weigh",
    )(probs, *values, *stats)


def fresh_kernel(scale, query, smooth, new_keys, new_values, group_scale, summed, highest, total):
    steps, requests, width = new_keys.shape
    lines = steps * requests

    def by_line(x):
        x = x.astype(jnp.bfloat16).astype(jnp.float32)
        return jnp.concatenate([x] * steps, axis=0)

    def clip(x, row):
        limit = group_scale[row : row + 1, :]
        return jnp.clip(x, -8.0 * limit, 7.0 * limit)

    keys = [by_line(clip(new_keys[u] / smooth[...], 0)) for u in range(steps)]
    values = [by_line(clip(new_values[u], 1)) for u in range(steps)]
    line = lax.broadcasted_iota(jnp.int32, (lines, 1), 0)
    seen = [line >= u * requests for u in range(steps)]
    for head in range(query.shape[1] // width):
        at = pl.ds(head * lines, lines)
        mine = query[:, head * width : (head + 1) * width].astype(jnp.float32) * smooth[...]
        mine = mine.astype(jnp.bfloat16).astype(jnp.float32)
        scores = [
            jnp.where(seen[u], jnp.sum(mine * keys[u], axis=1, keepdims=True) * scale, NEGATIVE)
            for u in range(steps)
        ]
        top = functools.reduce(jnp.maximum, scores)
        expd = [jnp.where(seen[u], jnp.exp(scores[u] - top), 0.0) for u in range(steps)]
        highest[at, :] = jnp.broadcast_to(top, (lines, width))
        total[at, :] = jnp.broadcast_to(sum(expd), (lines, width))
        summed[at, :] = sum(
            e.astype(jnp.bfloat16).astype(jnp.float32) * value for e, value in zip(expd, values)
        )


def fresh(query, smooth, new_keys, new_values, group_scale, scale):
    lines, columns = query.shape
    width = smooth.shape[1]
    part = jax.ShapeDtypeStruct((lines * columns // width, width), jnp.float32)
    return pl.pallas_call(
        functools.partial(fresh_kernel, scale),
        out_shape=(part,) * 3,
        compiler_params=pltpu.CompilerParams(vmem_limit_bytes=16 * 2**20),
        name="fresh",
    )(query, smooth, new_keys, new_values, group_scale)


def finish_kernel(slots, *refs):
    messages, (summed, highest, total, out) = refs[:slots], refs[slots:]
    rows, width = summed.shape
    lines = out.shape[0]
    tails = [message[rows:, :].astype(jnp.float32) for message in messages]
    pieces = rows // width

    def column(slot, piece, which):
        row = [tails[slot][2 * (j * pieces + piece) + which :][:1] for j in range(3)]
        return jnp.transpose(jnp.broadcast_to(row[0] + row[1] + row[2], (width, width)))

    for piece in range(pieces):
        at = pl.ds(piece * width, width)
        parts = [
            (messages[k][at, :].astype(jnp.float32), column(k, piece, 0), column(k, piece, 1))
            for k in range(slots)
        ]
        parts.append((summed[at, :], highest[at, :], total[at, :]))
        top = functools.reduce(jnp.maximum, [part[1] for part in parts])
        shares = [jnp.exp(part[1] - top) for part in parts]
        norm = sum(share * part[2] for share, part in zip(shares, parts))
        merged = sum(share * part[0] for share, part in zip(shares, parts)) / norm
        merged = merged.astype(out.dtype)
        for first in range(0, width, lines):
            head = (piece * width + first) // lines
            out[:, head * width : (head + 1) * width] = merged[first : first + lines]


def finish(messages, own, lines):
    rows, width = own[0].shape
    return pl.pallas_call(
        functools.partial(finish_kernel, len(messages)),
        out_shape=jax.ShapeDtypeStruct((lines, rows * width // lines), jnp.bfloat16),
        compiler_params=pltpu.CompilerParams(vmem_limit_bytes=16 * 2**20),
        name="finish",
    )(*messages, *own)


def token_counts(page_table, lengths, first_pages, pages_dev):
    slots = page_table.shape[1]
    slot_ids = jnp.arange(slots, dtype=jnp.int32)
    whole_slots, rest = lengths // PAGE, lengths % PAGE
    pages = jnp.concatenate(
        [first + jnp.arange(pages_dev, dtype=jnp.int32) for first in first_pages]
    )
    same = page_table[:, :, None] == pages[None, None, :]
    whole = jnp.sum(same & (slot_ids[None, :] < whole_slots[:, None])[:, :, None], axis=1)
    last = jnp.sum(same & (slot_ids[None, :] == whole_slots[:, None])[:, :, None], axis=1)
    token = jnp.arange(pages.shape[0] * PAGE, dtype=jnp.int32)
    spread = token[None, :] // PAGE == jnp.arange(pages.shape[0], dtype=jnp.int32)[:, None]
    spread = spread.astype(jnp.bfloat16)
    whole = jnp.dot(whole.astype(jnp.bfloat16), spread, preferred_element_type=jnp.float32)
    last = jnp.dot(last.astype(jnp.bfloat16), spread, preferred_element_type=jnp.float32)
    return whole + jnp.where((token % PAGE)[None, :] < rest[:, None], last, 0.0)


def clip_keys(raw, smooth, scale):
    return jnp.clip(raw / smooth, -8.0 * scale[0], 7.0 * scale[0]).astype(jnp.bfloat16)


def clip_values(raw, scale):
    return jnp.clip(raw, -8.0 * scale[1], 7.0 * scale[1]).astype(jnp.bfloat16)


def my_part(x, axis, owner_is, ahead=0):
    owners = len(owner_is)
    size = x.shape[axis] // owners
    pieces = [lax.slice_in_dim(x, p * size, (p + 1) * size, axis=axis) for p in range(owners)]
    out = pieces[0]
    for p in range(1, owners):
        out = jnp.where(owner_is[(p - ahead) % owners], pieces[p], out)
    return out


def smooth_of(raw_keys):
    top = jnp.max(jnp.abs(raw_keys), axis=0, keepdims=True)
    top = functools.reduce(jnp.maximum, from_owners(top))
    top = functools.reduce(jnp.maximum, from_groups(top))
    return jnp.sqrt(top + EPSILON)


def line_pairs(hop, parity, groups):
    pairs = []
    for i in range(parity, groups - 1, 2):
        if i >= hop - 1:
            pairs.append((i, i + 1))
        if i + hop < groups:
            pairs.append((i + 1, i))
    return pairs


def line_project(hidden, key_weight, value_weight, own_query, early):
    groups, owners = lax.axis_size("seq"), lax.axis_size("rep")
    depth = key_weight.shape[0]
    barrier = lax.optimization_barrier

    def send(x, hop, parity):
        return lax.ppermute(x, "seq", line_pairs(hop, parity, groups))

    def absorb(name, blocks, hops, first=0):
        passed = [[shifted(block, "rep", k) for block in blocks] for k in range(1, owners)]
        for k, ready in enumerate([blocks] + passed):
            if k < first:
                continue
            totals[name] = project(
                hidden, totals[name], ready, depth, early[0], hops, k, groups, owners
            )

    totals = {}
    ka1 = send(key_weight, 1, 0)
    kb1 = send(key_weight, 1, 1)
    value_block = pack(value_weight, own_query)
    va1 = send(value_block, 1, 0)
    early, first = barrier((early, (key_weight, value_weight)))
    hidden, totals["k"], totals["v"] = load(hidden, *first, early[0], owners)
    for name, weight in (("k", key_weight), ("v", value_weight)):
        absorb(name, [weight], (((0, 0),),), 1)

    ka1, kb1, value_block, totals = barrier((ka1, kb1, value_block, totals))
    kb2 = send(ka1, 2, 1)
    ka2 = send(kb1, 2, 0)
    vb1 = send(value_block, 1, 1)
    absorb("k", [ka1, kb1], (((0, 1),), ((1, 1),)))

    kb2, va1, totals = barrier((kb2, va1, totals))
    ka3 = send(kb2, 3, 0)
    vb2 = send(va1, 2, 1)
    absorb("v", [va1], (((0, 1),),))

    ka2, totals = barrier((ka2, totals))
    absorb("k", [ka2 + kb2], (((0, 2), (1, 2)),))

    vb1, totals = barrier((vb1, totals))
    va2 = send(vb1, 2, 0)
    absorb("v", [vb1], (((1, 1),),))

    ka3, totals = barrier((ka3, totals))
    absorb("k", [ka3], (((0, 3),),))
    raw_keys = totals["k"]
    vb2, raw_keys = barrier((vb2, raw_keys))
    far_query = lax.ppermute(vb2[depth:], "seq", line_pairs(3, 0, groups))
    va3 = send(vb2, 3, 0)
    smooth = smooth_of(raw_keys)
    va2, vb2, smooth = barrier((va2, vb2, smooth))
    absorb("v", [va2 + vb2], (((0, 2), (1, 2)),))
    queries = [
        value_block[depth:],
        va1[depth:],
        va2[depth:] + vb2[depth:],
        vb1[depth:] + far_query,
    ]

    def finish_values(scored, *args):
        args, totals["v"] = barrier((args, totals["v"]))
        probs, stats = scored(*args)
        block, stats = barrier((va3, stats))
        absorb("v", [block], (((0, 3),),))
        return probs, stats, totals["v"]

    return raw_keys, smooth, queries, early, finish_values


def on_device(
    hidden, key_weight, value_weight, group_scale, new_kv, decode_query, page_table, lengths
):
    tokens = hidden.shape[0]
    columns = key_weight.shape[1]
    groups, owners = lax.axis_size("seq"), lax.axis_size("rep")
    my_group, my_owner = lax.axis_index("seq"), lax.axis_index("rep")
    assert columns // HD == owners
    pages_dev = tokens // PAGE
    step_count, per_group = decode_query.shape[:2]

    owner_is = [my_owner == owner for owner in range(owners)]
    own_query = my_part(decode_query, 2, owner_is).reshape(step_count * per_group, -1)

    first_pages = [
        (my_group * owners + (my_owner - k) % owners) * pages_dev for k in range(owners)
    ]
    early = (
        jnp.stack([my_group, my_owner]),
        owner_is,
        first_pages,
        partner(my_group, jnp.arange(groups, dtype=jnp.int32), groups),
        own_query,
    )
    if groups == LINE:
        raw_keys, smooth, queries, early, finish_values = line_project(
            hidden, key_weight, value_weight, own_query, early
        )
    else:
        raw_keys, raw_values = (
            jnp.dot(
                hidden,
                lax.all_gather(weight, ("seq", "rep"), axis=0, tiled=True),
                preferred_element_type=jnp.float32,
            )
            for weight in (key_weight, value_weight)
        )
        queries = from_groups(
            jnp.concatenate(jnp.split(own_query, own_query.shape[1] // columns, axis=1))
        )
        smooth = smooth_of(raw_keys)
    _, owner_is, first_pages, group_at, own_query = early
    counts = token_counts(page_table, lengths, first_pages, pages_dev)
    counts = counts.reshape(groups, per_group, -1)
    my_kv = my_part(new_kv, 3, owner_is).astype(jnp.float32)
    my_new = (my_kv[:, :, 0], my_kv[:, :, 1], my_part(group_scale, 1, owner_is))

    def by_head(x):
        return [my_part(x, 1, owner_is)] + [
            shifted(my_part(x, 1, owner_is, k), "rep", k) for k in range(1, owners)
        ]

    smoothing = smooth.reshape(-1)
    my_smooth = my_part(smooth, 1, owner_is)
    keys = clip_keys(raw_keys, smooth, group_scale)
    score_scale = HD ** (-0.5)
    scored = functools.partial(score, steps=step_count, scale=score_scale)
    args = (group_at, jnp.stack(queries), my_smooth, counts, by_head(keys))
    if groups == LINE:
        probs, stats, raw_values = finish_values(scored, *args)
    else:
        probs, stats = scored(*args)
    values = clip_values(raw_values, group_scale)
    messages = weigh(probs, by_head(values), stats)

    messages, keys, values, late = lax.optimization_barrier(
        (messages, keys, values, (own_query, my_smooth))
    )
    messages = to_groups(messages)
    kv_cache = with_layout_constraint(jnp.stack([keys, values], axis=1), Layout((0, 1, 2)))
    own = fresh(late[0], late[1], *my_new, score_scale)
    messages, kv_cache, own = lax.optimization_barrier((messages, kv_cache, own))
    attention = finish(messages, own, step_count * per_group)
    by_owner = from_owners(attention)
    attention = jnp.concatenate(
        [
            functools.reduce(
                lambda out, k: jnp.where(owner_is[(head + k) % owners], by_owner[k], out),
                range(1, owners),
                by_owner[0],
            )
            for head in range(owners)
        ],
        axis=1,
    ).reshape(decode_query.shape)
    return (kv_cache, smoothing, attention)


def solution(mesh):
    placed = (
        P(("seq", "rep"), None),
        P(("seq", "rep"), "head"),
        P(("seq", "rep"), "head"),
        P(None, "head"),
        P(None, "seq", None, "head"),
        P(None, "seq", "head"),
        P(),
        P(),
    )

    return jax.shard_map(
        on_device,
        mesh=mesh,
        in_specs=placed,
        out_specs=(P(("seq", "rep"), None, "head"), P("head"), P(None, "seq", "head")),
        check_vma=False,
    )
```

```python
import functools

import jax
import jax.numpy as jnp
from jax import lax
from jax.experimental import pallas as pl
from jax.experimental.layout import Layout, with_layout_constraint
from jax.experimental.pallas import tpu as pltpu
from jax.sharding import PartitionSpec as P


HD = 128
PAGE = 32


EPSILON = 1e-05
NEGATIVE = -1e30
LINE = 4


def shifted(x, axis, k):
    n = lax.axis_size(axis)
    return lax.ppermute(x, axis, [(i, (i + k) % n) for i in range(n)])


def partner(me, k, n):
    return me ^ k if n == LINE else (k - me) % n


def swapped(x, axis, k):
    n = lax.axis_size(axis)
    return lax.ppermute(x, axis, [(i, partner(i, k, n)) for i in range(n)])


def from_owners(x):
    return [x] + [shifted(x, "rep", k) for k in range(1, lax.axis_size("rep"))]


def from_groups(x):
    n = lax.axis_size("seq")
    if n != LINE:
        return list(lax.all_gather(x, "seq")[partner(lax.axis_index("seq"), jnp.arange(n), n)])
    return [x] + [swapped(x, "seq", k) for k in range(1, n)]


def to_groups(x):
    n = lax.axis_size("seq")
    if n != LINE:
        order = partner(lax.axis_index("seq"), jnp.arange(n), n)
        back = lax.all_to_all(jnp.stack(x)[order], "seq", split_axis=0, concat_axis=0)
        return list(back[order])
    return [x[0]] + [swapped(x[k], "seq", k) for k in range(1, n)]


def pack_kernel(weight, query, out, sem):
    depth, columns = weight.shape
    copy = pltpu.make_async_copy(weight, out.at[pl.ds(0, depth)], sem)
    copy.start()
    lines = query.shape[0]
    for k in range(query.shape[1] // columns):
        at = pl.ds(depth + k * lines, lines)
        out[at, :] = query[:, k * columns : (k + 1) * columns]
    copy.wait()


def pack(weight, query):
    depth, columns = weight.shape
    whole = pl.BlockSpec(memory_space=pltpu.VMEM)
    return pl.pallas_call(
        pack_kernel,
        out_shape=jax.ShapeDtypeStruct((depth + query.size // columns, columns), weight.dtype),
        in_specs=[pl.BlockSpec(memory_space=pl.ANY), whole],
        out_specs=whole,
        scratch_shapes=[pltpu.SemaphoreType.DMA],
        compiler_params=pltpu.CompilerParams(vmem_limit_bytes=8 * 2**20),
        name="pack",
    )(weight, query)


def load_kernel(owners, place, hidden, *refs):
    weights, (held, keys, values, taken, arrived, taken_arrived) = refs[:2], refs[2:]
    depth = taken.shape[1]
    blocks = held.shape[1] // depth
    takes = [
        pltpu.make_async_copy(weight, taken.at[j], taken_arrived.at[j])
        for j, weight in enumerate(weights)
    ]

    def block(j):
        index = lax.rem(place[0] * owners + place[1] + j, blocks)
        return pl.ds(pl.multiple_of(index * depth, depth), depth)

    def copy(j):
        return pltpu.make_async_copy(hidden.at[:, block(j)], held.at[:, block(j)], arrived.at[j])

    copy(0).start()
    for take in takes:
        take.start()
    for j in range(1, blocks):
        copy(j).start()
    copy(0).wait()
    for j, out in enumerate((keys, values)):
        takes[j].wait()
        out[...] = jnp.dot(held[:, block(0)], taken[j], preferred_element_type=jnp.float32)
    for j in range(1, blocks):
        copy(j).wait()


def load(hidden, key_weight, value_weight, place, owners):
    tokens, width = hidden.shape
    depth, columns = key_weight.shape
    whole = pl.BlockSpec(memory_space=pltpu.VMEM)
    total = jax.ShapeDtypeStruct((tokens, columns), jnp.float32)
    return pl.pallas_call(
        functools.partial(load_kernel, owners),
        out_shape=(jax.ShapeDtypeStruct(hidden.shape, hidden.dtype), total, total),
        in_specs=[
            pl.BlockSpec(memory_space=pltpu.SMEM),
            pl.BlockSpec(memory_space=pltpu.HBM),
            pl.BlockSpec(memory_space=pl.ANY),
            pl.BlockSpec(memory_space=pl.ANY),
        ],
        out_specs=(whole,) * 3,
        scratch_shapes=[
            pltpu.VMEM((2, depth, columns), key_weight.dtype),
            pltpu.SemaphoreType.DMA((width // depth,)),
            pltpu.SemaphoreType.DMA((2,)),
        ],
        compiler_params=pltpu.CompilerParams(vmem_limit_bytes=30 * 2**20),
        cost_estimate=pl.CostEstimate(
            flops=4 * tokens * depth * columns,
            bytes_accessed=2 * tokens * width,
            transcendentals=0,
        ),
        name="load",
    )(place, hidden, key_weight, value_weight)


def project_kernel(hops, back, groups, owners, place, left, *refs):
    count = len(hops)
    weights, total = refs[:count], refs[count]
    out, held, arrived = refs[-3:]
    depth = held.shape[1]
    copies = [
        pltpu.make_async_copy(weights[j].at[pl.ds(0, depth)], held.at[j], arrived.at[j])
        for j in range(count)
    ]
    for copy in copies:
        copy.start()
    out[...] = total[...]
    owner = lax.rem(place[1] + owners - back, owners)
    for j, copy in enumerate(copies):
        copy.wait()
        group = jnp.int32(-1)
        for parity, hop in hops[j]:
            there = place[0] + jnp.where(lax.rem(place[0], 2) == parity, hop, -hop)
            group = jnp.where((there >= 0) & (there < groups), there, group)

        @pl.when((group >= 0) & (group < groups))
        def _(j=j, group=group):
            block = pl.ds(pl.multiple_of((group * owners + owner) * depth, depth), depth)
            out[...] += jnp.dot(left[:, block], held[j], preferred_element_type=jnp.float32)


def project(hidden, total, weights, depth, place, hops, back, groups, owners):
    tokens = hidden.shape[0]
    columns = weights[0].shape[1]
    count = len(weights)
    whole = pl.BlockSpec(memory_space=pltpu.VMEM)
    return pl.pallas_call(
        functools.partial(project_kernel, hops, back, groups, owners),
        out_shape=jax.ShapeDtypeStruct((tokens, columns), jnp.float32),
        in_specs=[pl.BlockSpec(memory_space=pltpu.SMEM), whole]
        + [pl.BlockSpec(memory_space=pl.ANY)] * count
        + [whole],
        out_specs=whole,
        scratch_shapes=[
            pltpu.VMEM((count, depth, columns), weights[0].dtype),
            pltpu.SemaphoreType.DMA((count,)),
        ],
        compiler_params=pltpu.CompilerParams(vmem_limit_bytes=12 * 2**20),
        cost_estimate=pl.CostEstimate(
            flops=2 * tokens * depth * columns * count,
            bytes_accessed=2 * count * depth * (tokens + columns) + 8 * tokens * columns,
            transcendentals=0,
        ),
        input_output_aliases={2 + count: 0},
        name="project",
    )(place, hidden, *weights, total)


def score_kernel(slots, parts, steps, scale, group, query, smooth, count, *refs):
    keys, probs, stats = refs[:parts], refs[parts], refs[parts + 1 : parts + 1 + slots]
    scores, tops, sums = refs[-3:]
    tokens = keys[0].shape[0]
    width = keys[0].shape[1]
    requests = count.shape[1]
    rows = scores.shape[0]
    heads = query.shape[1] * query.shape[2] // (steps * requests * width)
    per_line = query.shape[2] // width
    raw = [
        query[0][
            (head // per_line) * steps * requests : (head // per_line + 1) * steps * requests,
            (head % per_line) * width : (head % per_line + 1) * width,
        ]
        for head in range(heads)
    ]
    raw = jnp.concatenate(raw, axis=0)
    scaled = (raw.astype(jnp.float32) * smooth[...]).astype(jnp.bfloat16)
    for p in range(parts):
        scores[:, p * tokens : (p + 1) * tokens] = lax.dot_general(
            scaled, keys[p][...], (((1,), (1,)), ((), ())), preferred_element_type=jnp.float32
        )
    again = 2 if (rows // requests) % 2 == 0 else 1
    times = jnp.concatenate([count[0]] * again, axis=0)
    bias = jnp.where(times > 0.0, 0.0, NEGATIVE)
    for start in range(0, rows, again * requests):
        at = pl.ds(start, again * requests)
        raw = scores[at, :] * scale + bias
        top = jnp.max(raw, axis=1, keepdims=True)
        counted = jnp.exp(raw - top) * times
        probs[0, at, :] = counted.astype(jnp.bfloat16)
        tops[at, :] = jnp.broadcast_to(top, (again * requests, 128))
        sums[at, :] = jnp.broadcast_to(
            jnp.sum(counted, axis=1, keepdims=True), (again * requests, 128)
        )
    for slot in range(slots):

        @pl.when(pl.program_id(0) == slot)
        def _(slot=slot):
            stats[slot][0:1, :] = jnp.transpose(tops[...])[0:1, :]
            stats[slot][1:2, :] = jnp.transpose(sums[...])[0:1, :]


def score(groups, query, smooth, count, keys, steps, scale):
    slots, packed, columns = query.shape
    tokens, width = keys[0].shape
    rows = packed * columns // width
    parts = len(keys)
    requests = count.shape[1]
    probs, *stats = pl.pallas_call(
        functools.partial(score_kernel, slots, parts, steps, scale),
        out_shape=[jax.ShapeDtypeStruct((slots, rows, parts * tokens), jnp.bfloat16)]
        + [jax.ShapeDtypeStruct((2, rows), jnp.float32)] * slots,
        grid_spec=pltpu.PrefetchScalarGridSpec(
            num_scalar_prefetch=1,
            grid=(slots,),
            in_specs=[
                pl.BlockSpec((1, packed, columns), lambda k, group: (k, 0, 0)),
                pl.BlockSpec((1, width), lambda k, group: (0, 0)),
                pl.BlockSpec((1, requests, parts * tokens), lambda k, group: (group[k], 0, 0)),
            ]
            + [pl.BlockSpec((tokens, width), lambda k, group: (0, 0))] * parts,
            out_specs=[pl.BlockSpec((1, rows, parts * tokens), lambda k, group: (k, 0, 0))]
            + [pl.BlockSpec((2, rows), lambda k, group: (0, 0))] * slots,
            scratch_shapes=[
                pltpu.VMEM((rows, parts * tokens), jnp.float32),
                pltpu.VMEM((rows, 128), jnp.float32),
                pltpu.VMEM((rows, 128), jnp.float32),
            ],
        ),
        compiler_params=pltpu.CompilerParams(vmem_limit_bytes=16 * 2**20),
        cost_estimate=pl.CostEstimate(
            flops=2 * slots * rows * width * parts * tokens,
            bytes_accessed=2 * slots * rows * parts * tokens,
            transcendentals=slots * rows * parts * tokens,
        ),
        name="score",
    )(groups, query, smooth, count, *keys)
    return probs, stats


def thirds(x):
    out = []
    for _ in range(3):
        out.append(x.astype(jnp.bfloat16))
        x = x - out[-1].astype(jnp.float32)
    return out


def weigh_kernel(slots, parts, probs, *refs):
    values, stats, outs = refs[:parts], refs[parts : parts + slots], refs[parts + slots :]
    tokens, width = values[0].shape
    rows = probs.shape[1]
    summed = sum(
        jnp.dot(
            probs[0, :, p * tokens : (p + 1) * tokens],
            values[p][...],
            preferred_element_type=jnp.float32,
        )
        for p in range(parts)
    ).astype(jnp.bfloat16)
    for slot in range(slots):

        @pl.when(pl.program_id(0) == slot)
        def _(slot=slot):
            outs[slot][0:rows, :] = summed
            lines = []
            for third in thirds(stats[slot][...]):
                third = third.astype(jnp.float32)
                lines += [third[:, c : c + width] for c in range(0, rows, width)]
            tail = outs[slot].shape[0] - rows
            lines.append(jnp.zeros((tail - 2 * len(lines), width), jnp.float32))
            outs[slot][rows:, :] = jnp.concatenate(lines, axis=0).astype(jnp.bfloat16)


def packed_rows(rows, width):
    return rows + (6 * (rows // width) // 16 + 1) * 16


def weigh(probs, values, stats):
    slots, rows, _ = probs.shape
    tokens, width = values[0].shape
    parts = len(values)
    total_rows = packed_rows(rows, width)
    return pl.pallas_call(
        functools.partial(weigh_kernel, slots, parts),
        out_shape=[jax.ShapeDtypeStruct((total_rows, width), jnp.bfloat16)] * slots,
        grid=(slots,),
        in_specs=[pl.BlockSpec((1, rows, parts * tokens), lambda k: (k, 0, 0))]
        + [pl.BlockSpec((tokens, width), lambda k: (0, 0))] * parts
        + [pl.BlockSpec((2, rows), lambda k: (0, 0))] * slots,
        out_specs=[pl.BlockSpec((total_rows, width), lambda k: (0, 0))] * slots,
        compiler_params=pltpu.CompilerParams(vmem_limit_bytes=16 * 2**20),
        cost_estimate=pl.CostEstimate(
            flops=2 * slots * rows * width * parts * tokens,
            bytes_accessed=2 * slots * rows * parts * tokens,
            transcendentals=0,
        ),
        name="weigh",
    )(probs, *values, *stats)


def fresh_kernel(scale, query, smooth, new_keys, new_values, group_scale, summed, highest, total):
    steps, requests, width = new_keys.shape
    lines = steps * requests

    def by_line(x):
        x = x.astype(jnp.bfloat16).astype(jnp.float32)
        return jnp.concatenate([x] * steps, axis=0)

    def clip(x, row):
        limit = group_scale[row : row + 1, :]
        return jnp.clip(x, -8.0 * limit, 7.0 * limit)

    keys = [by_line(clip(new_keys[u] / smooth[...], 0)) for u in range(steps)]
    values = [by_line(clip(new_values[u], 1)) for u in range(steps)]
    line = lax.broadcasted_iota(jnp.int32, (lines, 1), 0)
    seen = [line >= u * requests for u in range(steps)]
    for head in range(query.shape[1] // width):
        at = pl.ds(head * lines, lines)
        mine = query[:, head * width : (head + 1) * width].astype(jnp.float32) * smooth[...]
        mine = mine.astype(jnp.bfloat16).astype(jnp.float32)
        scores = [
            jnp.where(seen[u], jnp.sum(mine * keys[u], axis=1, keepdims=True) * scale, NEGATIVE)
            for u in range(steps)
        ]
        top = functools.reduce(jnp.maximum, scores)
        expd = [jnp.where(seen[u], jnp.exp(scores[u] - top), 0.0) for u in range(steps)]
        highest[at, :] = jnp.broadcast_to(top, (lines, width))
        total[at, :] = jnp.broadcast_to(sum(expd), (lines, width))
        summed[at, :] = sum(
            e.astype(jnp.bfloat16).astype(jnp.float32) * value for e, value in zip(expd, values)
        )


def fresh(query, smooth, new_keys, new_values, group_scale, scale):
    lines, columns = query.shape
    width = smooth.shape[1]
    part = jax.ShapeDtypeStruct((lines * columns // width, width), jnp.float32)
    return pl.pallas_call(
        functools.partial(fresh_kernel, scale),
        out_shape=(part,) * 3,
        compiler_params=pltpu.CompilerParams(vmem_limit_bytes=16 * 2**20),
        name="fresh",
    )(query, smooth, new_keys, new_values, group_scale)


def finish_kernel(slots, *refs):
    messages, (summed, highest, total, out) = refs[:slots], refs[slots:]
    rows, width = summed.shape
    lines = out.shape[0]
    tails = [message[rows:, :].astype(jnp.float32) for message in messages]
    pieces = rows // width

    def column(slot, piece, which):
        row = [tails[slot][2 * (j * pieces + piece) + which :][:1] for j in range(3)]
        return jnp.transpose(jnp.broadcast_to(row[0] + row[1] + row[2], (width, width)))

    for piece in range(pieces):
        at = pl.ds(piece * width, width)
        parts = [
            (messages[k][at, :].astype(jnp.float32), column(k, piece, 0), column(k, piece, 1))
            for k in range(slots)
        ]
        parts.append((summed[at, :], highest[at, :], total[at, :]))
        top = functools.reduce(jnp.maximum, [part[1] for part in parts])
        shares = [jnp.exp(part[1] - top) for part in parts]
        norm = sum(share * part[2] for share, part in zip(shares, parts))
        merged = sum(share * part[0] for share, part in zip(shares, parts)) / norm
        merged = merged.astype(out.dtype)
        for first in range(0, width, lines):
            head = (piece * width + first) // lines
            out[:, head * width : (head + 1) * width] = merged[first : first + lines]


def finish(messages, own, lines):
    rows, width = own[0].shape
    return pl.pallas_call(
        functools.partial(finish_kernel, len(messages)),
        out_shape=jax.ShapeDtypeStruct((lines, rows * width // lines), jnp.bfloat16),
        compiler_params=pltpu.CompilerParams(vmem_limit_bytes=16 * 2**20),
        name="finish",
    )(*messages, *own)


def token_counts(page_table, lengths, first_pages, pages_dev):
    slots = page_table.shape[1]
    slot_ids = jnp.arange(slots, dtype=jnp.int32)
    whole_slots, rest = lengths // PAGE, lengths % PAGE
    pages = jnp.concatenate(
        [first + jnp.arange(pages_dev, dtype=jnp.int32) for first in first_pages]
    )
    same = page_table[:, :, None] == pages[None, None, :]
    whole = jnp.sum(same & (slot_ids[None, :] < whole_slots[:, None])[:, :, None], axis=1)
    last = jnp.sum(same & (slot_ids[None, :] == whole_slots[:, None])[:, :, None], axis=1)
    token = jnp.arange(pages.shape[0] * PAGE, dtype=jnp.int32)
    spread = token[None, :] // PAGE == jnp.arange(pages.shape[0], dtype=jnp.int32)[:, None]
    spread = spread.astype(jnp.bfloat16)
    whole = jnp.dot(whole.astype(jnp.bfloat16), spread, preferred_element_type=jnp.float32)
    last = jnp.dot(last.astype(jnp.bfloat16), spread, preferred_element_type=jnp.float32)
    return whole + jnp.where((token % PAGE)[None, :] < rest[:, None], last, 0.0)


def clip_keys(raw, smooth, scale):
    return jnp.clip(raw / smooth, -8.0 * scale[0], 7.0 * scale[0]).astype(jnp.bfloat16)


def clip_values(raw, scale):
    return jnp.clip(raw, -8.0 * scale[1], 7.0 * scale[1]).astype(jnp.bfloat16)


def my_part(x, axis, owner_is, ahead=0):
    owners = len(owner_is)
    size = x.shape[axis] // owners
    pieces = [lax.slice_in_dim(x, p * size, (p + 1) * size, axis=axis) for p in range(owners)]
    out = pieces[0]
    for p in range(1, owners):
        out = jnp.where(owner_is[(p - ahead) % owners], pieces[p], out)
    return out


def chip_top(raw_keys):
    top = jnp.max(jnp.abs(raw_keys), axis=0, keepdims=True)
    return functools.reduce(jnp.maximum, from_owners(top))


def smooth_of(top):
    top = functools.reduce(jnp.maximum, from_groups(top))
    return jnp.sqrt(top + EPSILON)


def line_pairs(hop, parity, groups):
    pairs = []
    for i in range(parity, groups - 1, 2):
        if i >= hop - 1:
            pairs.append((i, i + 1))
        if i + hop < groups:
            pairs.append((i + 1, i))
    return pairs


def line_project(hidden, key_weight, value_weight, own_query, early):
    groups, owners = lax.axis_size("seq"), lax.axis_size("rep")
    depth = key_weight.shape[0]
    barrier = lax.optimization_barrier

    def send(x, hop, parity):
        return lax.ppermute(x, "seq", line_pairs(hop, parity, groups))

    def absorb(name, blocks, hops, first=0):
        passed = [[shifted(block, "rep", k) for block in blocks] for k in range(1, owners)]
        for k, ready in enumerate([blocks] + passed):
            if k < first:
                continue
            totals[name] = project(
                hidden, totals[name], ready, depth, early[0], hops, k, groups, owners
            )

    totals = {}
    ka1 = send(key_weight, 1, 0)
    kb1 = send(key_weight, 1, 1)
    value_block = pack(value_weight, own_query)
    va1 = send(value_block, 1, 0)
    early, first = barrier((early, (key_weight, value_weight)))
    hidden, totals["k"], totals["v"] = load(hidden, *first, early[0], owners)
    for name, weight in (("k", key_weight), ("v", value_weight)):
        absorb(name, [weight], (((0, 0),),), 1)

    ka1, kb1, value_block, totals = barrier((ka1, kb1, value_block, totals))
    kb2 = send(ka1, 2, 1)
    ka2 = send(kb1, 2, 0)
    vb1 = send(value_block, 1, 1)
    absorb("k", [ka1, kb1], (((0, 1),), ((1, 1),)))

    kb2, va1, totals = barrier((kb2, va1, totals))
    ka3 = send(kb2, 3, 0)
    vb2 = send(va1, 2, 1)
    absorb("v", [va1], (((0, 1),),))

    ka2, totals = barrier((ka2, totals))
    absorb("k", [ka2 + kb2], (((0, 2), (1, 2)),))

    vb1, totals = barrier((vb1, totals))
    va2 = send(vb1, 2, 0)
    absorb("v", [vb1], (((1, 1),),))

    ka3, totals = barrier((ka3, totals))
    absorb("k", [ka3], (((0, 3),),))
    raw_keys = totals["k"]
    top = chip_top(raw_keys)
    smooth = smooth_of(top)
    vb2, top = barrier((vb2, top))
    far_query = lax.ppermute(vb2[depth:], "seq", line_pairs(3, 0, groups))
    va3 = send(vb2, 3, 0)
    va2, vb2, smooth = barrier((va2, vb2, smooth))
    absorb("v", [va2 + vb2], (((0, 2), (1, 2)),))
    queries = [
        value_block[depth:],
        va1[depth:],
        va2[depth:] + vb2[depth:],
        vb1[depth:] + far_query,
    ]

    def finish_values(scored, *args):
        args, totals["v"] = barrier((args, totals["v"]))
        probs, stats = scored(*args)
        block, stats = barrier((va3, stats))
        absorb("v", [block], (((0, 3),),))
        return probs, stats, totals["v"]

    return raw_keys, smooth, queries, early, finish_values


def on_device(
    hidden, key_weight, value_weight, group_scale, new_kv, decode_query, page_table, lengths
):
    tokens = hidden.shape[0]
    columns = key_weight.shape[1]
    groups, owners = lax.axis_size("seq"), lax.axis_size("rep")
    my_group, my_owner = lax.axis_index("seq"), lax.axis_index("rep")
    assert columns // HD == owners
    pages_dev = tokens // PAGE
    step_count, per_group = decode_query.shape[:2]

    owner_is = [my_owner == owner for owner in range(owners)]
    own_query = my_part(decode_query, 2, owner_is).reshape(step_count * per_group, -1)

    first_pages = [
        (my_group * owners + (my_owner - k) % owners) * pages_dev for k in range(owners)
    ]
    early = (
        jnp.stack([my_group, my_owner]),
        owner_is,
        first_pages,
        partner(my_group, jnp.arange(groups, dtype=jnp.int32), groups),
        own_query,
    )
    if groups == LINE:
        raw_keys, smooth, queries, early, finish_values = line_project(
            hidden, key_weight, value_weight, own_query, early
        )
    else:
        raw_keys, raw_values = (
            jnp.dot(
                hidden,
                lax.all_gather(weight, ("seq", "rep"), axis=0, tiled=True),
                preferred_element_type=jnp.float32,
            )
            for weight in (key_weight, value_weight)
        )
        queries = from_groups(
            jnp.concatenate(jnp.split(own_query, own_query.shape[1] // columns, axis=1))
        )
        smooth = smooth_of(chip_top(raw_keys))
    _, owner_is, first_pages, group_at, own_query = early
    counts = token_counts(page_table, lengths, first_pages, pages_dev)
    counts = counts.reshape(groups, per_group, -1)
    my_kv = my_part(new_kv, 3, owner_is).astype(jnp.float32)
    my_new = (my_kv[:, :, 0], my_kv[:, :, 1], my_part(group_scale, 1, owner_is))

    def by_head(x):
        return [my_part(x, 1, owner_is)] + [
            shifted(my_part(x, 1, owner_is, k), "rep", k) for k in range(1, owners)
        ]

    smoothing = smooth.reshape(-1)
    my_smooth = my_part(smooth, 1, owner_is)
    keys = clip_keys(raw_keys, smooth, group_scale)
    score_scale = HD ** (-0.5)
    scored = functools.partial(score, steps=step_count, scale=score_scale)
    args = (group_at, jnp.stack(queries), my_smooth, counts, by_head(keys))
    if groups == LINE:
        probs, stats, raw_values = finish_values(scored, *args)
    else:
        probs, stats = scored(*args)
    values = clip_values(raw_values, group_scale)
    messages = weigh(probs, by_head(values), stats)

    messages, keys, values, late = lax.optimization_barrier(
        (messages, keys, values, (own_query, my_smooth))
    )
    messages = to_groups(messages)
    is_key = lax.broadcasted_iota(jnp.int32, (1, 2, 1), 1) == 0
    kv_cache = jnp.where(is_key, keys[:, None, :], values[:, None, :])
    kv_cache = with_layout_constraint(kv_cache, Layout((0, 1, 2)))
    own = fresh(late[0], late[1], *my_new, score_scale)
    messages, kv_cache, own = lax.optimization_barrier((messages, kv_cache, own))
    attention = finish(messages, own, step_count * per_group)
    by_owner = from_owners(attention)
    attention = jnp.concatenate(
        [
            functools.reduce(
                lambda out, k: jnp.where(owner_is[(head + k) % owners], by_owner[k], out),
                range(1, owners),
                by_owner[0],
            )
            for head in range(owners)
        ],
        axis=1,
    ).reshape(decode_query.shape)
    return (kv_cache, smoothing, attention)


def solution(mesh):
    placed = (
        P(("seq", "rep"), None),
        P(("seq", "rep"), "head"),
        P(("seq", "rep"), "head"),
        P(None, "head"),
        P(None, "seq", None, "head"),
        P(None, "seq", "head"),
        P(),
        P(),
    )

    return jax.shard_map(
        on_device,
        mesh=mesh,
        in_specs=placed,
        out_specs=(P(("seq", "rep"), None, "head"), P("head"), P(None, "seq", "head")),
        check_vma=False,
    )
```

```python
import functools

import jax
import jax.numpy as jnp
from jax import lax
from jax.experimental import pallas as pl
from jax.experimental.layout import Layout, with_layout_constraint
from jax.experimental.pallas import tpu as pltpu
from jax.sharding import PartitionSpec as P


HD = 128
PAGE = 32


EPSILON = 1e-05
NEGATIVE = -1e30
LINE = 4


def shifted(x, axis, k):
    n = lax.axis_size(axis)
    return lax.ppermute(x, axis, [(i, (i + k) % n) for i in range(n)])


def partner(me, k, n):
    return me ^ k if n == LINE else (k - me) % n


def swapped(x, axis, k):
    n = lax.axis_size(axis)
    return lax.ppermute(x, axis, [(i, partner(i, k, n)) for i in range(n)])


def from_owners(x):
    return [x] + [shifted(x, "rep", k) for k in range(1, lax.axis_size("rep"))]


def from_groups(x):
    n = lax.axis_size("seq")
    if n != LINE:
        return list(lax.all_gather(x, "seq")[partner(lax.axis_index("seq"), jnp.arange(n), n)])
    return [x] + [swapped(x, "seq", k) for k in range(1, n)]


def to_groups(x):
    n = lax.axis_size("seq")
    if n != LINE:
        order = partner(lax.axis_index("seq"), jnp.arange(n), n)
        back = lax.all_to_all(jnp.stack(x)[order], "seq", split_axis=0, concat_axis=0)
        return list(back[order])
    return [x[0]] + [swapped(x[k], "seq", k) for k in range(1, n)]


def pack_kernel(weight, query, out, sem):
    depth, columns = weight.shape
    copy = pltpu.make_async_copy(weight, out.at[pl.ds(0, depth)], sem)
    copy.start()
    lines = query.shape[0]
    for k in range(query.shape[1] // columns):
        at = pl.ds(depth + k * lines, lines)
        out[at, :] = query[:, k * columns : (k + 1) * columns]
    copy.wait()


def pack(weight, query):
    depth, columns = weight.shape
    whole = pl.BlockSpec(memory_space=pltpu.VMEM)
    return pl.pallas_call(
        pack_kernel,
        out_shape=jax.ShapeDtypeStruct((depth + query.size // columns, columns), weight.dtype),
        in_specs=[pl.BlockSpec(memory_space=pl.ANY), whole],
        out_specs=whole,
        scratch_shapes=[pltpu.SemaphoreType.DMA],
        compiler_params=pltpu.CompilerParams(vmem_limit_bytes=8 * 2**20),
        name="pack",
    )(weight, query)


def load_kernel(owners, place, hidden, *refs):
    weights, (held, keys, values, taken, arrived, taken_arrived) = refs[:2], refs[2:]
    depth = taken.shape[1]
    blocks = held.shape[1] // depth
    takes = [
        pltpu.make_async_copy(weight, taken.at[j], taken_arrived.at[j])
        for j, weight in enumerate(weights)
    ]

    def block(j):
        index = lax.rem(place[0] * owners + place[1] + j, blocks)
        return pl.ds(pl.multiple_of(index * depth, depth), depth)

    def copy(j):
        return pltpu.make_async_copy(hidden.at[:, block(j)], held.at[:, block(j)], arrived.at[j])

    copy(0).start()
    for take in takes:
        take.start()
    for j in range(1, blocks):
        copy(j).start()
    copy(0).wait()
    for j, out in enumerate((keys, values)):
        takes[j].wait()
        out[...] = jnp.dot(held[:, block(0)], taken[j], preferred_element_type=jnp.float32)
    for j in range(1, blocks):
        copy(j).wait()


def load(hidden, key_weight, value_weight, place, owners):
    tokens, width = hidden.shape
    depth, columns = key_weight.shape
    whole = pl.BlockSpec(memory_space=pltpu.VMEM)
    total = jax.ShapeDtypeStruct((tokens, columns), jnp.float32)
    return pl.pallas_call(
        functools.partial(load_kernel, owners),
        out_shape=(jax.ShapeDtypeStruct(hidden.shape, hidden.dtype), total, total),
        in_specs=[
            pl.BlockSpec(memory_space=pltpu.SMEM),
            pl.BlockSpec(memory_space=pltpu.HBM),
            pl.BlockSpec(memory_space=pl.ANY),
            pl.BlockSpec(memory_space=pl.ANY),
        ],
        out_specs=(whole,) * 3,
        scratch_shapes=[
            pltpu.VMEM((2, depth, columns), key_weight.dtype),
            pltpu.SemaphoreType.DMA((width // depth,)),
            pltpu.SemaphoreType.DMA((2,)),
        ],
        compiler_params=pltpu.CompilerParams(vmem_limit_bytes=30 * 2**20),
        cost_estimate=pl.CostEstimate(
            flops=4 * tokens * depth * columns,
            bytes_accessed=2 * tokens * width,
            transcendentals=0,
        ),
        name="load",
    )(place, hidden, key_weight, value_weight)


def project_kernel(hops, back, groups, owners, place, left, *refs):
    count = len(hops)
    weights, total = refs[:count], refs[count]
    out, held, arrived = refs[-3:]
    depth = held.shape[1]
    copies = [
        pltpu.make_async_copy(weights[j].at[pl.ds(0, depth)], held.at[j], arrived.at[j])
        for j in range(count)
    ]
    for copy in copies:
        copy.start()
    out[...] = total[...]
    owner = lax.rem(place[1] + owners - back, owners)
    for j, copy in enumerate(copies):
        copy.wait()
        group = jnp.int32(-1)
        for parity, hop in hops[j]:
            there = place[0] + jnp.where(lax.rem(place[0], 2) == parity, hop, -hop)
            group = jnp.where((there >= 0) & (there < groups), there, group)

        @pl.when((group >= 0) & (group < groups))
        def _(j=j, group=group):
            block = pl.ds(pl.multiple_of((group * owners + owner) * depth, depth), depth)
            out[...] += jnp.dot(left[:, block], held[j], preferred_element_type=jnp.float32)


def project(hidden, total, weights, depth, place, hops, back, groups, owners):
    tokens = hidden.shape[0]
    columns = weights[0].shape[1]
    count = len(weights)
    whole = pl.BlockSpec(memory_space=pltpu.VMEM)
    return pl.pallas_call(
        functools.partial(project_kernel, hops, back, groups, owners),
        out_shape=jax.ShapeDtypeStruct((tokens, columns), jnp.float32),
        in_specs=[pl.BlockSpec(memory_space=pltpu.SMEM), whole]
        + [pl.BlockSpec(memory_space=pl.ANY)] * count
        + [whole],
        out_specs=whole,
        scratch_shapes=[
            pltpu.VMEM((count, depth, columns), weights[0].dtype),
            pltpu.SemaphoreType.DMA((count,)),
        ],
        compiler_params=pltpu.CompilerParams(vmem_limit_bytes=12 * 2**20),
        cost_estimate=pl.CostEstimate(
            flops=2 * tokens * depth * columns * count,
            bytes_accessed=2 * count * depth * (tokens + columns) + 8 * tokens * columns,
            transcendentals=0,
        ),
        input_output_aliases={2 + count: 0},
        name="project",
    )(place, hidden, *weights, total)


def score_kernel(slots, parts, steps, scale, group, query, smooth, count, *refs):
    keys, probs, stats = refs[:parts], refs[parts], refs[parts + 1 : parts + 1 + slots]
    scores, tops, sums = refs[-3:]
    tokens = keys[0].shape[0]
    width = keys[0].shape[1]
    requests = count.shape[1]
    rows = scores.shape[0]
    heads = query.shape[1] * query.shape[2] // (steps * requests * width)
    per_line = query.shape[2] // width
    raw = [
        query[0][
            (head // per_line) * steps * requests : (head // per_line + 1) * steps * requests,
            (head % per_line) * width : (head % per_line + 1) * width,
        ]
        for head in range(heads)
    ]
    raw = jnp.concatenate(raw, axis=0)
    scaled = (raw.astype(jnp.float32) * smooth[...]).astype(jnp.bfloat16)
    for p in range(parts):
        scores[:, p * tokens : (p + 1) * tokens] = lax.dot_general(
            scaled, keys[p][...], (((1,), (1,)), ((), ())), preferred_element_type=jnp.float32
        )
    again = 2 if (rows // requests) % 2 == 0 else 1
    times = jnp.concatenate([count[0]] * again, axis=0)
    bias = jnp.where(times > 0.0, 0.0, NEGATIVE)
    for start in range(0, rows, again * requests):
        at = pl.ds(start, again * requests)
        raw = scores[at, :] * scale + bias
        top = jnp.max(raw, axis=1, keepdims=True)
        counted = jnp.exp(raw - top) * times
        probs[0, at, :] = counted.astype(jnp.bfloat16)
        tops[at, :] = jnp.broadcast_to(top, (again * requests, 128))
        sums[at, :] = jnp.broadcast_to(
            jnp.sum(counted, axis=1, keepdims=True), (again * requests, 128)
        )
    for slot in range(slots):

        @pl.when(pl.program_id(0) == slot)
        def _(slot=slot):
            stats[slot][0:1, :] = jnp.transpose(tops[...])[0:1, :]
            stats[slot][1:2, :] = jnp.transpose(sums[...])[0:1, :]


def score(groups, query, smooth, count, keys, steps, scale):
    slots, packed, columns = query.shape
    tokens, width = keys[0].shape
    rows = packed * columns // width
    parts = len(keys)
    requests = count.shape[1]
    probs, *stats = pl.pallas_call(
        functools.partial(score_kernel, slots, parts, steps, scale),
        out_shape=[jax.ShapeDtypeStruct((slots, rows, parts * tokens), jnp.bfloat16)]
        + [jax.ShapeDtypeStruct((2, rows), jnp.float32)] * slots,
        grid_spec=pltpu.PrefetchScalarGridSpec(
            num_scalar_prefetch=1,
            grid=(slots,),
            in_specs=[
                pl.BlockSpec((1, packed, columns), lambda k, group: (k, 0, 0)),
                pl.BlockSpec((1, width), lambda k, group: (0, 0)),
                pl.BlockSpec((1, requests, parts * tokens), lambda k, group: (group[k], 0, 0)),
            ]
            + [pl.BlockSpec((tokens, width), lambda k, group: (0, 0))] * parts,
            out_specs=[pl.BlockSpec((1, rows, parts * tokens), lambda k, group: (k, 0, 0))]
            + [pl.BlockSpec((2, rows), lambda k, group: (0, 0))] * slots,
            scratch_shapes=[
                pltpu.VMEM((rows, parts * tokens), jnp.float32),
                pltpu.VMEM((rows, 128), jnp.float32),
                pltpu.VMEM((rows, 128), jnp.float32),
            ],
        ),
        compiler_params=pltpu.CompilerParams(vmem_limit_bytes=16 * 2**20),
        cost_estimate=pl.CostEstimate(
            flops=2 * slots * rows * width * parts * tokens,
            bytes_accessed=2 * slots * rows * parts * tokens,
            transcendentals=slots * rows * parts * tokens,
        ),
        name="score",
    )(groups, query, smooth, count, *keys)
    return probs, stats


def thirds(x):
    out = []
    for _ in range(3):
        out.append(x.astype(jnp.bfloat16))
        x = x - out[-1].astype(jnp.float32)
    return out


def weigh_kernel(slots, parts, probs, *refs):
    values, stats, outs = refs[:parts], refs[parts : parts + slots], refs[parts + slots :]
    tokens, width = values[0].shape
    rows = probs.shape[1]
    summed = sum(
        jnp.dot(
            probs[0, :, p * tokens : (p + 1) * tokens],
            values[p][...],
            preferred_element_type=jnp.float32,
        )
        for p in range(parts)
    ).astype(jnp.bfloat16)
    for slot in range(slots):

        @pl.when(pl.program_id(0) == slot)
        def _(slot=slot):
            outs[slot][0:rows, :] = summed
            lines = []
            for third in thirds(stats[slot][...]):
                third = third.astype(jnp.float32)
                lines += [third[:, c : c + width] for c in range(0, rows, width)]
            tail = outs[slot].shape[0] - rows
            lines.append(jnp.zeros((tail - 2 * len(lines), width), jnp.float32))
            outs[slot][rows:, :] = jnp.concatenate(lines, axis=0).astype(jnp.bfloat16)


def packed_rows(rows, width):
    return rows + (6 * (rows // width) // 16 + 1) * 16


def weigh(probs, values, stats):
    slots, rows, _ = probs.shape
    tokens, width = values[0].shape
    parts = len(values)
    total_rows = packed_rows(rows, width)
    return pl.pallas_call(
        functools.partial(weigh_kernel, slots, parts),
        out_shape=[jax.ShapeDtypeStruct((total_rows, width), jnp.bfloat16)] * slots,
        grid=(slots,),
        in_specs=[pl.BlockSpec((1, rows, parts * tokens), lambda k: (k, 0, 0))]
        + [pl.BlockSpec((tokens, width), lambda k: (0, 0))] * parts
        + [pl.BlockSpec((2, rows), lambda k: (0, 0))] * slots,
        out_specs=[pl.BlockSpec((total_rows, width), lambda k: (0, 0))] * slots,
        compiler_params=pltpu.CompilerParams(vmem_limit_bytes=16 * 2**20),
        cost_estimate=pl.CostEstimate(
            flops=2 * slots * rows * width * parts * tokens,
            bytes_accessed=2 * slots * rows * parts * tokens,
            transcendentals=0,
        ),
        name="weigh",
    )(probs, *values, *stats)


def fresh_kernel(scale, query, smooth, new_keys, new_values, group_scale, summed, highest, total):
    steps, requests, width = new_keys.shape
    lines = steps * requests

    def by_line(x):
        x = x.astype(jnp.bfloat16).astype(jnp.float32)
        return jnp.concatenate([x] * steps, axis=0)

    def clip(x, row):
        limit = group_scale[row : row + 1, :]
        return jnp.clip(x, -8.0 * limit, 7.0 * limit)

    keys = [by_line(clip(new_keys[u] / smooth[...], 0)) for u in range(steps)]
    values = [by_line(clip(new_values[u], 1)) for u in range(steps)]
    line = lax.broadcasted_iota(jnp.int32, (lines, 1), 0)
    seen = [line >= u * requests for u in range(steps)]
    for head in range(query.shape[1] // width):
        at = pl.ds(head * lines, lines)
        mine = query[:, head * width : (head + 1) * width].astype(jnp.float32) * smooth[...]
        mine = mine.astype(jnp.bfloat16).astype(jnp.float32)
        scores = [
            jnp.where(seen[u], jnp.sum(mine * keys[u], axis=1, keepdims=True) * scale, NEGATIVE)
            for u in range(steps)
        ]
        top = functools.reduce(jnp.maximum, scores)
        expd = [jnp.where(seen[u], jnp.exp(scores[u] - top), 0.0) for u in range(steps)]
        highest[at, :] = jnp.broadcast_to(top, (lines, width))
        total[at, :] = jnp.broadcast_to(sum(expd), (lines, width))
        summed[at, :] = sum(
            e.astype(jnp.bfloat16).astype(jnp.float32) * value for e, value in zip(expd, values)
        )


def fresh(query, smooth, new_keys, new_values, group_scale, scale):
    lines, columns = query.shape
    width = smooth.shape[1]
    part = jax.ShapeDtypeStruct((lines * columns // width, width), jnp.float32)
    return pl.pallas_call(
        functools.partial(fresh_kernel, scale),
        out_shape=(part,) * 3,
        compiler_params=pltpu.CompilerParams(vmem_limit_bytes=16 * 2**20),
        name="fresh",
    )(query, smooth, new_keys, new_values, group_scale)


def finish_kernel(slots, *refs):
    messages, (summed, highest, total, out) = refs[:slots], refs[slots:]
    rows, width = summed.shape
    lines = out.shape[0]
    tails = [message[rows:, :].astype(jnp.float32) for message in messages]
    pieces = rows // width

    def column(slot, piece, which):
        row = [tails[slot][2 * (j * pieces + piece) + which :][:1] for j in range(3)]
        return jnp.transpose(jnp.broadcast_to(row[0] + row[1] + row[2], (width, width)))

    for piece in range(pieces):
        at = pl.ds(piece * width, width)
        parts = [
            (messages[k][at, :].astype(jnp.float32), column(k, piece, 0), column(k, piece, 1))
            for k in range(slots)
        ]
        parts.append((summed[at, :], highest[at, :], total[at, :]))
        top = functools.reduce(jnp.maximum, [part[1] for part in parts])
        shares = [jnp.exp(part[1] - top) for part in parts]
        norm = sum(share * part[2] for share, part in zip(shares, parts))
        merged = sum(share * part[0] for share, part in zip(shares, parts)) / norm
        merged = merged.astype(out.dtype)
        for first in range(0, width, lines):
            head = (piece * width + first) // lines
            out[:, head * width : (head + 1) * width] = merged[first : first + lines]


def finish(messages, own, lines):
    rows, width = own[0].shape
    return pl.pallas_call(
        functools.partial(finish_kernel, len(messages)),
        out_shape=jax.ShapeDtypeStruct((lines, rows * width // lines), jnp.bfloat16),
        compiler_params=pltpu.CompilerParams(vmem_limit_bytes=16 * 2**20),
        name="finish",
    )(*messages, *own)


def token_counts(page_table, lengths, first_pages, pages_dev):
    slots = page_table.shape[1]
    slot_ids = jnp.arange(slots, dtype=jnp.int32)
    whole_slots, rest = lengths // PAGE, lengths % PAGE
    pages = jnp.concatenate(
        [first + jnp.arange(pages_dev, dtype=jnp.int32) for first in first_pages]
    )
    same = page_table[:, :, None] == pages[None, None, :]
    whole = jnp.sum(same & (slot_ids[None, :] < whole_slots[:, None])[:, :, None], axis=1)
    last = jnp.sum(same & (slot_ids[None, :] == whole_slots[:, None])[:, :, None], axis=1)
    token = jnp.arange(pages.shape[0] * PAGE, dtype=jnp.int32)
    spread = token[None, :] // PAGE == jnp.arange(pages.shape[0], dtype=jnp.int32)[:, None]
    spread = spread.astype(jnp.bfloat16)
    whole = jnp.dot(whole.astype(jnp.bfloat16), spread, preferred_element_type=jnp.float32)
    last = jnp.dot(last.astype(jnp.bfloat16), spread, preferred_element_type=jnp.float32)
    return whole + jnp.where((token % PAGE)[None, :] < rest[:, None], last, 0.0)


def clip_keys(raw, smooth, scale):
    return jnp.clip(raw / smooth, -8.0 * scale[0], 7.0 * scale[0]).astype(jnp.bfloat16)


def clip_values(raw, scale):
    return jnp.clip(raw, -8.0 * scale[1], 7.0 * scale[1]).astype(jnp.bfloat16)


def my_part(x, axis, owner_is, ahead=0):
    owners = len(owner_is)
    size = x.shape[axis] // owners
    pieces = [lax.slice_in_dim(x, p * size, (p + 1) * size, axis=axis) for p in range(owners)]
    out = pieces[0]
    for p in range(1, owners):
        out = jnp.where(owner_is[(p - ahead) % owners], pieces[p], out)
    return out


def chip_top(raw_keys):
    top = jnp.max(jnp.abs(raw_keys), axis=0, keepdims=True)
    return functools.reduce(jnp.maximum, from_owners(top))


def smooth_of(top):
    top = functools.reduce(jnp.maximum, from_groups(top))
    return jnp.sqrt(top + EPSILON)


def line_pairs(hop, parity, groups):
    pairs = []
    for i in range(parity, groups - 1, 2):
        if i >= hop - 1:
            pairs.append((i, i + 1))
        if i + hop < groups:
            pairs.append((i + 1, i))
    return pairs


def line_project(hidden, key_weight, value_weight, own_query, early):
    groups, owners = lax.axis_size("seq"), lax.axis_size("rep")
    depth = key_weight.shape[0]
    barrier = lax.optimization_barrier

    def send(x, hop, parity):
        return lax.ppermute(x, "seq", line_pairs(hop, parity, groups))

    def absorb(name, blocks, hops, first=0):
        passed = [[shifted(block, "rep", k) for block in blocks] for k in range(1, owners)]
        for k, ready in enumerate([blocks] + passed):
            if k < first:
                continue
            totals[name] = project(
                hidden, totals[name], ready, depth, early[0], hops, k, groups, owners
            )

    totals = {}
    ka1 = send(key_weight, 1, 0)
    kb1 = send(key_weight, 1, 1)
    value_block = pack(value_weight, own_query)
    va1 = send(value_block, 1, 0)
    vb1 = send(value_block, 1, 1)
    early, first = barrier((early, (key_weight, value_weight)))
    hidden, totals["k"], totals["v"] = load(hidden, *first, early[0], owners)
    for name, weight in (("k", key_weight), ("v", value_weight)):
        absorb(name, [weight], (((0, 0),),), 1)

    ka1, kb1, totals = barrier((ka1, kb1, totals))
    kb2 = send(ka1, 2, 1)
    ka2 = send(kb1, 2, 0)
    absorb("k", [ka1, kb1], (((0, 1),), ((1, 1),)))

    va1, vb1, totals = barrier((va1, vb1, totals))
    vb2 = send(va1, 2, 1)
    absorb("v", [va1, vb1], (((0, 1),), ((1, 1),)))

    kb2, vb1, totals = barrier((kb2, vb1, totals))
    ka3 = send(kb2, 3, 0)
    va2 = send(vb1, 2, 0)

    ka2, totals = barrier((ka2, totals))
    absorb("k", [ka2 + kb2], (((0, 2), (1, 2)),))

    ka3, totals = barrier((ka3, totals))
    absorb("k", [ka3], (((0, 3),),))
    raw_keys = totals["k"]
    top = chip_top(raw_keys)
    smooth = smooth_of(top)
    vb2, top = barrier((vb2, top))
    far_query = lax.ppermute(vb2[depth:], "seq", line_pairs(3, 0, groups))
    va3 = send(vb2, 3, 0)
    va2, vb2, smooth = barrier((va2, vb2, smooth))
    absorb("v", [va2 + vb2], (((0, 2), (1, 2)),))
    queries = [
        value_block[depth:],
        va1[depth:],
        va2[depth:] + vb2[depth:],
        vb1[depth:] + far_query,
    ]

    def finish_values(scored, *args):
        args, totals["v"] = barrier((args, totals["v"]))
        probs, stats = scored(*args)
        block, stats = barrier((va3, stats))
        absorb("v", [block], (((0, 3),),))
        return probs, stats, totals["v"]

    return raw_keys, smooth, queries, early, finish_values


def on_device(
    hidden, key_weight, value_weight, group_scale, new_kv, decode_query, page_table, lengths
):
    tokens = hidden.shape[0]
    columns = key_weight.shape[1]
    groups, owners = lax.axis_size("seq"), lax.axis_size("rep")
    my_group, my_owner = lax.axis_index("seq"), lax.axis_index("rep")
    assert columns // HD == owners
    pages_dev = tokens // PAGE
    step_count, per_group = decode_query.shape[:2]

    owner_is = [my_owner == owner for owner in range(owners)]
    own_query = my_part(decode_query, 2, owner_is).reshape(step_count * per_group, -1)

    first_pages = [
        (my_group * owners + (my_owner - k) % owners) * pages_dev for k in range(owners)
    ]
    early = (
        jnp.stack([my_group, my_owner]),
        owner_is,
        first_pages,
        partner(my_group, jnp.arange(groups, dtype=jnp.int32), groups),
        own_query,
    )
    if groups == LINE:
        raw_keys, smooth, queries, early, finish_values = line_project(
            hidden, key_weight, value_weight, own_query, early
        )
    else:
        raw_keys, raw_values = (
            jnp.dot(
                hidden,
                lax.all_gather(weight, ("seq", "rep"), axis=0, tiled=True),
                preferred_element_type=jnp.float32,
            )
            for weight in (key_weight, value_weight)
        )
        queries = from_groups(
            jnp.concatenate(jnp.split(own_query, own_query.shape[1] // columns, axis=1))
        )
        smooth = smooth_of(chip_top(raw_keys))
    _, owner_is, first_pages, group_at, own_query = early
    counts = token_counts(page_table, lengths, first_pages, pages_dev)
    counts = counts.reshape(groups, per_group, -1)
    my_kv = my_part(new_kv, 3, owner_is).astype(jnp.float32)
    my_new = (my_kv[:, :, 0], my_kv[:, :, 1], my_part(group_scale, 1, owner_is))

    def by_head(x):
        return [my_part(x, 1, owner_is)] + [
            shifted(my_part(x, 1, owner_is, k), "rep", k) for k in range(1, owners)
        ]

    smoothing = smooth.reshape(-1)
    my_smooth = my_part(smooth, 1, owner_is)
    keys = clip_keys(raw_keys, smooth, group_scale)
    score_scale = HD ** (-0.5)
    scored = functools.partial(score, steps=step_count, scale=score_scale)
    args = (group_at, jnp.stack(queries), my_smooth, counts, by_head(keys))
    if groups == LINE:
        probs, stats, raw_values = finish_values(scored, *args)
    else:
        probs, stats = scored(*args)
    values = clip_values(raw_values, group_scale)
    messages = weigh(probs, by_head(values), stats)

    messages, keys, values, late = lax.optimization_barrier(
        (messages, keys, values, (own_query, my_smooth))
    )
    messages = to_groups(messages)
    is_key = lax.broadcasted_iota(jnp.int32, (1, 2, 1), 1) == 0
    kv_cache = jnp.where(is_key, keys[:, None, :], values[:, None, :])
    kv_cache = with_layout_constraint(kv_cache, Layout((0, 1, 2)))
    own = fresh(late[0], late[1], *my_new, score_scale)
    messages, kv_cache, own = lax.optimization_barrier((messages, kv_cache, own))
    attention = finish(messages, own, step_count * per_group)
    by_owner = from_owners(attention)
    attention = jnp.concatenate(
        [
            functools.reduce(
                lambda out, k: jnp.where(owner_is[(head + k) % owners], by_owner[k], out),
                range(1, owners),
                by_owner[0],
            )
            for head in range(owners)
        ],
        axis=1,
    ).reshape(decode_query.shape)
    return (kv_cache, smoothing, attention)


def solution(mesh):
    placed = (
        P(("seq", "rep"), None),
        P(("seq", "rep"), "head"),
        P(("seq", "rep"), "head"),
        P(None, "head"),
        P(None, "seq", None, "head"),
        P(None, "seq", "head"),
        P(),
        P(),
    )

    return jax.shard_map(
        on_device,
        mesh=mesh,
        in_specs=placed,
        out_specs=(P(("seq", "rep"), None, "head"), P("head"), P(None, "seq", "head")),
        check_vma=False,
    )
```

```python
import functools

import jax
import jax.numpy as jnp
from jax import lax
from jax.experimental import pallas as pl
from jax.experimental.layout import Layout, with_layout_constraint
from jax.experimental.pallas import tpu as pltpu
from jax.sharding import PartitionSpec as P


HD = 128
PAGE = 32


EPSILON = 1e-05
NEGATIVE = -1e30
LINE = 4


def shifted(x, axis, k):
    n = lax.axis_size(axis)
    return lax.ppermute(x, axis, [(i, (i + k) % n) for i in range(n)])


def partner(me, k, n):
    return me ^ k if n == LINE else (k - me) % n


def swapped(x, axis, k):
    n = lax.axis_size(axis)
    return lax.ppermute(x, axis, [(i, partner(i, k, n)) for i in range(n)])


def from_owners(x):
    return [x] + [shifted(x, "rep", k) for k in range(1, lax.axis_size("rep"))]


def from_groups(x):
    n = lax.axis_size("seq")
    if n != LINE:
        return list(lax.all_gather(x, "seq")[partner(lax.axis_index("seq"), jnp.arange(n), n)])
    return [x] + [swapped(x, "seq", k) for k in range(1, n)]


def to_groups(x):
    n = lax.axis_size("seq")
    if n != LINE:
        order = partner(lax.axis_index("seq"), jnp.arange(n), n)
        back = lax.all_to_all(jnp.stack(x)[order], "seq", split_axis=0, concat_axis=0)
        return list(back[order])
    return [x[0]] + [swapped(x[k], "seq", k) for k in range(1, n)]


def pack_kernel(weight, query, out, sem):
    depth, columns = weight.shape
    copy = pltpu.make_async_copy(weight, out.at[pl.ds(0, depth)], sem)
    copy.start()
    lines = query.shape[0]
    for k in range(query.shape[1] // columns):
        at = pl.ds(depth + k * lines, lines)
        out[at, :] = query[:, k * columns : (k + 1) * columns]
    copy.wait()


def pack(weight, query):
    depth, columns = weight.shape
    whole = pl.BlockSpec(memory_space=pltpu.VMEM)
    return pl.pallas_call(
        pack_kernel,
        out_shape=jax.ShapeDtypeStruct((depth + query.size // columns, columns), weight.dtype),
        in_specs=[pl.BlockSpec(memory_space=pl.ANY), whole],
        out_specs=whole,
        scratch_shapes=[pltpu.SemaphoreType.DMA],
        compiler_params=pltpu.CompilerParams(vmem_limit_bytes=8 * 2**20),
        name="pack",
    )(weight, query)


def load_kernel(owners, place, hidden, *refs):
    weights, (held, keys, values, taken, arrived, taken_arrived) = refs[:2], refs[2:]
    depth = taken.shape[1]
    blocks = held.shape[1] // depth
    takes = [
        pltpu.make_async_copy(weight.at[pl.ds(0, depth)], taken.at[j], taken_arrived.at[j])
        for j, weight in enumerate(weights)
    ]

    def block(j):
        index = lax.rem(place[0] * owners + place[1] + j, blocks)
        return pl.ds(pl.multiple_of(index * depth, depth), depth)

    def copy(j):
        return pltpu.make_async_copy(hidden.at[:, block(j)], held.at[:, block(j)], arrived.at[j])

    copy(0).start()
    for take in takes:
        take.start()
    for j in range(1, blocks):
        copy(j).start()
    copy(0).wait()
    for j, out in enumerate((keys, values)):
        takes[j].wait()
        out[...] = jnp.dot(held[:, block(0)], taken[j], preferred_element_type=jnp.float32)
    for j in range(1, blocks):
        copy(j).wait()


def load(hidden, key_weight, value_weight, place, owners):
    tokens, width = hidden.shape
    depth, columns = key_weight.shape
    whole = pl.BlockSpec(memory_space=pltpu.VMEM)
    total = jax.ShapeDtypeStruct((tokens, columns), jnp.float32)
    return pl.pallas_call(
        functools.partial(load_kernel, owners),
        out_shape=(jax.ShapeDtypeStruct(hidden.shape, hidden.dtype), total, total),
        in_specs=[
            pl.BlockSpec(memory_space=pltpu.SMEM),
            pl.BlockSpec(memory_space=pltpu.HBM),
            pl.BlockSpec(memory_space=pl.ANY),
            pl.BlockSpec(memory_space=pl.ANY),
        ],
        out_specs=(whole,) * 3,
        scratch_shapes=[
            pltpu.VMEM((2, depth, columns), key_weight.dtype),
            pltpu.SemaphoreType.DMA((width // depth,)),
            pltpu.SemaphoreType.DMA((2,)),
        ],
        compiler_params=pltpu.CompilerParams(vmem_limit_bytes=30 * 2**20),
        cost_estimate=pl.CostEstimate(
            flops=4 * tokens * depth * columns,
            bytes_accessed=2 * tokens * width,
            transcendentals=0,
        ),
        name="load",
    )(place, hidden, key_weight, value_weight)


def project_kernel(hops, back, groups, owners, place, left, *refs):
    count = len(hops)
    weights, total = refs[:count], refs[count]
    out, held, arrived = refs[-3:]
    depth = held.shape[1]
    copies = [
        pltpu.make_async_copy(weights[j].at[pl.ds(0, depth)], held.at[j], arrived.at[j])
        for j in range(count)
    ]
    for copy in copies:
        copy.start()
    out[...] = total[...]
    owner = lax.rem(place[1] + owners - back, owners)
    for j, copy in enumerate(copies):
        copy.wait()
        group = jnp.int32(-1)
        for parity, hop in hops[j]:
            there = place[0] + jnp.where(lax.rem(place[0], 2) == parity, hop, -hop)
            group = jnp.where((there >= 0) & (there < groups), there, group)

        @pl.when((group >= 0) & (group < groups))
        def _(j=j, group=group):
            block = pl.ds(pl.multiple_of((group * owners + owner) * depth, depth), depth)
            out[...] += jnp.dot(left[:, block], held[j], preferred_element_type=jnp.float32)


def project(hidden, total, weights, depth, place, hops, back, groups, owners):
    tokens = hidden.shape[0]
    columns = weights[0].shape[1]
    count = len(weights)
    whole = pl.BlockSpec(memory_space=pltpu.VMEM)
    return pl.pallas_call(
        functools.partial(project_kernel, hops, back, groups, owners),
        out_shape=jax.ShapeDtypeStruct((tokens, columns), jnp.float32),
        in_specs=[pl.BlockSpec(memory_space=pltpu.SMEM), whole]
        + [pl.BlockSpec(memory_space=pl.ANY)] * count
        + [whole],
        out_specs=whole,
        scratch_shapes=[
            pltpu.VMEM((count, depth, columns), weights[0].dtype),
            pltpu.SemaphoreType.DMA((count,)),
        ],
        compiler_params=pltpu.CompilerParams(vmem_limit_bytes=12 * 2**20),
        cost_estimate=pl.CostEstimate(
            flops=2 * tokens * depth * columns * count,
            bytes_accessed=2 * count * depth * (tokens + columns) + 8 * tokens * columns,
            transcendentals=0,
        ),
        input_output_aliases={2 + count: 0},
        name="project",
    )(place, hidden, *weights, total)


def score_kernel(slots, parts, steps, scale, group, query, smooth, count, *refs):
    keys, probs, stats = refs[:parts], refs[parts], refs[parts + 1 : parts + 1 + slots]
    scores, tops, sums = refs[-3:]
    tokens = keys[0].shape[0]
    width = keys[0].shape[1]
    requests = count.shape[1]
    rows = scores.shape[0]
    heads = query.shape[1] * query.shape[2] // (steps * requests * width)
    per_line = query.shape[2] // width
    raw = [
        query[0][
            (head // per_line) * steps * requests : (head // per_line + 1) * steps * requests,
            (head % per_line) * width : (head % per_line + 1) * width,
        ]
        for head in range(heads)
    ]
    raw = jnp.concatenate(raw, axis=0)
    scaled = (raw.astype(jnp.float32) * smooth[...]).astype(jnp.bfloat16)
    for p in range(parts):
        scores[:, p * tokens : (p + 1) * tokens] = lax.dot_general(
            scaled, keys[p][...], (((1,), (1,)), ((), ())), preferred_element_type=jnp.float32
        )
    again = 2 if (rows // requests) % 2 == 0 else 1
    times = jnp.concatenate([count[0]] * again, axis=0)
    bias = jnp.where(times > 0.0, 0.0, NEGATIVE)
    for start in range(0, rows, again * requests):
        at = pl.ds(start, again * requests)
        raw = scores[at, :] * scale + bias
        top = jnp.max(raw, axis=1, keepdims=True)
        counted = jnp.exp(raw - top) * times
        probs[0, at, :] = counted.astype(jnp.bfloat16)
        tops[at, :] = jnp.broadcast_to(top, (again * requests, 128))
        sums[at, :] = jnp.broadcast_to(
            jnp.sum(counted, axis=1, keepdims=True), (again * requests, 128)
        )
    for slot in range(slots):

        @pl.when(pl.program_id(0) == slot)
        def _(slot=slot):
            stats[slot][0:1, :] = jnp.transpose(tops[...])[0:1, :]
            stats[slot][1:2, :] = jnp.transpose(sums[...])[0:1, :]


def score(groups, query, smooth, count, keys, steps, scale):
    slots, packed, columns = query.shape
    tokens, width = keys[0].shape
    rows = packed * columns // width
    parts = len(keys)
    requests = count.shape[1]
    probs, *stats = pl.pallas_call(
        functools.partial(score_kernel, slots, parts, steps, scale),
        out_shape=[jax.ShapeDtypeStruct((slots, rows, parts * tokens), jnp.bfloat16)]
        + [jax.ShapeDtypeStruct((2, rows), jnp.float32)] * slots,
        grid_spec=pltpu.PrefetchScalarGridSpec(
            num_scalar_prefetch=1,
            grid=(slots,),
            in_specs=[
                pl.BlockSpec((1, packed, columns), lambda k, group: (k, 0, 0)),
                pl.BlockSpec((1, width), lambda k, group: (0, 0)),
                pl.BlockSpec((1, requests, parts * tokens), lambda k, group: (group[k], 0, 0)),
            ]
            + [pl.BlockSpec((tokens, width), lambda k, group: (0, 0))] * parts,
            out_specs=[pl.BlockSpec((1, rows, parts * tokens), lambda k, group: (k, 0, 0))]
            + [pl.BlockSpec((2, rows), lambda k, group: (0, 0))] * slots,
            scratch_shapes=[
                pltpu.VMEM((rows, parts * tokens), jnp.float32),
                pltpu.VMEM((rows, 128), jnp.float32),
                pltpu.VMEM((rows, 128), jnp.float32),
            ],
        ),
        compiler_params=pltpu.CompilerParams(vmem_limit_bytes=16 * 2**20),
        cost_estimate=pl.CostEstimate(
            flops=2 * slots * rows * width * parts * tokens,
            bytes_accessed=2 * slots * rows * parts * tokens,
            transcendentals=slots * rows * parts * tokens,
        ),
        name="score",
    )(groups, query, smooth, count, *keys)
    return probs, stats


def thirds(x):
    out = []
    for _ in range(3):
        out.append(x.astype(jnp.bfloat16))
        x = x - out[-1].astype(jnp.float32)
    return out


def weigh_kernel(slots, parts, probs, *refs):
    values, stats, outs = refs[:parts], refs[parts : parts + slots], refs[parts + slots :]
    tokens, width = values[0].shape
    rows = probs.shape[1]
    summed = sum(
        jnp.dot(
            probs[0, :, p * tokens : (p + 1) * tokens],
            values[p][...],
            preferred_element_type=jnp.float32,
        )
        for p in range(parts)
    ).astype(jnp.bfloat16)
    for slot in range(slots):

        @pl.when(pl.program_id(0) == slot)
        def _(slot=slot):
            outs[slot][0:rows, :] = summed
            lines = []
            for third in thirds(stats[slot][...]):
                third = third.astype(jnp.float32)
                lines += [third[:, c : c + width] for c in range(0, rows, width)]
            tail = outs[slot].shape[0] - rows
            lines.append(jnp.zeros((tail - 2 * len(lines), width), jnp.float32))
            outs[slot][rows:, :] = jnp.concatenate(lines, axis=0).astype(jnp.bfloat16)


def packed_rows(rows, width):
    return rows + (6 * (rows // width) // 16 + 1) * 16


def weigh(probs, values, stats):
    slots, rows, _ = probs.shape
    tokens, width = values[0].shape
    parts = len(values)
    total_rows = packed_rows(rows, width)
    return pl.pallas_call(
        functools.partial(weigh_kernel, slots, parts),
        out_shape=[jax.ShapeDtypeStruct((total_rows, width), jnp.bfloat16)] * slots,
        grid=(slots,),
        in_specs=[pl.BlockSpec((1, rows, parts * tokens), lambda k: (k, 0, 0))]
        + [pl.BlockSpec((tokens, width), lambda k: (0, 0))] * parts
        + [pl.BlockSpec((2, rows), lambda k: (0, 0))] * slots,
        out_specs=[pl.BlockSpec((total_rows, width), lambda k: (0, 0))] * slots,
        compiler_params=pltpu.CompilerParams(vmem_limit_bytes=16 * 2**20),
        cost_estimate=pl.CostEstimate(
            flops=2 * slots * rows * width * parts * tokens,
            bytes_accessed=2 * slots * rows * parts * tokens,
            transcendentals=0,
        ),
        name="weigh",
    )(probs, *values, *stats)


def fresh_kernel(scale, query, smooth, new_keys, new_values, group_scale, summed, highest, total):
    steps, requests, width = new_keys.shape
    lines = steps * requests

    def by_line(x):
        x = x.astype(jnp.bfloat16).astype(jnp.float32)
        return jnp.concatenate([x] * steps, axis=0)

    def clip(x, row):
        limit = group_scale[row : row + 1, :]
        return jnp.clip(x, -8.0 * limit, 7.0 * limit)

    keys = [by_line(clip(new_keys[u] / smooth[...], 0)) for u in range(steps)]
    values = [by_line(clip(new_values[u], 1)) for u in range(steps)]
    line = lax.broadcasted_iota(jnp.int32, (lines, 1), 0)
    seen = [line >= u * requests for u in range(steps)]
    for head in range(query.shape[1] // width):
        at = pl.ds(head * lines, lines)
        mine = query[:, head * width : (head + 1) * width].astype(jnp.float32) * smooth[...]
        mine = mine.astype(jnp.bfloat16).astype(jnp.float32)
        scores = [
            jnp.where(seen[u], jnp.sum(mine * keys[u], axis=1, keepdims=True) * scale, NEGATIVE)
            for u in range(steps)
        ]
        top = functools.reduce(jnp.maximum, scores)
        expd = [jnp.where(seen[u], jnp.exp(scores[u] - top), 0.0) for u in range(steps)]
        highest[at, :] = jnp.broadcast_to(top, (lines, width))
        total[at, :] = jnp.broadcast_to(sum(expd), (lines, width))
        summed[at, :] = sum(
            e.astype(jnp.bfloat16).astype(jnp.float32) * value for e, value in zip(expd, values)
        )


def fresh(query, smooth, new_keys, new_values, group_scale, scale):
    lines, columns = query.shape
    width = smooth.shape[1]
    part = jax.ShapeDtypeStruct((lines * columns // width, width), jnp.float32)
    return pl.pallas_call(
        functools.partial(fresh_kernel, scale),
        out_shape=(part,) * 3,
        compiler_params=pltpu.CompilerParams(vmem_limit_bytes=16 * 2**20),
        name="fresh",
    )(query, smooth, new_keys, new_values, group_scale)


def finish_kernel(slots, *refs):
    messages, (summed, highest, total, out) = refs[:slots], refs[slots:]
    rows, width = summed.shape
    lines = out.shape[0]
    tails = [message[rows:, :].astype(jnp.float32) for message in messages]
    pieces = rows // width

    def column(slot, piece, which):
        row = [tails[slot][2 * (j * pieces + piece) + which :][:1] for j in range(3)]
        return jnp.transpose(jnp.broadcast_to(row[0] + row[1] + row[2], (width, width)))

    for piece in range(pieces):
        at = pl.ds(piece * width, width)
        parts = [
            (messages[k][at, :].astype(jnp.float32), column(k, piece, 0), column(k, piece, 1))
            for k in range(slots)
        ]
        parts.append((summed[at, :], highest[at, :], total[at, :]))
        top = functools.reduce(jnp.maximum, [part[1] for part in parts])
        shares = [jnp.exp(part[1] - top) for part in parts]
        norm = sum(share * part[2] for share, part in zip(shares, parts))
        merged = sum(share * part[0] for share, part in zip(shares, parts)) / norm
        merged = merged.astype(out.dtype)
        for first in range(0, width, lines):
            head = (piece * width + first) // lines
            out[:, head * width : (head + 1) * width] = merged[first : first + lines]


def finish(messages, own, lines):
    rows, width = own[0].shape
    return pl.pallas_call(
        functools.partial(finish_kernel, len(messages)),
        out_shape=jax.ShapeDtypeStruct((lines, rows * width // lines), jnp.bfloat16),
        compiler_params=pltpu.CompilerParams(vmem_limit_bytes=16 * 2**20),
        name="finish",
    )(*messages, *own)


def token_counts(page_table, lengths, first_pages, pages_dev):
    slots = page_table.shape[1]
    slot_ids = jnp.arange(slots, dtype=jnp.int32)
    whole_slots, rest = lengths // PAGE, lengths % PAGE
    pages = jnp.concatenate(
        [first + jnp.arange(pages_dev, dtype=jnp.int32) for first in first_pages]
    )
    same = page_table[:, :, None] == pages[None, None, :]
    whole = jnp.sum(same & (slot_ids[None, :] < whole_slots[:, None])[:, :, None], axis=1)
    last = jnp.sum(same & (slot_ids[None, :] == whole_slots[:, None])[:, :, None], axis=1)
    token = jnp.arange(pages.shape[0] * PAGE, dtype=jnp.int32)
    spread = token[None, :] // PAGE == jnp.arange(pages.shape[0], dtype=jnp.int32)[:, None]
    spread = spread.astype(jnp.bfloat16)
    whole = jnp.dot(whole.astype(jnp.bfloat16), spread, preferred_element_type=jnp.float32)
    last = jnp.dot(last.astype(jnp.bfloat16), spread, preferred_element_type=jnp.float32)
    return whole + jnp.where((token % PAGE)[None, :] < rest[:, None], last, 0.0)


def clip_keys(raw, smooth, scale):
    return jnp.clip(raw / smooth, -8.0 * scale[0], 7.0 * scale[0]).astype(jnp.bfloat16)


def clip_values(raw, scale):
    return jnp.clip(raw, -8.0 * scale[1], 7.0 * scale[1]).astype(jnp.bfloat16)


def my_part(x, axis, owner_is, ahead=0):
    owners = len(owner_is)
    size = x.shape[axis] // owners
    pieces = [lax.slice_in_dim(x, p * size, (p + 1) * size, axis=axis) for p in range(owners)]
    out = pieces[0]
    for p in range(1, owners):
        out = jnp.where(owner_is[(p - ahead) % owners], pieces[p], out)
    return out


def chip_top(raw_keys):
    top = jnp.max(jnp.abs(raw_keys), axis=0, keepdims=True)
    return functools.reduce(jnp.maximum, from_owners(top))


def smooth_of(top):
    top = functools.reduce(jnp.maximum, from_groups(top))
    return jnp.sqrt(top + EPSILON)


def line_pairs(hop, parity, groups):
    pairs = []
    for i in range(parity, groups - 1, 2):
        if i >= hop - 1:
            pairs.append((i, i + 1))
        if i + hop < groups:
            pairs.append((i + 1, i))
    return pairs


def line_project(hidden, key_weight, value_weight, own_query, early):
    groups, owners = lax.axis_size("seq"), lax.axis_size("rep")
    depth = key_weight.shape[0]
    barrier = lax.optimization_barrier

    def send(x, hop, parity):
        return lax.ppermute(x, "seq", line_pairs(hop, parity, groups))

    def absorb(name, blocks, hops, first=0):
        passed = [[shifted(block, "rep", k) for block in blocks] for k in range(1, owners)]
        for k, ready in enumerate([blocks] + passed):
            if k < first:
                continue
            totals[name] = project(
                hidden, totals[name], ready, depth, early[0], hops, k, groups, owners
            )

    totals = {}
    ka1 = send(key_weight, 1, 0)
    kb1 = send(key_weight, 1, 1)
    value_block = pack(value_weight, own_query)
    va1 = send(value_block, 1, 0)
    early, first = barrier((early, (key_weight, value_block)))
    hidden, totals["k"], totals["v"] = load(hidden, *first, early[0], owners)

    ka1, kb1, value_block, totals = barrier((ka1, kb1, value_block, totals))
    kb2 = send(ka1, 2, 1)
    ka2 = send(kb1, 2, 0)
    vb1 = send(value_block, 1, 1)
    for name, weight in (("k", key_weight), ("v", value_weight)):
        absorb(name, [weight], (((0, 0),),), 1)
    absorb("k", [ka1, kb1], (((0, 1),), ((1, 1),)))

    kb2, va1, own_block, totals = barrier((kb2, va1, value_block, totals))
    ends = [(0, groups - 1), (groups - 1, 0)]
    far_query = lax.ppermute(own_block[depth:], "seq", ends)
    ka3 = send(kb2, 3, 0)
    vb2 = send(va1, 2, 1)
    absorb("v", [va1], (((0, 1),),))

    ka2, totals = barrier((ka2, totals))
    absorb("k", [ka2 + kb2], (((0, 2), (1, 2)),))

    vb1, totals = barrier((vb1, totals))
    va2 = send(vb1, 2, 0)
    absorb("v", [vb1], (((1, 1),),))

    ka3, totals = barrier((ka3, totals))
    absorb("k", [ka3], (((0, 3),),))
    raw_keys = totals["k"]
    top = chip_top(raw_keys)
    smooth = smooth_of(top)
    vb2, top = barrier((vb2, top))
    va3 = send(vb2, 3, 0)
    va2, vb2, smooth = barrier((va2, vb2, smooth))
    absorb("v", [va2 + vb2], (((0, 2), (1, 2)),))
    queries = [
        value_block[depth:],
        va1[depth:],
        va2[depth:] + vb2[depth:],
        vb1[depth:] + far_query,
    ]

    def finish_values(scored, *args):
        args, totals["v"] = barrier((args, totals["v"]))
        probs, stats = scored(*args)
        block, stats = barrier((va3, stats))
        absorb("v", [block], (((0, 3),),))
        return probs, stats, totals["v"]

    return raw_keys, smooth, queries, early, finish_values


def on_device(
    hidden, key_weight, value_weight, group_scale, new_kv, decode_query, page_table, lengths
):
    tokens = hidden.shape[0]
    columns = key_weight.shape[1]
    groups, owners = lax.axis_size("seq"), lax.axis_size("rep")
    my_group, my_owner = lax.axis_index("seq"), lax.axis_index("rep")
    assert columns // HD == owners
    pages_dev = tokens // PAGE
    step_count, per_group = decode_query.shape[:2]

    owner_is = [my_owner == owner for owner in range(owners)]
    own_query = my_part(decode_query, 2, owner_is).reshape(step_count * per_group, -1)

    first_pages = [
        (my_group * owners + (my_owner - k) % owners) * pages_dev for k in range(owners)
    ]
    early = (
        jnp.stack([my_group, my_owner]),
        owner_is,
        first_pages,
        partner(my_group, jnp.arange(groups, dtype=jnp.int32), groups),
        own_query,
    )
    if groups == LINE:
        raw_keys, smooth, queries, early, finish_values = line_project(
            hidden, key_weight, value_weight, own_query, early
        )
    else:
        raw_keys, raw_values = (
            jnp.dot(
                hidden,
                lax.all_gather(weight, ("seq", "rep"), axis=0, tiled=True),
                preferred_element_type=jnp.float32,
            )
            for weight in (key_weight, value_weight)
        )
        queries = from_groups(
            jnp.concatenate(jnp.split(own_query, own_query.shape[1] // columns, axis=1))
        )
        smooth = smooth_of(chip_top(raw_keys))
    _, owner_is, first_pages, group_at, own_query = early
    counts = token_counts(page_table, lengths, first_pages, pages_dev)
    counts = counts.reshape(groups, per_group, -1)
    my_kv = my_part(new_kv, 3, owner_is).astype(jnp.float32)
    my_new = (my_kv[:, :, 0], my_kv[:, :, 1], my_part(group_scale, 1, owner_is))

    def by_head(x):
        return [my_part(x, 1, owner_is)] + [
            shifted(my_part(x, 1, owner_is, k), "rep", k) for k in range(1, owners)
        ]

    smoothing = smooth.reshape(-1)
    my_smooth = my_part(smooth, 1, owner_is)
    keys = clip_keys(raw_keys, smooth, group_scale)
    score_scale = HD ** (-0.5)
    scored = functools.partial(score, steps=step_count, scale=score_scale)
    args = (group_at, jnp.stack(queries), my_smooth, counts, by_head(keys))
    if groups == LINE:
        probs, stats, raw_values = finish_values(scored, *args)
    else:
        probs, stats = scored(*args)
    values = clip_values(raw_values, group_scale)
    messages = weigh(probs, by_head(values), stats)

    messages, keys, values, late = lax.optimization_barrier(
        (messages, keys, values, (own_query, my_smooth))
    )
    messages = to_groups(messages)
    is_key = lax.broadcasted_iota(jnp.int32, (1, 2, 1), 1) == 0
    kv_cache = jnp.where(is_key, keys[:, None, :], values[:, None, :])
    kv_cache = with_layout_constraint(kv_cache, Layout((0, 1, 2)))
    own = fresh(late[0], late[1], *my_new, score_scale)
    messages, kv_cache, own = lax.optimization_barrier((messages, kv_cache, own))
    attention = finish(messages, own, step_count * per_group)
    by_owner = from_owners(attention)
    attention = jnp.concatenate(
        [
            functools.reduce(
                lambda out, k: jnp.where(owner_is[(head + k) % owners], by_owner[k], out),
                range(1, owners),
                by_owner[0],
            )
            for head in range(owners)
        ],
        axis=1,
    ).reshape(decode_query.shape)
    return (kv_cache, smoothing, attention)


def solution(mesh):
    placed = (
        P(("seq", "rep"), None),
        P(("seq", "rep"), "head"),
        P(("seq", "rep"), "head"),
        P(None, "head"),
        P(None, "seq", None, "head"),
        P(None, "seq", "head"),
        P(),
        P(),
    )

    return jax.shard_map(
        on_device,
        mesh=mesh,
        in_specs=placed,
        out_specs=(P(("seq", "rep"), None, "head"), P("head"), P(None, "seq", "head")),
        check_vma=False,
    )
```

```python
import functools

import jax
import jax.numpy as jnp
from jax import lax
from jax.experimental import pallas as pl
from jax.experimental.layout import Layout, with_layout_constraint
from jax.experimental.pallas import tpu as pltpu
from jax.sharding import PartitionSpec as P


HD = 128
PAGE = 32


EPSILON = 1e-05
NEGATIVE = -1e30
LINE = 4


def shifted(x, axis, k):
    n = lax.axis_size(axis)
    return lax.ppermute(x, axis, [(i, (i + k) % n) for i in range(n)])


def partner(me, k, n):
    return me ^ k if n == LINE else (k - me) % n


def swapped(x, axis, k):
    n = lax.axis_size(axis)
    return lax.ppermute(x, axis, [(i, partner(i, k, n)) for i in range(n)])


def from_owners(x):
    return [x] + [shifted(x, "rep", k) for k in range(1, lax.axis_size("rep"))]


def from_groups(x):
    n = lax.axis_size("seq")
    if n != LINE:
        return list(lax.all_gather(x, "seq")[partner(lax.axis_index("seq"), jnp.arange(n), n)])
    return [x] + [swapped(x, "seq", k) for k in range(1, n)]


def to_groups(x):
    n = lax.axis_size("seq")
    if n != LINE:
        order = partner(lax.axis_index("seq"), jnp.arange(n), n)
        back = lax.all_to_all(jnp.stack(x)[order], "seq", split_axis=0, concat_axis=0)
        return list(back[order])
    return [x[0]] + [swapped(x[k], "seq", k) for k in range(1, n)]


def pack_kernel(weight, query, out, sem):
    depth, columns = weight.shape
    copy = pltpu.make_async_copy(weight, out.at[pl.ds(0, depth)], sem)
    copy.start()
    lines = query.shape[0]
    for k in range(query.shape[1] // columns):
        at = pl.ds(depth + k * lines, lines)
        out[at, :] = query[:, k * columns : (k + 1) * columns]
    copy.wait()


def pack(weight, query):
    depth, columns = weight.shape
    whole = pl.BlockSpec(memory_space=pltpu.VMEM)
    return pl.pallas_call(
        pack_kernel,
        out_shape=jax.ShapeDtypeStruct((depth + query.size // columns, columns), weight.dtype),
        in_specs=[pl.BlockSpec(memory_space=pl.ANY), whole],
        out_specs=whole,
        scratch_shapes=[pltpu.SemaphoreType.DMA],
        compiler_params=pltpu.CompilerParams(vmem_limit_bytes=8 * 2**20),
        name="pack",
    )(weight, query)


def load_kernel(owners, place, hidden, *refs):
    weights, (held, keys, values, taken, arrived, taken_arrived) = refs[:2], refs[2:]
    depth = taken.shape[1]
    blocks = held.shape[1] // depth
    takes = [
        pltpu.make_async_copy(weight.at[pl.ds(0, depth)], taken.at[j], taken_arrived.at[j])
        for j, weight in enumerate(weights)
    ]

    def block(j):
        index = lax.rem(place[0] * owners + place[1] + j, blocks)
        return pl.ds(pl.multiple_of(index * depth, depth), depth)

    def copy(j):
        return pltpu.make_async_copy(hidden.at[:, block(j)], held.at[:, block(j)], arrived.at[j])

    copy(0).start()
    for take in takes:
        take.start()
    for j in range(1, blocks):
        copy(j).start()
    copy(0).wait()
    for j, out in enumerate((keys, values)):
        takes[j].wait()
        out[...] = jnp.dot(held[:, block(0)], taken[j], preferred_element_type=jnp.float32)
    for j in range(1, blocks):
        copy(j).wait()


def load(hidden, key_weight, value_weight, place, owners):
    tokens, width = hidden.shape
    depth, columns = key_weight.shape
    whole = pl.BlockSpec(memory_space=pltpu.VMEM)
    total = jax.ShapeDtypeStruct((tokens, columns), jnp.float32)
    return pl.pallas_call(
        functools.partial(load_kernel, owners),
        out_shape=(jax.ShapeDtypeStruct(hidden.shape, hidden.dtype), total, total),
        in_specs=[
            pl.BlockSpec(memory_space=pltpu.SMEM),
            pl.BlockSpec(memory_space=pltpu.HBM),
            pl.BlockSpec(memory_space=pl.ANY),
            pl.BlockSpec(memory_space=pl.ANY),
        ],
        out_specs=(whole,) * 3,
        scratch_shapes=[
            pltpu.VMEM((2, depth, columns), key_weight.dtype),
            pltpu.SemaphoreType.DMA((width // depth,)),
            pltpu.SemaphoreType.DMA((2,)),
        ],
        compiler_params=pltpu.CompilerParams(vmem_limit_bytes=30 * 2**20),
        cost_estimate=pl.CostEstimate(
            flops=4 * tokens * depth * columns,
            bytes_accessed=2 * tokens * width,
            transcendentals=0,
        ),
        name="load",
    )(place, hidden, key_weight, value_weight)


def project_kernel(hops, back, groups, owners, place, left, *refs):
    count = len(hops)
    weights, total = refs[:count], refs[count]
    out, held, arrived = refs[-3:]
    depth = held.shape[1]
    copies = [
        pltpu.make_async_copy(weights[j].at[pl.ds(0, depth)], held.at[j], arrived.at[j])
        for j in range(count)
    ]
    for copy in copies:
        copy.start()
    out[...] = total[...]
    owner = lax.rem(place[1] + owners - back, owners)
    for j, copy in enumerate(copies):
        copy.wait()
        group = jnp.int32(-1)
        for parity, hop in hops[j]:
            there = place[0] + jnp.where(lax.rem(place[0], 2) == parity, hop, -hop)
            group = jnp.where((there >= 0) & (there < groups), there, group)

        @pl.when((group >= 0) & (group < groups))
        def _(j=j, group=group):
            block = pl.ds(pl.multiple_of((group * owners + owner) * depth, depth), depth)
            out[...] += jnp.dot(left[:, block], held[j], preferred_element_type=jnp.float32)


def project(hidden, total, weights, depth, place, hops, back, groups, owners):
    tokens = hidden.shape[0]
    columns = weights[0].shape[1]
    count = len(weights)
    whole = pl.BlockSpec(memory_space=pltpu.VMEM)
    return pl.pallas_call(
        functools.partial(project_kernel, hops, back, groups, owners),
        out_shape=jax.ShapeDtypeStruct((tokens, columns), jnp.float32),
        in_specs=[pl.BlockSpec(memory_space=pltpu.SMEM), whole]
        + [pl.BlockSpec(memory_space=pl.ANY)] * count
        + [whole],
        out_specs=whole,
        scratch_shapes=[
            pltpu.VMEM((count, depth, columns), weights[0].dtype),
            pltpu.SemaphoreType.DMA((count,)),
        ],
        compiler_params=pltpu.CompilerParams(vmem_limit_bytes=12 * 2**20),
        cost_estimate=pl.CostEstimate(
            flops=2 * tokens * depth * columns * count,
            bytes_accessed=2 * count * depth * (tokens + columns) + 8 * tokens * columns,
            transcendentals=0,
        ),
        input_output_aliases={2 + count: 0},
        name="project",
    )(place, hidden, *weights, total)


def score_kernel(slots, parts, steps, scale, group, query, smooth, count, *refs):
    keys, probs, stats = refs[:parts], refs[parts], refs[parts + 1 : parts + 1 + slots]
    scores, tops, sums = refs[-3:]
    tokens = keys[0].shape[0]
    width = keys[0].shape[1]
    requests = count.shape[1]
    rows = scores.shape[0]
    heads = query.shape[1] * query.shape[2] // (steps * requests * width)
    per_line = query.shape[2] // width
    raw = [
        query[0][
            (head // per_line) * steps * requests : (head // per_line + 1) * steps * requests,
            (head % per_line) * width : (head % per_line + 1) * width,
        ]
        for head in range(heads)
    ]
    raw = jnp.concatenate(raw, axis=0)
    scaled = (raw.astype(jnp.float32) * smooth[...]).astype(jnp.bfloat16)
    for p in range(parts):
        scores[:, p * tokens : (p + 1) * tokens] = lax.dot_general(
            scaled, keys[p][...], (((1,), (1,)), ((), ())), preferred_element_type=jnp.float32
        )
    again = 2 if (rows // requests) % 2 == 0 else 1
    times = jnp.concatenate([count[0]] * again, axis=0)
    bias = jnp.where(times > 0.0, 0.0, NEGATIVE)
    for start in range(0, rows, again * requests):
        at = pl.ds(start, again * requests)
        raw = scores[at, :] * scale + bias
        top = jnp.max(raw, axis=1, keepdims=True)
        counted = jnp.exp(raw - top) * times
        probs[0, at, :] = counted.astype(jnp.bfloat16)
        tops[at, :] = jnp.broadcast_to(top, (again * requests, 128))
        sums[at, :] = jnp.broadcast_to(
            jnp.sum(counted, axis=1, keepdims=True), (again * requests, 128)
        )
    for slot in range(slots):

        @pl.when(pl.program_id(0) == slot)
        def _(slot=slot):
            stats[slot][0:1, :] = jnp.transpose(tops[...])[0:1, :]
            stats[slot][1:2, :] = jnp.transpose(sums[...])[0:1, :]


def score(groups, query, smooth, count, keys, steps, scale):
    slots, packed, columns = query.shape
    tokens, width = keys[0].shape
    rows = packed * columns // width
    parts = len(keys)
    requests = count.shape[1]
    probs, *stats = pl.pallas_call(
        functools.partial(score_kernel, slots, parts, steps, scale),
        out_shape=[jax.ShapeDtypeStruct((slots, rows, parts * tokens), jnp.bfloat16)]
        + [jax.ShapeDtypeStruct((2, rows), jnp.float32)] * slots,
        grid_spec=pltpu.PrefetchScalarGridSpec(
            num_scalar_prefetch=1,
            grid=(slots,),
            in_specs=[
                pl.BlockSpec((1, packed, columns), lambda k, group: (k, 0, 0)),
                pl.BlockSpec((1, width), lambda k, group: (0, 0)),
                pl.BlockSpec((1, requests, parts * tokens), lambda k, group: (group[k], 0, 0)),
            ]
            + [pl.BlockSpec((tokens, width), lambda k, group: (0, 0))] * parts,
            out_specs=[pl.BlockSpec((1, rows, parts * tokens), lambda k, group: (k, 0, 0))]
            + [pl.BlockSpec((2, rows), lambda k, group: (0, 0))] * slots,
            scratch_shapes=[
                pltpu.VMEM((rows, parts * tokens), jnp.float32),
                pltpu.VMEM((rows, 128), jnp.float32),
                pltpu.VMEM((rows, 128), jnp.float32),
            ],
        ),
        compiler_params=pltpu.CompilerParams(vmem_limit_bytes=16 * 2**20),
        cost_estimate=pl.CostEstimate(
            flops=2 * slots * rows * width * parts * tokens,
            bytes_accessed=2 * slots * rows * parts * tokens,
            transcendentals=slots * rows * parts * tokens,
        ),
        name="score",
    )(groups, query, smooth, count, *keys)
    return probs, stats


def thirds(x):
    out = []
    for _ in range(3):
        out.append(x.astype(jnp.bfloat16))
        x = x - out[-1].astype(jnp.float32)
    return out


def weigh_own_kernel(probs, values, out):
    out[0] = jnp.dot(probs[0], values[...], preferred_element_type=jnp.float32)


def weigh_kernel(slots, parts, own, *refs):
    probs, values = refs[:parts], refs[parts : 2 * parts]
    stats, outs = refs[2 * parts : 2 * parts + slots], refs[2 * parts + slots :]
    rows, width = own.shape[1:]
    summed = own[0]
    for p in range(parts):
        summed += jnp.dot(probs[p][0], values[p][...], preferred_element_type=jnp.float32)
    for slot in range(slots):

        @pl.when(pl.program_id(0) == slot)
        def _(slot=slot):
            outs[slot][0:rows, :] = summed.astype(jnp.bfloat16)
            lines = []
            for third in thirds(stats[slot][...]):
                third = third.astype(jnp.float32)
                lines += [third[:, c : c + width] for c in range(0, rows, width)]
            tail = outs[slot].shape[0] - rows
            lines.append(jnp.zeros((tail - 2 * len(lines), width), jnp.float32))
            outs[slot][rows:, :] = jnp.concatenate(lines, axis=0).astype(jnp.bfloat16)


def packed_rows(rows, width):
    return rows + (6 * (rows // width) // 16 + 1) * 16


def weigh(probs, values, stats):
    slots, rows, _ = probs.shape
    tokens, width = values[0].shape
    parts = len(values) - 1
    total_rows = packed_rows(rows, width)
    flops = 2 * slots * rows * width * tokens

    def probs_spec(p):
        return pl.BlockSpec((1, rows, tokens), lambda k, p=p: (k, 0, p))

    values_spec = pl.BlockSpec((tokens, width), lambda k: (0, 0))
    own_spec = pl.BlockSpec((1, rows, width), lambda k: (k, 0, 0))
    own = pl.pallas_call(
        weigh_own_kernel,
        out_shape=jax.ShapeDtypeStruct((slots, rows, width), jnp.float32),
        grid=(slots,),
        in_specs=[probs_spec(0), values_spec],
        out_specs=own_spec,
        compiler_params=pltpu.CompilerParams(vmem_limit_bytes=16 * 2**20),
        cost_estimate=pl.CostEstimate(
            flops=flops, bytes_accessed=2 * slots * rows * tokens, transcendentals=0
        ),
        name="weigh_own",
    )(probs, values[0])
    return pl.pallas_call(
        functools.partial(weigh_kernel, slots, parts),
        out_shape=[jax.ShapeDtypeStruct((total_rows, width), jnp.bfloat16)] * slots,
        grid=(slots,),
        in_specs=[own_spec]
        + [probs_spec(p + 1) for p in range(parts)]
        + [values_spec] * parts
        + [pl.BlockSpec((2, rows), lambda k: (0, 0))] * slots,
        out_specs=[pl.BlockSpec((total_rows, width), lambda k: (0, 0))] * slots,
        compiler_params=pltpu.CompilerParams(vmem_limit_bytes=16 * 2**20),
        cost_estimate=pl.CostEstimate(
            flops=flops * parts,
            bytes_accessed=2 * slots * rows * tokens * parts,
            transcendentals=0,
        ),
        name="weigh",
    )(own, *([probs] * parts), *values[1:], *stats)


def fresh_kernel(scale, query, smooth, new_keys, new_values, group_scale, summed, highest, total):
    steps, requests, width = new_keys.shape
    lines = steps * requests

    def by_line(x):
        x = x.astype(jnp.bfloat16).astype(jnp.float32)
        return jnp.concatenate([x] * steps, axis=0)

    def clip(x, row):
        limit = group_scale[row : row + 1, :]
        return jnp.clip(x, -8.0 * limit, 7.0 * limit)

    keys = [by_line(clip(new_keys[u] / smooth[...], 0)) for u in range(steps)]
    values = [by_line(clip(new_values[u], 1)) for u in range(steps)]
    line = lax.broadcasted_iota(jnp.int32, (lines, 1), 0)
    seen = [line >= u * requests for u in range(steps)]
    for head in range(query.shape[1] // width):
        at = pl.ds(head * lines, lines)
        mine = query[:, head * width : (head + 1) * width].astype(jnp.float32) * smooth[...]
        mine = mine.astype(jnp.bfloat16).astype(jnp.float32)
        scores = [
            jnp.where(seen[u], jnp.sum(mine * keys[u], axis=1, keepdims=True) * scale, NEGATIVE)
            for u in range(steps)
        ]
        top = functools.reduce(jnp.maximum, scores)
        expd = [jnp.where(seen[u], jnp.exp(scores[u] - top), 0.0) for u in range(steps)]
        highest[at, :] = jnp.broadcast_to(top, (lines, width))
        total[at, :] = jnp.broadcast_to(sum(expd), (lines, width))
        summed[at, :] = sum(
            e.astype(jnp.bfloat16).astype(jnp.float32) * value for e, value in zip(expd, values)
        )


def fresh(query, smooth, new_keys, new_values, group_scale, scale):
    lines, columns = query.shape
    width = smooth.shape[1]
    part = jax.ShapeDtypeStruct((lines * columns // width, width), jnp.float32)
    return pl.pallas_call(
        functools.partial(fresh_kernel, scale),
        out_shape=(part,) * 3,
        compiler_params=pltpu.CompilerParams(vmem_limit_bytes=16 * 2**20),
        name="fresh",
    )(query, smooth, new_keys, new_values, group_scale)


def finish_kernel(slots, *refs):
    messages, (summed, highest, total, out) = refs[:slots], refs[slots:]
    rows, width = summed.shape
    lines = out.shape[0]
    tails = [message[rows:, :].astype(jnp.float32) for message in messages]
    pieces = rows // width

    def column(slot, piece, which):
        row = [tails[slot][2 * (j * pieces + piece) + which :][:1] for j in range(3)]
        return jnp.transpose(jnp.broadcast_to(row[0] + row[1] + row[2], (width, width)))

    for piece in range(pieces):
        at = pl.ds(piece * width, width)
        parts = [
            (messages[k][at, :].astype(jnp.float32), column(k, piece, 0), column(k, piece, 1))
            for k in range(slots)
        ]
        parts.append((summed[at, :], highest[at, :], total[at, :]))
        top = functools.reduce(jnp.maximum, [part[1] for part in parts])
        shares = [jnp.exp(part[1] - top) for part in parts]
        norm = sum(share * part[2] for share, part in zip(shares, parts))
        merged = sum(share * part[0] for share, part in zip(shares, parts)) / norm
        merged = merged.astype(out.dtype)
        for first in range(0, width, lines):
            head = (piece * width + first) // lines
            out[:, head * width : (head + 1) * width] = merged[first : first + lines]


def finish(messages, own, lines):
    rows, width = own[0].shape
    return pl.pallas_call(
        functools.partial(finish_kernel, len(messages)),
        out_shape=jax.ShapeDtypeStruct((lines, rows * width // lines), jnp.bfloat16),
        compiler_params=pltpu.CompilerParams(vmem_limit_bytes=16 * 2**20),
        name="finish",
    )(*messages, *own)


def token_counts(page_table, lengths, first_pages, pages_dev):
    slots = page_table.shape[1]
    slot_ids = jnp.arange(slots, dtype=jnp.int32)
    whole_slots, rest = lengths // PAGE, lengths % PAGE
    pages = jnp.concatenate(
        [first + jnp.arange(pages_dev, dtype=jnp.int32) for first in first_pages]
    )
    same = page_table[:, :, None] == pages[None, None, :]
    whole = jnp.sum(same & (slot_ids[None, :] < whole_slots[:, None])[:, :, None], axis=1)
    last = jnp.sum(same & (slot_ids[None, :] == whole_slots[:, None])[:, :, None], axis=1)
    token = jnp.arange(pages.shape[0] * PAGE, dtype=jnp.int32)
    spread = token[None, :] // PAGE == jnp.arange(pages.shape[0], dtype=jnp.int32)[:, None]
    spread = spread.astype(jnp.bfloat16)
    whole = jnp.dot(whole.astype(jnp.bfloat16), spread, preferred_element_type=jnp.float32)
    last = jnp.dot(last.astype(jnp.bfloat16), spread, preferred_element_type=jnp.float32)
    return whole + jnp.where((token % PAGE)[None, :] < rest[:, None], last, 0.0)


def clip_keys(raw, smooth, scale):
    return jnp.clip(raw / smooth, -8.0 * scale[0], 7.0 * scale[0]).astype(jnp.bfloat16)


def clip_values(raw, scale):
    return jnp.clip(raw, -8.0 * scale[1], 7.0 * scale[1]).astype(jnp.bfloat16)


def my_part(x, axis, owner_is, ahead=0):
    owners = len(owner_is)
    size = x.shape[axis] // owners
    pieces = [lax.slice_in_dim(x, p * size, (p + 1) * size, axis=axis) for p in range(owners)]
    out = pieces[0]
    for p in range(1, owners):
        out = jnp.where(owner_is[(p - ahead) % owners], pieces[p], out)
    return out


def chip_top(raw_keys):
    top = jnp.max(jnp.abs(raw_keys), axis=0, keepdims=True)
    return functools.reduce(jnp.maximum, from_owners(top))


def smooth_of(top):
    groups, owners = lax.axis_size("seq"), lax.axis_size("rep")
    if groups != LINE:
        return jnp.sqrt(lax.pmax(top, "seq") + EPSILON)
    partners = list(range(1, groups))
    found = [top]
    for first in range(0, len(partners), owners):
        pairs = [
            (group * owners + owner, partner(group, k, groups) * owners + owner)
            for owner, k in enumerate(partners[first : first + owners])
            for group in range(groups)
        ]
        found.append(lax.ppermute(top, ("seq", "rep"), pairs))
    top = functools.reduce(jnp.maximum, from_owners(functools.reduce(jnp.maximum, found)))
    return jnp.sqrt(top + EPSILON)


def line_pairs(hop, parity, groups):
    pairs = []
    for i in range(parity, groups - 1, 2):
        if i >= hop - 1:
            pairs.append((i, i + 1))
        if i + hop < groups:
            pairs.append((i + 1, i))
    return pairs


def line_project(hidden, key_weight, value_weight, own_query, early):
    groups, owners = lax.axis_size("seq"), lax.axis_size("rep")
    depth = key_weight.shape[0]
    barrier = lax.optimization_barrier

    def send(x, hop, parity):
        return lax.ppermute(x, "seq", line_pairs(hop, parity, groups))

    def absorb(name, blocks, hops, first=0):
        passed = [[shifted(block, "rep", k) for block in blocks] for k in range(1, owners)]
        for k, ready in enumerate([blocks] + passed):
            if k < first:
                continue
            totals[name] = project(
                hidden, totals[name], ready, depth, early[0], hops, k, groups, owners
            )

    totals = {}
    ka1 = send(key_weight, 1, 0)
    kb1 = send(key_weight, 1, 1)
    value_block = pack(value_weight, own_query)
    va1 = send(value_block, 1, 0)
    early, first = barrier((early, (key_weight, value_block)))
    hidden, totals["k"], totals["v"] = load(hidden, *first, early[0], owners)

    ka1, kb1, value_block, totals = barrier((ka1, kb1, value_block, totals))
    kb2 = send(ka1, 2, 1)
    ka2 = send(kb1, 2, 0)
    vb1 = send(value_block, 1, 1)
    for name, weight in (("k", key_weight), ("v", value_weight)):
        absorb(name, [weight], (((0, 0),),), 1)
    absorb("k", [ka1, kb1], (((0, 1),), ((1, 1),)))

    kb2, va1, own_block, totals = barrier((kb2, va1, value_block, totals))
    ends = [(0, groups - 1), (groups - 1, 0)]
    far_query = lax.ppermute(own_block[depth:], "seq", ends)
    ka3 = send(kb2, 3, 0)
    vb2 = send(va1, 2, 1)
    absorb("v", [va1], (((0, 1),),))

    ka2, totals = barrier((ka2, totals))
    absorb("k", [ka2 + kb2], (((0, 2), (1, 2)),))

    vb1, totals = barrier((vb1, totals))
    va2 = send(vb1, 2, 0)
    absorb("v", [vb1], (((1, 1),),))

    ka3, totals = barrier((ka3, totals))
    absorb("k", [ka3], (((0, 3),),))
    raw_keys = totals["k"]
    top = chip_top(raw_keys)
    smooth = smooth_of(top)
    vb2, top = barrier((vb2, top))
    va3 = send(vb2, 3, 0)
    va2, vb2, smooth = barrier((va2, vb2, smooth))
    absorb("v", [va2 + vb2], (((0, 2), (1, 2)),))
    queries = [
        value_block[depth:],
        va1[depth:],
        va2[depth:] + vb2[depth:],
        vb1[depth:] + far_query,
    ]

    def finish_values(scored, *args):
        args, totals["v"] = barrier((args, totals["v"]))
        probs, stats = scored(*args)
        block, stats = barrier((va3, stats))
        absorb("v", [block], (((0, 3),),))
        return probs, stats, totals["v"]

    return raw_keys, smooth, queries, early, finish_values


def on_device(
    hidden, key_weight, value_weight, group_scale, new_kv, decode_query, page_table, lengths
):
    tokens = hidden.shape[0]
    columns = key_weight.shape[1]
    groups, owners = lax.axis_size("seq"), lax.axis_size("rep")
    my_group, my_owner = lax.axis_index("seq"), lax.axis_index("rep")
    assert columns // HD == owners
    pages_dev = tokens // PAGE
    step_count, per_group = decode_query.shape[:2]

    owner_is = [my_owner == owner for owner in range(owners)]
    own_query = my_part(decode_query, 2, owner_is).reshape(step_count * per_group, -1)

    first_pages = [
        (my_group * owners + (my_owner - k) % owners) * pages_dev for k in range(owners)
    ]
    early = (
        jnp.stack([my_group, my_owner]),
        owner_is,
        first_pages,
        partner(my_group, jnp.arange(groups, dtype=jnp.int32), groups),
        own_query,
    )
    if groups == LINE:
        raw_keys, smooth, queries, early, finish_values = line_project(
            hidden, key_weight, value_weight, own_query, early
        )
    else:
        raw_keys, raw_values = (
            jnp.dot(
                hidden,
                lax.all_gather(weight, ("seq", "rep"), axis=0, tiled=True),
                preferred_element_type=jnp.float32,
            )
            for weight in (key_weight, value_weight)
        )
        queries = from_groups(
            jnp.concatenate(jnp.split(own_query, own_query.shape[1] // columns, axis=1))
        )
        smooth = smooth_of(chip_top(raw_keys))
    _, owner_is, first_pages, group_at, own_query = early
    counts = token_counts(page_table, lengths, first_pages, pages_dev)
    counts = counts.reshape(groups, per_group, -1)
    my_kv = my_part(new_kv, 3, owner_is).astype(jnp.float32)
    my_new = (my_kv[:, :, 0], my_kv[:, :, 1], my_part(group_scale, 1, owner_is))

    def by_head(x):
        return [my_part(x, 1, owner_is)] + [
            shifted(my_part(x, 1, owner_is, k), "rep", k) for k in range(1, owners)
        ]

    smoothing = smooth.reshape(-1)
    my_smooth = my_part(smooth, 1, owner_is)
    keys = clip_keys(raw_keys, smooth, group_scale)
    score_scale = HD ** (-0.5)
    scored = functools.partial(score, steps=step_count, scale=score_scale)
    args = (group_at, jnp.stack(queries), my_smooth, counts, by_head(keys))
    if groups == LINE:
        probs, stats, raw_values = finish_values(scored, *args)
    else:
        probs, stats = scored(*args)
    values = clip_values(raw_values, group_scale)
    messages = weigh(probs, by_head(values), stats)

    messages, keys, values, late = lax.optimization_barrier(
        (messages, keys, values, (own_query, my_smooth))
    )
    messages = to_groups(messages)
    is_key = lax.broadcasted_iota(jnp.int32, (1, 2, 1), 1) == 0
    kv_cache = jnp.where(is_key, keys[:, None, :], values[:, None, :])
    kv_cache = with_layout_constraint(kv_cache, Layout((0, 1, 2)))
    own = fresh(late[0], late[1], *my_new, score_scale)
    messages, kv_cache, own = lax.optimization_barrier((messages, kv_cache, own))
    attention = finish(messages, own, step_count * per_group)
    by_owner = from_owners(attention)
    attention = jnp.concatenate(
        [
            functools.reduce(
                lambda out, k: jnp.where(owner_is[(head + k) % owners], by_owner[k], out),
                range(1, owners),
                by_owner[0],
            )
            for head in range(owners)
        ],
        axis=1,
    ).reshape(decode_query.shape)
    return (kv_cache, smoothing, attention)


def solution(mesh):
    placed = (
        P(("seq", "rep"), None),
        P(("seq", "rep"), "head"),
        P(("seq", "rep"), "head"),
        P(None, "head"),
        P(None, "seq", None, "head"),
        P(None, "seq", "head"),
        P(),
        P(),
    )

    return jax.shard_map(
        on_device,
        mesh=mesh,
        in_specs=placed,
        out_specs=(P(("seq", "rep"), None, "head"), P("head"), P(None, "seq", "head")),
        check_vma=False,
    )
```

```python
import functools

import jax
import jax.numpy as jnp
from jax import lax
from jax.experimental import pallas as pl
from jax.experimental.layout import Layout, with_layout_constraint
from jax.experimental.pallas import tpu as pltpu
from jax.sharding import PartitionSpec as P


HD = 128
PAGE = 32


EPSILON = 1e-05
NEGATIVE = -1e30
LINE = 4


def shifted(x, axis, k):
    n = lax.axis_size(axis)
    return lax.ppermute(x, axis, [(i, (i + k) % n) for i in range(n)])


def partner(me, k, n):
    return me ^ k if n == LINE else (k - me) % n


def swapped(x, axis, k):
    n = lax.axis_size(axis)
    return lax.ppermute(x, axis, [(i, partner(i, k, n)) for i in range(n)])


def from_owners(x):
    return [x] + [shifted(x, "rep", k) for k in range(1, lax.axis_size("rep"))]


def from_groups(x):
    n = lax.axis_size("seq")
    if n != LINE:
        return list(lax.all_gather(x, "seq")[partner(lax.axis_index("seq"), jnp.arange(n), n)])
    return [x] + [swapped(x, "seq", k) for k in range(1, n)]


def to_groups(x):
    n = lax.axis_size("seq")
    if n != LINE:
        order = partner(lax.axis_index("seq"), jnp.arange(n), n)
        back = lax.all_to_all(jnp.stack(x)[order], "seq", split_axis=0, concat_axis=0)
        return list(back[order])
    return [x[0]] + [swapped(x[k], "seq", k) for k in range(1, n)]


def pack_kernel(weight, query, out, sem):
    depth, columns = weight.shape
    copy = pltpu.make_async_copy(weight, out.at[pl.ds(0, depth)], sem)
    copy.start()
    lines = query.shape[0]
    for k in range(query.shape[1] // columns):
        at = pl.ds(depth + k * lines, lines)
        out[at, :] = query[:, k * columns : (k + 1) * columns]
    copy.wait()


def pack(weight, query):
    depth, columns = weight.shape
    whole = pl.BlockSpec(memory_space=pltpu.VMEM)
    return pl.pallas_call(
        pack_kernel,
        out_shape=jax.ShapeDtypeStruct((depth + query.size // columns, columns), weight.dtype),
        in_specs=[pl.BlockSpec(memory_space=pl.ANY), whole],
        out_specs=whole,
        scratch_shapes=[pltpu.SemaphoreType.DMA],
        compiler_params=pltpu.CompilerParams(vmem_limit_bytes=8 * 2**20),
        name="pack",
    )(weight, query)


def load_kernel(owners, place, hidden, *refs):
    weights, (held, keys, values, taken, arrived, taken_arrived) = refs[:2], refs[2:]
    depth = taken.shape[1]
    blocks = held.shape[1] // depth
    takes = [
        pltpu.make_async_copy(weight.at[pl.ds(0, depth)], taken.at[j], taken_arrived.at[j])
        for j, weight in enumerate(weights)
    ]

    def block(j):
        index = lax.rem(place[0] * owners + place[1] + j, blocks)
        return pl.ds(pl.multiple_of(index * depth, depth), depth)

    def copy(j):
        return pltpu.make_async_copy(hidden.at[:, block(j)], held.at[:, block(j)], arrived.at[j])

    copy(0).start()
    for take in takes:
        take.start()
    for j in range(1, blocks):
        copy(j).start()
    copy(0).wait()
    for j, out in enumerate((keys, values)):
        takes[j].wait()
        out[...] = jnp.dot(held[:, block(0)], taken[j], preferred_element_type=jnp.float32)
    for j in range(1, blocks):
        copy(j).wait()


def load(hidden, key_weight, value_weight, place, owners):
    tokens, width = hidden.shape
    depth, columns = key_weight.shape
    whole = pl.BlockSpec(memory_space=pltpu.VMEM)
    total = jax.ShapeDtypeStruct((tokens, columns), jnp.float32)
    return pl.pallas_call(
        functools.partial(load_kernel, owners),
        out_shape=(jax.ShapeDtypeStruct(hidden.shape, hidden.dtype), total, total),
        in_specs=[
            pl.BlockSpec(memory_space=pltpu.SMEM),
            pl.BlockSpec(memory_space=pltpu.HBM),
            pl.BlockSpec(memory_space=pl.ANY),
            pl.BlockSpec(memory_space=pl.ANY),
        ],
        out_specs=(whole,) * 3,
        scratch_shapes=[
            pltpu.VMEM((2, depth, columns), key_weight.dtype),
            pltpu.SemaphoreType.DMA((width // depth,)),
            pltpu.SemaphoreType.DMA((2,)),
        ],
        compiler_params=pltpu.CompilerParams(vmem_limit_bytes=30 * 2**20),
        cost_estimate=pl.CostEstimate(
            flops=4 * tokens * depth * columns,
            bytes_accessed=2 * tokens * width,
            transcendentals=0,
        ),
        name="load",
    )(place, hidden, key_weight, value_weight)


def project_kernel(hops, back, groups, owners, place, left, *refs):
    count = len(hops)
    weights, total = refs[:count], refs[count]
    out, held, arrived = refs[-3:]
    depth = held.shape[1]
    copies = [
        pltpu.make_async_copy(weights[j].at[pl.ds(0, depth)], held.at[j], arrived.at[j])
        for j in range(count)
    ]
    for copy in copies:
        copy.start()
    out[...] = total[...]
    owner = lax.rem(place[1] + owners - back, owners)
    for j, copy in enumerate(copies):
        copy.wait()
        group = jnp.int32(-1)
        for parity, hop in hops[j]:
            there = place[0] + jnp.where(lax.rem(place[0], 2) == parity, hop, -hop)
            group = jnp.where((there >= 0) & (there < groups), there, group)

        @pl.when((group >= 0) & (group < groups))
        def _(j=j, group=group):
            block = pl.ds(pl.multiple_of((group * owners + owner) * depth, depth), depth)
            out[...] += jnp.dot(left[:, block], held[j], preferred_element_type=jnp.float32)


def project(hidden, total, weights, depth, place, hops, back, groups, owners):
    tokens = hidden.shape[0]
    columns = weights[0].shape[1]
    count = len(weights)
    whole = pl.BlockSpec(memory_space=pltpu.VMEM)
    return pl.pallas_call(
        functools.partial(project_kernel, hops, back, groups, owners),
        out_shape=jax.ShapeDtypeStruct((tokens, columns), jnp.float32),
        in_specs=[pl.BlockSpec(memory_space=pltpu.SMEM), whole]
        + [pl.BlockSpec(memory_space=pl.ANY)] * count
        + [whole],
        out_specs=whole,
        scratch_shapes=[
            pltpu.VMEM((count, depth, columns), weights[0].dtype),
            pltpu.SemaphoreType.DMA((count,)),
        ],
        compiler_params=pltpu.CompilerParams(vmem_limit_bytes=12 * 2**20),
        cost_estimate=pl.CostEstimate(
            flops=2 * tokens * depth * columns * count,
            bytes_accessed=2 * count * depth * (tokens + columns) + 8 * tokens * columns,
            transcendentals=0,
        ),
        input_output_aliases={2 + count: 0},
        name="project",
    )(place, hidden, *weights, total)


def score_kernel(slots, parts, steps, scale, group, query, smooth, count, *refs):
    keys, probs, stats = refs[:parts], refs[parts], refs[parts + 1 : parts + 1 + slots]
    scores, tops, sums = refs[-3:]
    tokens = keys[0].shape[0]
    width = keys[0].shape[1]
    requests = count.shape[1]
    rows = scores.shape[0]
    heads = query.shape[1] * query.shape[2] // (steps * requests * width)
    per_line = query.shape[2] // width
    raw = [
        query[0][
            (head // per_line) * steps * requests : (head // per_line + 1) * steps * requests,
            (head % per_line) * width : (head % per_line + 1) * width,
        ]
        for head in range(heads)
    ]
    raw = jnp.concatenate(raw, axis=0)
    scaled = (raw.astype(jnp.float32) * smooth[...]).astype(jnp.bfloat16)
    for p in range(parts):
        scores[:, p * tokens : (p + 1) * tokens] = lax.dot_general(
            scaled, keys[p][...], (((1,), (1,)), ((), ())), preferred_element_type=jnp.float32
        )
    again = 2 if (rows // requests) % 2 == 0 else 1
    times = jnp.concatenate([count[0]] * again, axis=0)
    bias = jnp.where(times > 0.0, 0.0, NEGATIVE)
    for start in range(0, rows, again * requests):
        at = pl.ds(start, again * requests)
        raw = scores[at, :] * scale + bias
        top = jnp.max(raw, axis=1, keepdims=True)
        counted = jnp.exp(raw - top) * times
        probs[0, at, :] = counted.astype(jnp.bfloat16)
        tops[at, :] = jnp.broadcast_to(top, (again * requests, 128))
        sums[at, :] = jnp.broadcast_to(
            jnp.sum(counted, axis=1, keepdims=True), (again * requests, 128)
        )
    for slot in range(slots):

        @pl.when(pl.program_id(0) == slot)
        def _(slot=slot):
            stats[slot][0:1, :] = jnp.transpose(tops[...])[0:1, :]
            stats[slot][1:2, :] = jnp.transpose(sums[...])[0:1, :]


def score(groups, query, smooth, count, keys, steps, scale):
    slots, packed, columns = query.shape
    tokens, width = keys[0].shape
    rows = packed * columns // width
    parts = len(keys)
    requests = count.shape[1]
    probs, *stats = pl.pallas_call(
        functools.partial(score_kernel, slots, parts, steps, scale),
        out_shape=[jax.ShapeDtypeStruct((slots, rows, parts * tokens), jnp.bfloat16)]
        + [jax.ShapeDtypeStruct((2, rows), jnp.float32)] * slots,
        grid_spec=pltpu.PrefetchScalarGridSpec(
            num_scalar_prefetch=1,
            grid=(slots,),
            in_specs=[
                pl.BlockSpec((1, packed, columns), lambda k, group: (k, 0, 0)),
                pl.BlockSpec((1, width), lambda k, group: (0, 0)),
                pl.BlockSpec((1, requests, parts * tokens), lambda k, group: (group[k], 0, 0)),
            ]
            + [pl.BlockSpec((tokens, width), lambda k, group: (0, 0))] * parts,
            out_specs=[pl.BlockSpec((1, rows, parts * tokens), lambda k, group: (k, 0, 0))]
            + [pl.BlockSpec((2, rows), lambda k, group: (0, 0))] * slots,
            scratch_shapes=[
                pltpu.VMEM((rows, parts * tokens), jnp.float32),
                pltpu.VMEM((rows, 128), jnp.float32),
                pltpu.VMEM((rows, 128), jnp.float32),
            ],
        ),
        compiler_params=pltpu.CompilerParams(vmem_limit_bytes=16 * 2**20),
        cost_estimate=pl.CostEstimate(
            flops=2 * slots * rows * width * parts * tokens,
            bytes_accessed=2 * slots * rows * parts * tokens,
            transcendentals=slots * rows * parts * tokens,
        ),
        name="score",
    )(groups, query, smooth, count, *keys)
    return probs, stats


def thirds(x):
    out = []
    for _ in range(3):
        out.append(x.astype(jnp.bfloat16))
        x = x - out[-1].astype(jnp.float32)
    return out


def weigh_own_kernel(probs, values, out):
    out[0] = jnp.dot(probs[0], values[...], preferred_element_type=jnp.float32)


def weigh_kernel(slots, parts, own, *refs):
    probs, values = refs[:parts], refs[parts : 2 * parts]
    stats, outs = refs[2 * parts : 2 * parts + slots], refs[2 * parts + slots :]
    rows, width = own.shape[1:]
    summed = own[0]
    for p in range(parts):
        summed += jnp.dot(probs[p][0], values[p][...], preferred_element_type=jnp.float32)
    for slot in range(slots):

        @pl.when(pl.program_id(0) == slot)
        def _(slot=slot):
            outs[slot][0:rows, :] = summed.astype(jnp.bfloat16)
            lines = []
            for third in thirds(stats[slot][...]):
                third = third.astype(jnp.float32)
                lines += [third[:, c : c + width] for c in range(0, rows, width)]
            tail = outs[slot].shape[0] - rows
            lines.append(jnp.zeros((tail - 2 * len(lines), width), jnp.float32))
            outs[slot][rows:, :] = jnp.concatenate(lines, axis=0).astype(jnp.bfloat16)


def packed_rows(rows, width):
    return rows + (6 * (rows // width) // 16 + 1) * 16


def weigh(probs, values, stats):
    slots, rows, _ = probs.shape
    tokens, width = values[0].shape
    parts = len(values) - 1
    total_rows = packed_rows(rows, width)
    flops = 2 * slots * rows * width * tokens

    def probs_spec(p):
        return pl.BlockSpec((1, rows, tokens), lambda k, p=p: (k, 0, p))

    values_spec = pl.BlockSpec((tokens, width), lambda k: (0, 0))
    own_spec = pl.BlockSpec((1, rows, width), lambda k: (k, 0, 0))
    own = pl.pallas_call(
        weigh_own_kernel,
        out_shape=jax.ShapeDtypeStruct((slots, rows, width), jnp.float32),
        grid=(slots,),
        in_specs=[probs_spec(0), values_spec],
        out_specs=own_spec,
        compiler_params=pltpu.CompilerParams(vmem_limit_bytes=16 * 2**20),
        cost_estimate=pl.CostEstimate(
            flops=flops, bytes_accessed=2 * slots * rows * tokens, transcendentals=0
        ),
        name="weigh_own",
    )(probs, values[0])
    return pl.pallas_call(
        functools.partial(weigh_kernel, slots, parts),
        out_shape=[jax.ShapeDtypeStruct((total_rows, width), jnp.bfloat16)] * slots,
        grid=(slots,),
        in_specs=[own_spec]
        + [probs_spec(p + 1) for p in range(parts)]
        + [values_spec] * parts
        + [pl.BlockSpec((2, rows), lambda k: (0, 0))] * slots,
        out_specs=[pl.BlockSpec((total_rows, width), lambda k: (0, 0))] * slots,
        compiler_params=pltpu.CompilerParams(vmem_limit_bytes=16 * 2**20),
        cost_estimate=pl.CostEstimate(
            flops=flops * parts,
            bytes_accessed=2 * slots * rows * tokens * parts,
            transcendentals=0,
        ),
        name="weigh",
    )(own, *([probs] * parts), *values[1:], *stats)


def fresh_kernel(scale, query, smooth, new_keys, new_values, group_scale, summed, highest, total):
    steps, requests, width = new_keys.shape
    lines = steps * requests

    def by_line(x):
        x = x.astype(jnp.bfloat16).astype(jnp.float32)
        return jnp.concatenate([x] * steps, axis=0)

    def clip(x, row):
        limit = group_scale[row : row + 1, :]
        return jnp.clip(x, -8.0 * limit, 7.0 * limit)

    keys = [by_line(clip(new_keys[u] / smooth[...], 0)) for u in range(steps)]
    values = [by_line(clip(new_values[u], 1)) for u in range(steps)]
    line = lax.broadcasted_iota(jnp.int32, (lines, 1), 0)
    seen = [line >= u * requests for u in range(steps)]
    for head in range(query.shape[1] // width):
        at = pl.ds(head * lines, lines)
        mine = query[:, head * width : (head + 1) * width].astype(jnp.float32) * smooth[...]
        mine = mine.astype(jnp.bfloat16).astype(jnp.float32)
        scores = [
            jnp.where(seen[u], jnp.sum(mine * keys[u], axis=1, keepdims=True) * scale, NEGATIVE)
            for u in range(steps)
        ]
        top = functools.reduce(jnp.maximum, scores)
        expd = [jnp.where(seen[u], jnp.exp(scores[u] - top), 0.0) for u in range(steps)]
        highest[at, :] = jnp.broadcast_to(top, (lines, width))
        total[at, :] = jnp.broadcast_to(sum(expd), (lines, width))
        summed[at, :] = sum(
            e.astype(jnp.bfloat16).astype(jnp.float32) * value for e, value in zip(expd, values)
        )


def fresh(query, smooth, new_keys, new_values, group_scale, scale):
    lines, columns = query.shape
    width = smooth.shape[1]
    part = jax.ShapeDtypeStruct((lines * columns // width, width), jnp.float32)
    return pl.pallas_call(
        functools.partial(fresh_kernel, scale),
        out_shape=(part,) * 3,
        compiler_params=pltpu.CompilerParams(vmem_limit_bytes=16 * 2**20),
        name="fresh",
    )(query, smooth, new_keys, new_values, group_scale)


def finish_kernel(slots, *refs):
    messages, (summed, highest, total, out) = refs[:slots], refs[slots:]
    rows, width = summed.shape
    lines = out.shape[0]
    tails = [message[rows:, :].astype(jnp.float32) for message in messages]
    pieces = rows // width

    def column(slot, piece, which):
        row = [tails[slot][2 * (j * pieces + piece) + which :][:1] for j in range(3)]
        return jnp.transpose(jnp.broadcast_to(row[0] + row[1] + row[2], (width, width)))

    for piece in range(pieces):
        at = pl.ds(piece * width, width)
        parts = [
            (messages[k][at, :].astype(jnp.float32), column(k, piece, 0), column(k, piece, 1))
            for k in range(slots)
        ]
        parts.append((summed[at, :], highest[at, :], total[at, :]))
        top = functools.reduce(jnp.maximum, [part[1] for part in parts])
        shares = [jnp.exp(part[1] - top) for part in parts]
        norm = sum(share * part[2] for share, part in zip(shares, parts))
        merged = sum(share * part[0] for share, part in zip(shares, parts)) / norm
        merged = merged.astype(out.dtype)
        for first in range(0, width, lines):
            head = (piece * width + first) // lines
            out[:, head * width : (head + 1) * width] = merged[first : first + lines]


def finish(messages, own, lines):
    rows, width = own[0].shape
    return pl.pallas_call(
        functools.partial(finish_kernel, len(messages)),
        out_shape=jax.ShapeDtypeStruct((lines, rows * width // lines), jnp.bfloat16),
        compiler_params=pltpu.CompilerParams(vmem_limit_bytes=16 * 2**20),
        name="finish",
    )(*messages, *own)


def token_counts(page_table, lengths, first_pages, pages_dev):
    slots = page_table.shape[1]
    slot_ids = jnp.arange(slots, dtype=jnp.int32)
    whole_slots, rest = lengths // PAGE, lengths % PAGE
    pages = jnp.concatenate(
        [first + jnp.arange(pages_dev, dtype=jnp.int32) for first in first_pages]
    )
    same = page_table[:, :, None] == pages[None, None, :]
    whole = jnp.sum(same & (slot_ids[None, :] < whole_slots[:, None])[:, :, None], axis=1)
    last = jnp.sum(same & (slot_ids[None, :] == whole_slots[:, None])[:, :, None], axis=1)
    token = jnp.arange(pages.shape[0] * PAGE, dtype=jnp.int32)
    spread = token[None, :] // PAGE == jnp.arange(pages.shape[0], dtype=jnp.int32)[:, None]
    spread = spread.astype(jnp.bfloat16)
    whole = jnp.dot(whole.astype(jnp.bfloat16), spread, preferred_element_type=jnp.float32)
    last = jnp.dot(last.astype(jnp.bfloat16), spread, preferred_element_type=jnp.float32)
    return whole + jnp.where((token % PAGE)[None, :] < rest[:, None], last, 0.0)


def clip_keys(raw, smooth, scale):
    return jnp.clip(raw / smooth, -8.0 * scale[0], 7.0 * scale[0]).astype(jnp.bfloat16)


def clip_values(raw, scale):
    return jnp.clip(raw, -8.0 * scale[1], 7.0 * scale[1]).astype(jnp.bfloat16)


def my_part(x, axis, owner_is, ahead=0):
    owners = len(owner_is)
    size = x.shape[axis] // owners
    pieces = [lax.slice_in_dim(x, p * size, (p + 1) * size, axis=axis) for p in range(owners)]
    out = pieces[0]
    for p in range(1, owners):
        out = jnp.where(owner_is[(p - ahead) % owners], pieces[p], out)
    return out


def chip_top(raw_keys):
    top = jnp.max(jnp.abs(raw_keys), axis=0, keepdims=True)
    return functools.reduce(jnp.maximum, from_owners(top))


def smooth_of(top):
    top = functools.reduce(jnp.maximum, from_groups(top))
    return jnp.sqrt(top + EPSILON)


def line_pairs(hop, parity, groups):
    pairs = []
    for i in range(parity, groups - 1, 2):
        if i >= hop - 1:
            pairs.append((i, i + 1))
        if i + hop < groups:
            pairs.append((i + 1, i))
    return pairs


def line_project(hidden, key_weight, value_weight, own_query, early):
    groups, owners = lax.axis_size("seq"), lax.axis_size("rep")
    depth = key_weight.shape[0]
    barrier = lax.optimization_barrier

    def send(x, hop, parity):
        return lax.ppermute(x, "seq", line_pairs(hop, parity, groups))

    def absorb(name, blocks, hops, first=0):
        passed = [[shifted(block, "rep", k) for block in blocks] for k in range(1, owners)]
        for k, ready in enumerate([blocks] + passed):
            if k < first:
                continue
            totals[name] = project(
                hidden, totals[name], ready, depth, early[0], hops, k, groups, owners
            )

    totals = {}
    ka1 = send(key_weight, 1, 0)
    kb1 = send(key_weight, 1, 1)
    value_block = pack(value_weight, own_query)
    va1 = send(value_block, 1, 0)
    early, first = barrier((early, (key_weight, value_block)))
    hidden, totals["k"], totals["v"] = load(hidden, *first, early[0], owners)

    ka1, kb1, value_block, totals = barrier((ka1, kb1, value_block, totals))
    kb2 = send(ka1, 2, 1)
    ka2 = send(kb1, 2, 0)
    vb1 = send(value_block, 1, 1)
    for name, weight in (("k", key_weight), ("v", value_weight)):
        absorb(name, [weight], (((0, 0),),), 1)
    absorb("k", [ka1, kb1], (((0, 1),), ((1, 1),)))

    kb2, va1, own_block, totals = barrier((kb2, va1, value_block, totals))
    ends = [(0, groups - 1), (groups - 1, 0)]
    far_query = lax.ppermute(own_block[depth:], "seq", ends)
    ka3 = send(kb2, 3, 0)
    vb2 = send(va1, 2, 1)
    absorb("v", [va1], (((0, 1),),))

    ka2, totals = barrier((ka2, totals))
    absorb("k", [ka2 + kb2], (((0, 2), (1, 2)),))

    va2 = send(vb1, 2, 0)

    ka3, totals = barrier((ka3, totals))
    absorb("k", [ka3], (((0, 3),),))
    raw_keys = totals["k"]
    top = chip_top(raw_keys)
    smooth = smooth_of(top)
    vb1, vb2, top = barrier((vb1, vb2, top))
    va3 = send(vb2, 3, 0)
    absorb("v", [vb1], (((1, 1),),))
    va2, vb2, smooth = barrier((va2, vb2, smooth))
    absorb("v", [va2 + vb2], (((0, 2), (1, 2)),))
    queries = [
        value_block[depth:],
        va1[depth:],
        va2[depth:] + vb2[depth:],
        vb1[depth:] + far_query,
    ]

    def finish_values(scored, *args):
        args, totals["v"] = barrier((args, totals["v"]))
        probs, stats = scored(*args)
        block, stats = barrier((va3, stats))
        absorb("v", [block], (((0, 3),),))
        return probs, stats, totals["v"]

    return raw_keys, smooth, queries, early, finish_values


def on_device(
    hidden, key_weight, value_weight, group_scale, new_kv, decode_query, page_table, lengths
):
    tokens = hidden.shape[0]
    columns = key_weight.shape[1]
    groups, owners = lax.axis_size("seq"), lax.axis_size("rep")
    my_group, my_owner = lax.axis_index("seq"), lax.axis_index("rep")
    assert columns // HD == owners
    pages_dev = tokens // PAGE
    step_count, per_group = decode_query.shape[:2]

    owner_is = [my_owner == owner for owner in range(owners)]
    own_query = my_part(decode_query, 2, owner_is).reshape(step_count * per_group, -1)

    first_pages = [
        (my_group * owners + (my_owner - k) % owners) * pages_dev for k in range(owners)
    ]
    early = (
        jnp.stack([my_group, my_owner]),
        owner_is,
        first_pages,
        partner(my_group, jnp.arange(groups, dtype=jnp.int32), groups),
        own_query,
    )
    if groups == LINE:
        raw_keys, smooth, queries, early, finish_values = line_project(
            hidden, key_weight, value_weight, own_query, early
        )
    else:
        raw_keys, raw_values = (
            jnp.dot(
                hidden,
                lax.all_gather(weight, ("seq", "rep"), axis=0, tiled=True),
                preferred_element_type=jnp.float32,
            )
            for weight in (key_weight, value_weight)
        )
        queries = from_groups(
            jnp.concatenate(jnp.split(own_query, own_query.shape[1] // columns, axis=1))
        )
        smooth = smooth_of(chip_top(raw_keys))
    _, owner_is, first_pages, group_at, own_query = early
    counts = token_counts(page_table, lengths, first_pages, pages_dev)
    counts = counts.reshape(groups, per_group, -1)
    my_kv = my_part(new_kv, 3, owner_is).astype(jnp.float32)
    my_new = (my_kv[:, :, 0], my_kv[:, :, 1], my_part(group_scale, 1, owner_is))

    def by_head(x):
        return [my_part(x, 1, owner_is)] + [
            shifted(my_part(x, 1, owner_is, k), "rep", k) for k in range(1, owners)
        ]

    smoothing = smooth.reshape(-1)
    my_smooth = my_part(smooth, 1, owner_is)
    keys = clip_keys(raw_keys, smooth, group_scale)
    score_scale = HD ** (-0.5)
    scored = functools.partial(score, steps=step_count, scale=score_scale)
    args = (group_at, jnp.stack(queries), my_smooth, counts, by_head(keys))
    if groups == LINE:
        probs, stats, raw_values = finish_values(scored, *args)
    else:
        probs, stats = scored(*args)
    values = clip_values(raw_values, group_scale)
    messages = weigh(probs, by_head(values), stats)

    messages, keys, values, late = lax.optimization_barrier(
        (messages, keys, values, (own_query, my_smooth))
    )
    messages = to_groups(messages)
    is_key = lax.broadcasted_iota(jnp.int32, (1, 2, 1), 1) == 0
    kv_cache = jnp.where(is_key, keys[:, None, :], values[:, None, :])
    kv_cache = with_layout_constraint(kv_cache, Layout((0, 1, 2)))
    own = fresh(late[0], late[1], *my_new, score_scale)
    messages, kv_cache, own = lax.optimization_barrier((messages, kv_cache, own))
    attention = finish(messages, own, step_count * per_group)
    by_owner = from_owners(attention)
    attention = jnp.concatenate(
        [
            functools.reduce(
                lambda out, k: jnp.where(owner_is[(head + k) % owners], by_owner[k], out),
                range(1, owners),
                by_owner[0],
            )
            for head in range(owners)
        ],
        axis=1,
    ).reshape(decode_query.shape)
    return (kv_cache, smoothing, attention)


def solution(mesh):
    placed = (
        P(("seq", "rep"), None),
        P(("seq", "rep"), "head"),
        P(("seq", "rep"), "head"),
        P(None, "head"),
        P(None, "seq", None, "head"),
        P(None, "seq", "head"),
        P(),
        P(),
    )

    return jax.shard_map(
        on_device,
        mesh=mesh,
        in_specs=placed,
        out_specs=(P(("seq", "rep"), None, "head"), P("head"), P(None, "seq", "head")),
        check_vma=False,
    )
```

```python
import functools

import jax
import jax.numpy as jnp
from jax import lax
from jax.experimental import pallas as pl
from jax.experimental.layout import Layout, with_layout_constraint
from jax.experimental.pallas import tpu as pltpu
from jax.sharding import PartitionSpec as P


HD = 128
PAGE = 32


EPSILON = 1e-05
NEGATIVE = -1e30
LINE = 4


def shifted(x, axis, k):
    n = lax.axis_size(axis)
    return lax.ppermute(x, axis, [(i, (i + k) % n) for i in range(n)])


def partner(me, k, n):
    return me ^ k if n == LINE else (k - me) % n


def swapped(x, axis, k):
    n = lax.axis_size(axis)
    return lax.ppermute(x, axis, [(i, partner(i, k, n)) for i in range(n)])


def from_owners(x):
    return [x] + [shifted(x, "rep", k) for k in range(1, lax.axis_size("rep"))]


def from_groups(x):
    n = lax.axis_size("seq")
    if n != LINE:
        return list(lax.all_gather(x, "seq")[partner(lax.axis_index("seq"), jnp.arange(n), n)])
    return [x] + [swapped(x, "seq", k) for k in range(1, n)]


def to_groups(x):
    n = lax.axis_size("seq")
    if n != LINE:
        order = partner(lax.axis_index("seq"), jnp.arange(n), n)
        back = lax.all_to_all(jnp.stack(x)[order], "seq", split_axis=0, concat_axis=0)
        return list(back[order])
    out = [x[0]]
    for k in range(1, n):
        out.append(swapped(x[k], "seq", k))
    return out


def pack_kernel(weight, query, out, sem):
    depth, columns = weight.shape
    copy = pltpu.make_async_copy(weight, out.at[pl.ds(0, depth)], sem)
    copy.start()
    lines = query.shape[0]
    for k in range(query.shape[1] // columns):
        at = pl.ds(depth + k * lines, lines)
        out[at, :] = query[:, k * columns : (k + 1) * columns]
    copy.wait()


def pack(weight, query):
    depth, columns = weight.shape
    whole = pl.BlockSpec(memory_space=pltpu.VMEM)
    return pl.pallas_call(
        pack_kernel,
        out_shape=jax.ShapeDtypeStruct((depth + query.size // columns, columns), weight.dtype),
        in_specs=[pl.BlockSpec(memory_space=pl.ANY), whole],
        out_specs=whole,
        scratch_shapes=[pltpu.SemaphoreType.DMA],
        compiler_params=pltpu.CompilerParams(vmem_limit_bytes=8 * 2**20),
        name="pack",
    )(weight, query)


def load_kernel(owners, place, hidden, *refs):
    weights, (held, keys, values, taken, arrived, taken_arrived) = refs[:2], refs[2:]
    depth = taken.shape[1]
    blocks = held.shape[1] // depth
    takes = [
        pltpu.make_async_copy(weight.at[pl.ds(0, depth)], taken.at[j], taken_arrived.at[j])
        for j, weight in enumerate(weights)
    ]

    def block(j):
        index = lax.rem(place[0] * owners + place[1] + j, blocks)
        return pl.ds(pl.multiple_of(index * depth, depth), depth)

    def copy(j):
        return pltpu.make_async_copy(hidden.at[:, block(j)], held.at[:, block(j)], arrived.at[j])

    copy(0).start()
    for take in takes:
        take.start()
    for j in range(1, blocks):
        copy(j).start()
    copy(0).wait()
    for j, out in enumerate((keys, values)):
        takes[j].wait()
        out[...] = jnp.dot(held[:, block(0)], taken[j], preferred_element_type=jnp.float32)
    for j in range(1, blocks):
        copy(j).wait()


def load(hidden, key_weight, value_weight, place, owners):
    tokens, width = hidden.shape
    depth, columns = key_weight.shape
    whole = pl.BlockSpec(memory_space=pltpu.VMEM)
    total = jax.ShapeDtypeStruct((tokens, columns), jnp.float32)
    return pl.pallas_call(
        functools.partial(load_kernel, owners),
        out_shape=(jax.ShapeDtypeStruct(hidden.shape, hidden.dtype), total, total),
        in_specs=[
            pl.BlockSpec(memory_space=pltpu.SMEM),
            pl.BlockSpec(memory_space=pltpu.HBM),
            pl.BlockSpec(memory_space=pl.ANY),
            pl.BlockSpec(memory_space=pl.ANY),
        ],
        out_specs=(whole,) * 3,
        scratch_shapes=[
            pltpu.VMEM((2, depth, columns), key_weight.dtype),
            pltpu.SemaphoreType.DMA((width // depth,)),
            pltpu.SemaphoreType.DMA((2,)),
        ],
        compiler_params=pltpu.CompilerParams(vmem_limit_bytes=30 * 2**20),
        cost_estimate=pl.CostEstimate(
            flops=4 * tokens * depth * columns,
            bytes_accessed=2 * tokens * width,
            transcendentals=0,
        ),
        name="load",
    )(place, hidden, key_weight, value_weight)


def project_kernel(hops, back, groups, owners, place, left, *refs):
    count = len(hops)
    weights, total = refs[:count], refs[count]
    out, held, arrived = refs[-3:]
    depth = held.shape[1]
    copies = [
        pltpu.make_async_copy(weights[j].at[pl.ds(0, depth)], held.at[j], arrived.at[j])
        for j in range(count)
    ]
    for copy in copies:
        copy.start()
    out[...] = total[...]
    owner = lax.rem(place[1] + owners - back, owners)
    for j, copy in enumerate(copies):
        copy.wait()
        group = jnp.int32(-1)
        for parity, hop in hops[j]:
            there = place[0] + jnp.where(lax.rem(place[0], 2) == parity, hop, -hop)
            group = jnp.where((there >= 0) & (there < groups), there, group)

        @pl.when((group >= 0) & (group < groups))
        def _(j=j, group=group):
            block = pl.ds(pl.multiple_of((group * owners + owner) * depth, depth), depth)
            out[...] += jnp.dot(left[:, block], held[j], preferred_element_type=jnp.float32)


def project(hidden, total, weights, depth, place, hops, back, groups, owners):
    tokens = hidden.shape[0]
    columns = weights[0].shape[1]
    count = len(weights)
    whole = pl.BlockSpec(memory_space=pltpu.VMEM)
    return pl.pallas_call(
        functools.partial(project_kernel, hops, back, groups, owners),
        out_shape=jax.ShapeDtypeStruct((tokens, columns), jnp.float32),
        in_specs=[pl.BlockSpec(memory_space=pltpu.SMEM), whole]
        + [pl.BlockSpec(memory_space=pl.ANY)] * count
        + [whole],
        out_specs=whole,
        scratch_shapes=[
            pltpu.VMEM((count, depth, columns), weights[0].dtype),
            pltpu.SemaphoreType.DMA((count,)),
        ],
        compiler_params=pltpu.CompilerParams(vmem_limit_bytes=12 * 2**20),
        cost_estimate=pl.CostEstimate(
            flops=2 * tokens * depth * columns * count,
            bytes_accessed=2 * count * depth * (tokens + columns) + 8 * tokens * columns,
            transcendentals=0,
        ),
        input_output_aliases={2 + count: 0},
        name="project",
    )(place, hidden, *weights, total)


def score_kernel(slots, parts, steps, scale, group, query, smooth, count, *refs):
    keys, probs, stats = refs[:parts], refs[parts], refs[parts + 1 : parts + 1 + slots]
    scores, tops, sums = refs[-3:]
    tokens = keys[0].shape[0]
    width = keys[0].shape[1]
    requests = count.shape[1]
    rows = scores.shape[0]
    heads = query.shape[1] * query.shape[2] // (steps * requests * width)
    per_line = query.shape[2] // width
    raw = [
        query[0][
            (head // per_line) * steps * requests : (head // per_line + 1) * steps * requests,
            (head % per_line) * width : (head % per_line + 1) * width,
        ]
        for head in range(heads)
    ]
    raw = jnp.concatenate(raw, axis=0)
    scaled = (raw.astype(jnp.float32) * smooth[...]).astype(jnp.bfloat16)
    for p in range(parts):
        scores[:, p * tokens : (p + 1) * tokens] = lax.dot_general(
            scaled, keys[p][...], (((1,), (1,)), ((), ())), preferred_element_type=jnp.float32
        )
    again = 2 if (rows // requests) % 2 == 0 else 1
    times = jnp.concatenate([count[0]] * again, axis=0)
    bias = jnp.where(times > 0.0, 0.0, NEGATIVE)
    for start in range(0, rows, again * requests):
        at = pl.ds(start, again * requests)
        raw = scores[at, :] * scale + bias
        top = jnp.max(raw, axis=1, keepdims=True)
        counted = jnp.exp(raw - top) * times
        probs[0, at, :] = counted.astype(jnp.bfloat16)
        tops[at, :] = jnp.broadcast_to(top, (again * requests, 128))
        sums[at, :] = jnp.broadcast_to(
            jnp.sum(counted, axis=1, keepdims=True), (again * requests, 128)
        )
    for slot in range(slots):

        @pl.when(pl.program_id(0) == slot)
        def _(slot=slot):
            stats[slot][0:1, :] = jnp.transpose(tops[...])[0:1, :]
            stats[slot][1:2, :] = jnp.transpose(sums[...])[0:1, :]


def score(groups, query, smooth, count, keys, steps, scale):
    slots, packed, columns = query.shape
    tokens, width = keys[0].shape
    rows = packed * columns // width
    parts = len(keys)
    requests = count.shape[1]
    probs, *stats = pl.pallas_call(
        functools.partial(score_kernel, slots, parts, steps, scale),
        out_shape=[jax.ShapeDtypeStruct((slots, rows, parts * tokens), jnp.bfloat16)]
        + [jax.ShapeDtypeStruct((2, rows), jnp.float32)] * slots,
        grid_spec=pltpu.PrefetchScalarGridSpec(
            num_scalar_prefetch=1,
            grid=(slots,),
            in_specs=[
                pl.BlockSpec((1, packed, columns), lambda k, group: (k, 0, 0)),
                pl.BlockSpec((1, width), lambda k, group: (0, 0)),
                pl.BlockSpec((1, requests, parts * tokens), lambda k, group: (group[k], 0, 0)),
            ]
            + [pl.BlockSpec((tokens, width), lambda k, group: (0, 0))] * parts,
            out_specs=[pl.BlockSpec((1, rows, parts * tokens), lambda k, group: (k, 0, 0))]
            + [pl.BlockSpec((2, rows), lambda k, group: (0, 0))] * slots,
            scratch_shapes=[
                pltpu.VMEM((rows, parts * tokens), jnp.float32),
                pltpu.VMEM((rows, 128), jnp.float32),
                pltpu.VMEM((rows, 128), jnp.float32),
            ],
        ),
        compiler_params=pltpu.CompilerParams(vmem_limit_bytes=16 * 2**20),
        cost_estimate=pl.CostEstimate(
            flops=2 * slots * rows * width * parts * tokens,
            bytes_accessed=2 * slots * rows * parts * tokens,
            transcendentals=slots * rows * parts * tokens,
        ),
        name="score",
    )(groups, query, smooth, count, *keys)
    return probs, stats


def thirds(x):
    out = []
    for _ in range(3):
        out.append(x.astype(jnp.bfloat16))
        x = x - out[-1].astype(jnp.float32)
    return out


def weigh_own_kernel(probs, values, out):
    out[0] = jnp.dot(probs[0], values[...], preferred_element_type=jnp.float32)


def weigh_kernel(slots, parts, own, *refs):
    probs, values = refs[:parts], refs[parts : 2 * parts]
    stats, outs = refs[2 * parts : 2 * parts + slots], refs[2 * parts + slots :]
    rows, width = own.shape[1:]
    summed = own[0]
    for p in range(parts):
        summed += jnp.dot(probs[p][0], values[p][...], preferred_element_type=jnp.float32)
    for slot in range(slots):

        @pl.when(pl.program_id(0) == slot)
        def _(slot=slot):
            outs[slot][0:rows, :] = summed.astype(jnp.bfloat16)
            lines = []
            for third in thirds(stats[slot][...]):
                third = third.astype(jnp.float32)
                lines += [third[:, c : c + width] for c in range(0, rows, width)]
            tail = outs[slot].shape[0] - rows
            lines.append(jnp.zeros((tail - 2 * len(lines), width), jnp.float32))
            outs[slot][rows:, :] = jnp.concatenate(lines, axis=0).astype(jnp.bfloat16)


def packed_rows(rows, width):
    return rows + (6 * (rows // width) // 16 + 1) * 16


def weigh(probs, values, stats):
    slots, rows, _ = probs.shape
    tokens, width = values[0].shape
    parts = len(values) - 1
    total_rows = packed_rows(rows, width)
    flops = 2 * slots * rows * width * tokens

    def probs_spec(p):
        return pl.BlockSpec((1, rows, tokens), lambda k, p=p: (k, 0, p))

    values_spec = pl.BlockSpec((tokens, width), lambda k: (0, 0))
    own_spec = pl.BlockSpec((1, rows, width), lambda k: (k, 0, 0))
    own = pl.pallas_call(
        weigh_own_kernel,
        out_shape=jax.ShapeDtypeStruct((slots, rows, width), jnp.float32),
        grid=(slots,),
        in_specs=[probs_spec(0), values_spec],
        out_specs=own_spec,
        compiler_params=pltpu.CompilerParams(vmem_limit_bytes=16 * 2**20),
        cost_estimate=pl.CostEstimate(
            flops=flops, bytes_accessed=2 * slots * rows * tokens, transcendentals=0
        ),
        name="weigh_own",
    )(probs, values[0])
    return pl.pallas_call(
        functools.partial(weigh_kernel, slots, parts),
        out_shape=[jax.ShapeDtypeStruct((total_rows, width), jnp.bfloat16)] * slots,
        grid=(slots,),
        in_specs=[own_spec]
        + [probs_spec(p + 1) for p in range(parts)]
        + [values_spec] * parts
        + [pl.BlockSpec((2, rows), lambda k: (0, 0))] * slots,
        out_specs=[pl.BlockSpec((total_rows, width), lambda k: (0, 0))] * slots,
        compiler_params=pltpu.CompilerParams(vmem_limit_bytes=16 * 2**20),
        cost_estimate=pl.CostEstimate(
            flops=flops * parts,
            bytes_accessed=2 * slots * rows * tokens * parts,
            transcendentals=0,
        ),
        name="weigh",
    )(own, *([probs] * parts), *values[1:], *stats)


def fresh_kernel(scale, query, smooth, new_keys, new_values, group_scale, summed, highest, total):
    steps, requests, width = new_keys.shape
    lines = steps * requests

    def by_line(x):
        x = x.astype(jnp.bfloat16).astype(jnp.float32)
        return jnp.concatenate([x] * steps, axis=0)

    def clip(x, row):
        limit = group_scale[row : row + 1, :]
        return jnp.clip(x, -8.0 * limit, 7.0 * limit)

    keys = [by_line(clip(new_keys[u] / smooth[...], 0)) for u in range(steps)]
    values = [by_line(clip(new_values[u], 1)) for u in range(steps)]
    line = lax.broadcasted_iota(jnp.int32, (lines, 1), 0)
    seen = [line >= u * requests for u in range(steps)]
    for head in range(query.shape[1] // width):
        at = pl.ds(head * lines, lines)
        mine = query[:, head * width : (head + 1) * width].astype(jnp.float32) * smooth[...]
        mine = mine.astype(jnp.bfloat16).astype(jnp.float32)
        scores = [
            jnp.where(seen[u], jnp.sum(mine * keys[u], axis=1, keepdims=True) * scale, NEGATIVE)
            for u in range(steps)
        ]
        top = functools.reduce(jnp.maximum, scores)
        expd = [jnp.where(seen[u], jnp.exp(scores[u] - top), 0.0) for u in range(steps)]
        highest[at, :] = jnp.broadcast_to(top, (lines, width))
        total[at, :] = jnp.broadcast_to(sum(expd), (lines, width))
        summed[at, :] = sum(
            e.astype(jnp.bfloat16).astype(jnp.float32) * value for e, value in zip(expd, values)
        )


def fresh(query, smooth, new_keys, new_values, group_scale, scale):
    lines, columns = query.shape
    width = smooth.shape[1]
    part = jax.ShapeDtypeStruct((lines * columns // width, width), jnp.float32)
    return pl.pallas_call(
        functools.partial(fresh_kernel, scale),
        out_shape=(part,) * 3,
        compiler_params=pltpu.CompilerParams(vmem_limit_bytes=16 * 2**20),
        name="fresh",
    )(query, smooth, new_keys, new_values, group_scale)


def finish_kernel(slots, *refs):
    messages, (summed, highest, total, out) = refs[:slots], refs[slots:]
    rows, width = summed.shape
    lines = out.shape[0]
    tails = [message[rows:, :].astype(jnp.float32) for message in messages]
    pieces = rows // width

    def column(slot, piece, which):
        row = [tails[slot][2 * (j * pieces + piece) + which :][:1] for j in range(3)]
        return jnp.transpose(jnp.broadcast_to(row[0] + row[1] + row[2], (width, width)))

    for piece in range(pieces):
        at = pl.ds(piece * width, width)
        parts = [
            (messages[k][at, :].astype(jnp.float32), column(k, piece, 0), column(k, piece, 1))
            for k in range(slots)
        ]
        parts.append((summed[at, :], highest[at, :], total[at, :]))
        top = functools.reduce(jnp.maximum, [part[1] for part in parts])
        shares = [jnp.exp(part[1] - top) for part in parts]
        norm = sum(share * part[2] for share, part in zip(shares, parts))
        merged = sum(share * part[0] for share, part in zip(shares, parts)) / norm
        merged = merged.astype(out.dtype)
        for first in range(0, width, lines):
            head = (piece * width + first) // lines
            out[:, head * width : (head + 1) * width] = merged[first : first + lines]


def finish(messages, own, lines):
    rows, width = own[0].shape
    return pl.pallas_call(
        functools.partial(finish_kernel, len(messages)),
        out_shape=jax.ShapeDtypeStruct((lines, rows * width // lines), jnp.bfloat16),
        compiler_params=pltpu.CompilerParams(vmem_limit_bytes=16 * 2**20),
        name="finish",
    )(*messages, *own)


def token_counts(page_table, lengths, first_pages, pages_dev):
    slots = page_table.shape[1]
    slot_ids = jnp.arange(slots, dtype=jnp.int32)
    whole_slots, rest = lengths // PAGE, lengths % PAGE
    pages = jnp.concatenate(
        [first + jnp.arange(pages_dev, dtype=jnp.int32) for first in first_pages]
    )
    same = page_table[:, :, None] == pages[None, None, :]
    whole = jnp.sum(same & (slot_ids[None, :] < whole_slots[:, None])[:, :, None], axis=1)
    last = jnp.sum(same & (slot_ids[None, :] == whole_slots[:, None])[:, :, None], axis=1)
    token = jnp.arange(pages.shape[0] * PAGE, dtype=jnp.int32)
    spread = token[None, :] // PAGE == jnp.arange(pages.shape[0], dtype=jnp.int32)[:, None]
    spread = spread.astype(jnp.bfloat16)
    whole = jnp.dot(whole.astype(jnp.bfloat16), spread, preferred_element_type=jnp.float32)
    last = jnp.dot(last.astype(jnp.bfloat16), spread, preferred_element_type=jnp.float32)
    return whole + jnp.where((token % PAGE)[None, :] < rest[:, None], last, 0.0)


def clip_keys(raw, smooth, scale):
    return jnp.clip(raw / smooth, -8.0 * scale[0], 7.0 * scale[0]).astype(jnp.bfloat16)


def clip_values(raw, scale):
    return jnp.clip(raw, -8.0 * scale[1], 7.0 * scale[1]).astype(jnp.bfloat16)


def my_part(x, axis, owner_is, ahead=0):
    owners = len(owner_is)
    size = x.shape[axis] // owners
    pieces = [lax.slice_in_dim(x, p * size, (p + 1) * size, axis=axis) for p in range(owners)]
    out = pieces[0]
    for p in range(1, owners):
        out = jnp.where(owner_is[(p - ahead) % owners], pieces[p], out)
    return out


def chip_top(raw_keys):
    top = jnp.max(jnp.abs(raw_keys), axis=0, keepdims=True)
    return functools.reduce(jnp.maximum, from_owners(top))


def smooth_of(top):
    top = functools.reduce(jnp.maximum, from_groups(top))
    return jnp.sqrt(top + EPSILON)


def line_pairs(hop, parity, groups):
    pairs = []
    for i in range(parity, groups - 1, 2):
        if i >= hop - 1:
            pairs.append((i, i + 1))
        if i + hop < groups:
            pairs.append((i + 1, i))
    return pairs


def line_project(hidden, key_weight, value_weight, own_query, early):
    groups, owners = lax.axis_size("seq"), lax.axis_size("rep")
    depth = key_weight.shape[0]
    barrier = lax.optimization_barrier

    def send(x, hop, parity):
        return lax.ppermute(x, "seq", line_pairs(hop, parity, groups))

    def absorb(name, blocks, hops, first=0):
        passed = [[shifted(block, "rep", k) for block in blocks] for k in range(1, owners)]
        for k, ready in enumerate([blocks] + passed):
            if k < first:
                continue
            totals[name] = project(
                hidden, totals[name], ready, depth, early[0], hops, k, groups, owners
            )

    totals = {}
    ka1 = send(key_weight, 1, 0)
    kb1 = send(key_weight, 1, 1)
    value_block = pack(value_weight, own_query)
    va1 = send(value_block, 1, 0)
    early, first = barrier((early, (key_weight, value_block)))
    hidden, totals["k"], totals["v"] = load(hidden, *first, early[0], owners)

    ka1, kb1, value_block, totals = barrier((ka1, kb1, value_block, totals))
    kb2 = send(ka1, 2, 1)
    ka2 = send(kb1, 2, 0)
    vb1 = send(value_block, 1, 1)
    for name, weight in (("k", key_weight), ("v", value_weight)):
        absorb(name, [weight], (((0, 0),),), 1)
    absorb("k", [ka1, kb1], (((0, 1),), ((1, 1),)))

    kb2, va1, own_block, totals = barrier((kb2, va1, value_block, totals))
    ends = [(0, groups - 1), (groups - 1, 0)]
    far_query = lax.ppermute(own_block[depth:], "seq", ends)
    ka3 = send(kb2, 3, 0)
    vb2 = send(va1, 2, 1)
    absorb("v", [va1], (((0, 1),),))

    ka2, totals = barrier((ka2, totals))
    absorb("k", [ka2 + kb2], (((0, 2), (1, 2)),))

    va2 = send(vb1, 2, 0)

    ka3, totals = barrier((ka3, totals))
    absorb("k", [ka3], (((0, 3),),))
    raw_keys = totals["k"]
    top = chip_top(raw_keys)
    smooth = smooth_of(top)
    vb1, vb2, top = barrier((vb1, vb2, top))
    va3 = send(vb2, 3, 0)
    absorb("v", [vb1], (((1, 1),),))
    va2, vb2, smooth = barrier((va2, vb2, smooth))
    absorb("v", [va2 + vb2], (((0, 2), (1, 2)),))
    queries = [
        value_block[depth:],
        va1[depth:],
        va2[depth:] + vb2[depth:],
        vb1[depth:] + far_query,
    ]

    def finish_values(scored, *args):
        args, totals["v"] = barrier((args, totals["v"]))
        probs, stats = scored(*args)
        block, stats = barrier((va3, stats))
        absorb("v", [block], (((0, 3),),))
        return probs, stats, totals["v"]

    return raw_keys, smooth, queries, early, finish_values


def on_device(
    hidden, key_weight, value_weight, group_scale, new_kv, decode_query, page_table, lengths
):
    tokens = hidden.shape[0]
    columns = key_weight.shape[1]
    groups, owners = lax.axis_size("seq"), lax.axis_size("rep")
    my_group, my_owner = lax.axis_index("seq"), lax.axis_index("rep")
    assert columns // HD == owners
    pages_dev = tokens // PAGE
    step_count, per_group = decode_query.shape[:2]

    owner_is = [my_owner == owner for owner in range(owners)]
    own_query = my_part(decode_query, 2, owner_is).reshape(step_count * per_group, -1)

    first_pages = [
        (my_group * owners + (my_owner - k) % owners) * pages_dev for k in range(owners)
    ]
    early = (
        jnp.stack([my_group, my_owner]),
        owner_is,
        first_pages,
        partner(my_group, jnp.arange(groups, dtype=jnp.int32), groups),
        own_query,
    )
    if groups == LINE:
        raw_keys, smooth, queries, early, finish_values = line_project(
            hidden, key_weight, value_weight, own_query, early
        )
    else:
        raw_keys, raw_values = (
            jnp.dot(
                hidden,
                lax.all_gather(weight, ("seq", "rep"), axis=0, tiled=True),
                preferred_element_type=jnp.float32,
            )
            for weight in (key_weight, value_weight)
        )
        queries = from_groups(
            jnp.concatenate(jnp.split(own_query, own_query.shape[1] // columns, axis=1))
        )
        smooth = smooth_of(chip_top(raw_keys))
    _, owner_is, first_pages, group_at, own_query = early
    counts = token_counts(page_table, lengths, first_pages, pages_dev)
    counts = counts.reshape(groups, per_group, -1)
    my_kv = my_part(new_kv, 3, owner_is).astype(jnp.float32)
    my_new = (my_kv[:, :, 0], my_kv[:, :, 1], my_part(group_scale, 1, owner_is))

    def by_head(x):
        return [my_part(x, 1, owner_is)] + [
            shifted(my_part(x, 1, owner_is, k), "rep", k) for k in range(1, owners)
        ]

    smoothing = smooth.reshape(-1)
    my_smooth = my_part(smooth, 1, owner_is)
    keys = clip_keys(raw_keys, smooth, group_scale)
    score_scale = HD ** (-0.5)
    scored = functools.partial(score, steps=step_count, scale=score_scale)
    args = (group_at, jnp.stack(queries), my_smooth, counts, by_head(keys))
    if groups == LINE:
        probs, stats, raw_values = finish_values(scored, *args)
    else:
        probs, stats = scored(*args)
    values = clip_values(raw_values, group_scale)
    messages = weigh(probs, by_head(values), stats)

    messages, keys, values, late = lax.optimization_barrier(
        (messages, keys, values, (own_query, my_smooth))
    )
    messages = to_groups(messages)
    is_key = lax.broadcasted_iota(jnp.int32, (1, 2, 1), 1) == 0
    kv_cache = jnp.where(is_key, keys[:, None, :], values[:, None, :])
    kv_cache = with_layout_constraint(kv_cache, Layout((0, 1, 2)))
    own = fresh(late[0], late[1], *my_new, score_scale)
    messages, kv_cache, own = lax.optimization_barrier((messages, kv_cache, own))
    attention = finish(messages, own, step_count * per_group)
    by_owner = from_owners(attention)
    attention = jnp.concatenate(
        [
            functools.reduce(
                lambda out, k: jnp.where(owner_is[(head + k) % owners], by_owner[k], out),
                range(1, owners),
                by_owner[0],
            )
            for head in range(owners)
        ],
        axis=1,
    ).reshape(decode_query.shape)
    return (kv_cache, smoothing, attention)


def solution(mesh):
    placed = (
        P(("seq", "rep"), None),
        P(("seq", "rep"), "head"),
        P(("seq", "rep"), "head"),
        P(None, "head"),
        P(None, "seq", None, "head"),
        P(None, "seq", "head"),
        P(),
        P(),
    )

    return jax.shard_map(
        on_device,
        mesh=mesh,
        in_specs=placed,
        out_specs=(P(("seq", "rep"), None, "head"), P("head"), P(None, "seq", "head")),
        check_vma=False,
    )
```

```python
import functools
import math

import jax
import jax.numpy as jnp
from jax import lax
from jax.experimental import pallas as pl
from jax.experimental.layout import Layout, with_layout_constraint
from jax.experimental.pallas import tpu as pltpu
from jax.sharding import PartitionSpec as P


HD = 128
PAGE = 32


EPSILON = 1e-05
NEGATIVE = -1e30
LINE = 4


def shifted(x, axis, k):
    n = lax.axis_size(axis)
    return lax.ppermute(x, axis, [(i, (i + k) % n) for i in range(n)])


def partner(me, k, n):
    return me ^ k if n == LINE else (k - me) % n


def swapped(x, axis, k):
    n = lax.axis_size(axis)
    return lax.ppermute(x, axis, [(i, partner(i, k, n)) for i in range(n)])


def from_owners(x):
    return [x] + [shifted(x, "rep", k) for k in range(1, lax.axis_size("rep"))]


def from_groups(x):
    n = lax.axis_size("seq")
    if n != LINE:
        return list(lax.all_gather(x, "seq")[partner(lax.axis_index("seq"), jnp.arange(n), n)])
    return [x] + [swapped(x, "seq", k) for k in range(1, n)]


def to_groups(x):
    n = lax.axis_size("seq")
    if n != LINE:
        order = partner(lax.axis_index("seq"), jnp.arange(n), n)
        back = lax.all_to_all(jnp.stack(x)[order], "seq", split_axis=0, concat_axis=0)
        return list(back[order])
    out = [x[0]]
    for k in range(1, n):
        out.append(swapped(x[k], "seq", k))
    return out


def pack_kernel(weight, query, out, sem):
    depth, columns = weight.shape
    copy = pltpu.make_async_copy(weight, out.at[pl.ds(0, depth)], sem)
    copy.start()
    lines = query.shape[0]
    for k in range(query.shape[1] // columns):
        at = pl.ds(depth + k * lines, lines)
        out[at, :] = query[:, k * columns : (k + 1) * columns]
    copy.wait()


def pack(weight, query):
    depth, columns = weight.shape
    whole = pl.BlockSpec(memory_space=pltpu.VMEM)
    return pl.pallas_call(
        pack_kernel,
        out_shape=jax.ShapeDtypeStruct((depth + query.size // columns, columns), weight.dtype),
        in_specs=[pl.BlockSpec(memory_space=pl.ANY), whole],
        out_specs=whole,
        scratch_shapes=[pltpu.SemaphoreType.DMA],
        compiler_params=pltpu.CompilerParams(vmem_limit_bytes=8 * 2**20),
        name="pack",
    )(weight, query)


def load_kernel(owners, place, hidden, *refs):
    weights, (held, keys, values, taken, arrived, taken_arrived) = refs[:2], refs[2:]
    depth = taken.shape[1]
    blocks = held.shape[1] // depth
    takes = [
        pltpu.make_async_copy(weight.at[pl.ds(0, depth)], taken.at[j], taken_arrived.at[j])
        for j, weight in enumerate(weights)
    ]

    def block(j):
        index = lax.rem(place[0] * owners + place[1] + j, blocks)
        return pl.ds(pl.multiple_of(index * depth, depth), depth)

    def copy(j):
        return pltpu.make_async_copy(hidden.at[:, block(j)], held.at[:, block(j)], arrived.at[j])

    copy(0).start()
    for take in takes:
        take.start()
    for j in range(1, blocks):
        copy(j).start()
    copy(0).wait()
    for j, out in enumerate((keys, values)):
        takes[j].wait()
        out[...] = jnp.dot(held[:, block(0)], taken[j], preferred_element_type=jnp.float32)
    for j in range(1, blocks):
        copy(j).wait()


def load(hidden, key_weight, value_weight, place, owners):
    tokens, width = hidden.shape
    depth, columns = key_weight.shape
    whole = pl.BlockSpec(memory_space=pltpu.VMEM)
    total = jax.ShapeDtypeStruct((tokens, columns), jnp.float32)
    return pl.pallas_call(
        functools.partial(load_kernel, owners),
        out_shape=(jax.ShapeDtypeStruct(hidden.shape, hidden.dtype), total, total),
        in_specs=[
            pl.BlockSpec(memory_space=pltpu.SMEM),
            pl.BlockSpec(memory_space=pltpu.HBM),
            pl.BlockSpec(memory_space=pl.ANY),
            pl.BlockSpec(memory_space=pl.ANY),
        ],
        out_specs=(whole,) * 3,
        scratch_shapes=[
            pltpu.VMEM((2, depth, columns), key_weight.dtype),
            pltpu.SemaphoreType.DMA((width // depth,)),
            pltpu.SemaphoreType.DMA((2,)),
        ],
        compiler_params=pltpu.CompilerParams(vmem_limit_bytes=30 * 2**20),
        cost_estimate=pl.CostEstimate(
            flops=4 * tokens * depth * columns,
            bytes_accessed=2 * tokens * width,
            transcendentals=0,
        ),
        name="load",
    )(place, hidden, key_weight, value_weight)


def project_kernel(depth, start, hops, back, groups, owners, place, left, *refs):
    count = len(hops)
    weights = refs[:count]
    out, held, arrived = refs[-3:]
    size = held.shape[1]
    copies = [
        pltpu.make_async_copy(weights[j].at[pl.ds(0, size)], held.at[j], arrived.at[j])
        for j in range(count)
    ]
    for copy in copies:
        copy.start()
    owner = lax.rem(place[1] + owners - back, owners)
    for j, copy in enumerate(copies):
        copy.wait()
        group = jnp.int32(-1)
        for parity, hop in hops[j]:
            there = place[0] + jnp.where(lax.rem(place[0], 2) == parity, hop, -hop)
            group = jnp.where((there >= 0) & (there < groups), there, group)

        @pl.when((group >= 0) & (group < groups))
        def _(j=j, group=group):
            first = (group * owners + owner) * depth + start
            block = pl.ds(pl.multiple_of(first, math.gcd(depth, start)), size)
            out[...] += jnp.dot(left[:, block], held[j], preferred_element_type=jnp.float32)


def project(hidden, total, weights, depth, part, place, hops, back, groups, owners):
    tokens = hidden.shape[0]
    columns = weights[0].shape[1]
    count = len(weights)
    size = part[1] - part[0]
    whole = pl.BlockSpec(memory_space=pltpu.VMEM)
    return pl.pallas_call(
        functools.partial(project_kernel, depth, part[0], hops, back, groups, owners),
        out_shape=jax.ShapeDtypeStruct((tokens, columns), jnp.float32),
        in_specs=[pl.BlockSpec(memory_space=pltpu.SMEM), whole]
        + [pl.BlockSpec(memory_space=pl.ANY)] * count
        + [whole],
        out_specs=whole,
        scratch_shapes=[
            pltpu.VMEM((count, size, columns), weights[0].dtype),
            pltpu.SemaphoreType.DMA((count,)),
        ],
        compiler_params=pltpu.CompilerParams(vmem_limit_bytes=12 * 2**20),
        cost_estimate=pl.CostEstimate(
            flops=2 * tokens * size * columns * count,
            bytes_accessed=2 * count * size * (tokens + columns) + 8 * tokens * columns,
            transcendentals=0,
        ),
        input_output_aliases={2 + count: 0},
        name="project",
    )(place, hidden, *weights, total)


def score_kernel(slots, parts, steps, scale, group, query, smooth, count, *refs):
    keys, probs, stats = refs[:parts], refs[parts], refs[parts + 1 : parts + 1 + slots]
    scores, tops, sums = refs[-3:]
    tokens = keys[0].shape[0]
    width = keys[0].shape[1]
    requests = count.shape[1]
    rows = scores.shape[0]
    heads = query.shape[1] * query.shape[2] // (steps * requests * width)
    per_line = query.shape[2] // width
    raw = [
        query[0][
            (head // per_line) * steps * requests : (head // per_line + 1) * steps * requests,
            (head % per_line) * width : (head % per_line + 1) * width,
        ]
        for head in range(heads)
    ]
    raw = jnp.concatenate(raw, axis=0)
    scaled = (raw.astype(jnp.float32) * smooth[...]).astype(jnp.bfloat16)
    for p in range(parts):
        scores[:, p * tokens : (p + 1) * tokens] = lax.dot_general(
            scaled, keys[p][...], (((1,), (1,)), ((), ())), preferred_element_type=jnp.float32
        )
    again = 2 if (rows // requests) % 2 == 0 else 1
    times = jnp.concatenate([count[0]] * again, axis=0)
    bias = jnp.where(times > 0.0, 0.0, NEGATIVE)
    for start in range(0, rows, again * requests):
        at = pl.ds(start, again * requests)
        raw = scores[at, :] * scale + bias
        top = jnp.max(raw, axis=1, keepdims=True)
        counted = jnp.exp(raw - top) * times
        probs[0, at, :] = counted.astype(jnp.bfloat16)
        tops[at, :] = jnp.broadcast_to(top, (again * requests, 128))
        sums[at, :] = jnp.broadcast_to(
            jnp.sum(counted, axis=1, keepdims=True), (again * requests, 128)
        )
    for slot in range(slots):

        @pl.when(pl.program_id(0) == slot)
        def _(slot=slot):
            stats[slot][0:1, :] = jnp.transpose(tops[...])[0:1, :]
            stats[slot][1:2, :] = jnp.transpose(sums[...])[0:1, :]


def score(groups, query, smooth, count, keys, steps, scale):
    slots, packed, columns = query.shape
    tokens, width = keys[0].shape
    rows = packed * columns // width
    parts = len(keys)
    requests = count.shape[1]
    probs, *stats = pl.pallas_call(
        functools.partial(score_kernel, slots, parts, steps, scale),
        out_shape=[jax.ShapeDtypeStruct((slots, rows, parts * tokens), jnp.bfloat16)]
        + [jax.ShapeDtypeStruct((2, rows), jnp.float32)] * slots,
        grid_spec=pltpu.PrefetchScalarGridSpec(
            num_scalar_prefetch=1,
            grid=(slots,),
            in_specs=[
                pl.BlockSpec((1, packed, columns), lambda k, group: (k, 0, 0)),
                pl.BlockSpec((1, width), lambda k, group: (0, 0)),
                pl.BlockSpec((1, requests, parts * tokens), lambda k, group: (group[k], 0, 0)),
            ]
            + [pl.BlockSpec((tokens, width), lambda k, group: (0, 0))] * parts,
            out_specs=[pl.BlockSpec((1, rows, parts * tokens), lambda k, group: (k, 0, 0))]
            + [pl.BlockSpec((2, rows), lambda k, group: (0, 0))] * slots,
            scratch_shapes=[
                pltpu.VMEM((rows, parts * tokens), jnp.float32),
                pltpu.VMEM((rows, 128), jnp.float32),
                pltpu.VMEM((rows, 128), jnp.float32),
            ],
        ),
        compiler_params=pltpu.CompilerParams(vmem_limit_bytes=16 * 2**20),
        cost_estimate=pl.CostEstimate(
            flops=2 * slots * rows * width * parts * tokens,
            bytes_accessed=2 * slots * rows * parts * tokens,
            transcendentals=slots * rows * parts * tokens,
        ),
        name="score",
    )(groups, query, smooth, count, *keys)
    return probs, stats


def thirds(x):
    out = []
    for _ in range(3):
        out.append(x.astype(jnp.bfloat16))
        x = x - out[-1].astype(jnp.float32)
    return out


def weigh_own_kernel(probs, values, out):
    out[0] = jnp.dot(probs[0], values[...], preferred_element_type=jnp.float32)


def weigh_kernel(slots, parts, own, *refs):
    probs, values = refs[:parts], refs[parts : 2 * parts]
    stats, outs = refs[2 * parts : 2 * parts + slots], refs[2 * parts + slots :]
    rows, width = own.shape[1:]
    summed = own[0]
    for p in range(parts):
        summed += jnp.dot(probs[p][0], values[p][...], preferred_element_type=jnp.float32)
    for slot in range(slots):

        @pl.when(pl.program_id(0) == slot)
        def _(slot=slot):
            outs[slot][0:rows, :] = summed.astype(jnp.bfloat16)
            lines = []
            for third in thirds(stats[slot][...]):
                third = third.astype(jnp.float32)
                lines += [third[:, c : c + width] for c in range(0, rows, width)]
            tail = outs[slot].shape[0] - rows
            lines.append(jnp.zeros((tail - 2 * len(lines), width), jnp.float32))
            outs[slot][rows:, :] = jnp.concatenate(lines, axis=0).astype(jnp.bfloat16)


def packed_rows(rows, width):
    return rows + (6 * (rows // width) // 16 + 1) * 16


def weigh(probs, values, stats):
    slots, rows, _ = probs.shape
    tokens, width = values[0].shape
    parts = len(values) - 1
    total_rows = packed_rows(rows, width)
    flops = 2 * slots * rows * width * tokens

    def probs_spec(p):
        return pl.BlockSpec((1, rows, tokens), lambda k, p=p: (k, 0, p))

    values_spec = pl.BlockSpec((tokens, width), lambda k: (0, 0))
    own_spec = pl.BlockSpec((1, rows, width), lambda k: (k, 0, 0))
    own = pl.pallas_call(
        weigh_own_kernel,
        out_shape=jax.ShapeDtypeStruct((slots, rows, width), jnp.float32),
        grid=(slots,),
        in_specs=[probs_spec(0), values_spec],
        out_specs=own_spec,
        compiler_params=pltpu.CompilerParams(vmem_limit_bytes=16 * 2**20),
        cost_estimate=pl.CostEstimate(
            flops=flops, bytes_accessed=2 * slots * rows * tokens, transcendentals=0
        ),
        name="weigh_own",
    )(probs, values[0])
    return pl.pallas_call(
        functools.partial(weigh_kernel, slots, parts),
        out_shape=[jax.ShapeDtypeStruct((total_rows, width), jnp.bfloat16)] * slots,
        grid=(slots,),
        in_specs=[own_spec]
        + [probs_spec(p + 1) for p in range(parts)]
        + [values_spec] * parts
        + [pl.BlockSpec((2, rows), lambda k: (0, 0))] * slots,
        out_specs=[pl.BlockSpec((total_rows, width), lambda k: (0, 0))] * slots,
        compiler_params=pltpu.CompilerParams(vmem_limit_bytes=16 * 2**20),
        cost_estimate=pl.CostEstimate(
            flops=flops * parts,
            bytes_accessed=2 * slots * rows * tokens * parts,
            transcendentals=0,
        ),
        name="weigh",
    )(own, *([probs] * parts), *values[1:], *stats)


def fresh_kernel(scale, query, smooth, new_keys, new_values, group_scale, summed, highest, total):
    steps, requests, width = new_keys.shape
    lines = steps * requests

    def by_line(x):
        x = x.astype(jnp.bfloat16).astype(jnp.float32)
        return jnp.concatenate([x] * steps, axis=0)

    def clip(x, row):
        limit = group_scale[row : row + 1, :]
        return jnp.clip(x, -8.0 * limit, 7.0 * limit)

    keys = [by_line(clip(new_keys[u] / smooth[...], 0)) for u in range(steps)]
    values = [by_line(clip(new_values[u], 1)) for u in range(steps)]
    line = lax.broadcasted_iota(jnp.int32, (lines, 1), 0)
    seen = [line >= u * requests for u in range(steps)]
    for head in range(query.shape[1] // width):
        at = pl.ds(head * lines, lines)
        mine = query[:, head * width : (head + 1) * width].astype(jnp.float32) * smooth[...]
        mine = mine.astype(jnp.bfloat16).astype(jnp.float32)
        scores = [
            jnp.where(seen[u], jnp.sum(mine * keys[u], axis=1, keepdims=True) * scale, NEGATIVE)
            for u in range(steps)
        ]
        top = functools.reduce(jnp.maximum, scores)
        expd = [jnp.where(seen[u], jnp.exp(scores[u] - top), 0.0) for u in range(steps)]
        highest[at, :] = jnp.broadcast_to(top, (lines, width))
        total[at, :] = jnp.broadcast_to(sum(expd), (lines, width))
        summed[at, :] = sum(
            e.astype(jnp.bfloat16).astype(jnp.float32) * value for e, value in zip(expd, values)
        )


def fresh(query, smooth, new_keys, new_values, group_scale, scale):
    lines, columns = query.shape
    width = smooth.shape[1]
    part = jax.ShapeDtypeStruct((lines * columns // width, width), jnp.float32)
    return pl.pallas_call(
        functools.partial(fresh_kernel, scale),
        out_shape=(part,) * 3,
        compiler_params=pltpu.CompilerParams(vmem_limit_bytes=16 * 2**20),
        name="fresh",
    )(query, smooth, new_keys, new_values, group_scale)


def finish_kernel(slots, *refs):
    messages, (summed, highest, total, out) = refs[:slots], refs[slots:]
    rows, width = summed.shape
    lines = out.shape[0]
    tails = [message[rows:, :].astype(jnp.float32) for message in messages]
    pieces = rows // width

    def column(slot, piece, which):
        row = [tails[slot][2 * (j * pieces + piece) + which :][:1] for j in range(3)]
        return jnp.transpose(jnp.broadcast_to(row[0] + row[1] + row[2], (width, width)))

    for piece in range(pieces):
        at = pl.ds(piece * width, width)
        parts = [
            (messages[k][at, :].astype(jnp.float32), column(k, piece, 0), column(k, piece, 1))
            for k in range(slots)
        ]
        parts.append((summed[at, :], highest[at, :], total[at, :]))
        top = functools.reduce(jnp.maximum, [part[1] for part in parts])
        shares = [jnp.exp(part[1] - top) for part in parts]
        norm = sum(share * part[2] for share, part in zip(shares, parts))
        merged = sum(share * part[0] for share, part in zip(shares, parts)) / norm
        merged = merged.astype(out.dtype)
        for first in range(0, width, lines):
            head = (piece * width + first) // lines
            out[:, head * width : (head + 1) * width] = merged[first : first + lines]


def finish(messages, own, lines):
    rows, width = own[0].shape
    return pl.pallas_call(
        functools.partial(finish_kernel, len(messages)),
        out_shape=jax.ShapeDtypeStruct((lines, rows * width // lines), jnp.bfloat16),
        compiler_params=pltpu.CompilerParams(vmem_limit_bytes=16 * 2**20),
        name="finish",
    )(*messages, *own)


def token_counts(page_table, lengths, first_pages, pages_dev):
    slots = page_table.shape[1]
    slot_ids = jnp.arange(slots, dtype=jnp.int32)
    whole_slots, rest = lengths // PAGE, lengths % PAGE
    pages = jnp.concatenate(
        [first + jnp.arange(pages_dev, dtype=jnp.int32) for first in first_pages]
    )
    same = page_table[:, :, None] == pages[None, None, :]
    whole = jnp.sum(same & (slot_ids[None, :] < whole_slots[:, None])[:, :, None], axis=1)
    last = jnp.sum(same & (slot_ids[None, :] == whole_slots[:, None])[:, :, None], axis=1)
    token = jnp.arange(pages.shape[0] * PAGE, dtype=jnp.int32)
    spread = token[None, :] // PAGE == jnp.arange(pages.shape[0], dtype=jnp.int32)[:, None]
    spread = spread.astype(jnp.bfloat16)
    whole = jnp.dot(whole.astype(jnp.bfloat16), spread, preferred_element_type=jnp.float32)
    last = jnp.dot(last.astype(jnp.bfloat16), spread, preferred_element_type=jnp.float32)
    return whole + jnp.where((token % PAGE)[None, :] < rest[:, None], last, 0.0)


def clip_keys(raw, smooth, scale):
    return jnp.clip(raw / smooth, -8.0 * scale[0], 7.0 * scale[0]).astype(jnp.bfloat16)


def clip_values(raw, scale):
    return jnp.clip(raw, -8.0 * scale[1], 7.0 * scale[1]).astype(jnp.bfloat16)


def my_part(x, axis, owner_is, ahead=0):
    owners = len(owner_is)
    size = x.shape[axis] // owners
    pieces = [lax.slice_in_dim(x, p * size, (p + 1) * size, axis=axis) for p in range(owners)]
    out = pieces[0]
    for p in range(1, owners):
        out = jnp.where(owner_is[(p - ahead) % owners], pieces[p], out)
    return out


def chip_top(raw_keys):
    top = jnp.max(jnp.abs(raw_keys), axis=0, keepdims=True)
    return functools.reduce(jnp.maximum, from_owners(top))


def smooth_of(top):
    top = functools.reduce(jnp.maximum, from_groups(top))
    return jnp.sqrt(top + EPSILON)


def line_pairs(hop, parity, groups):
    pairs = []
    for i in range(parity, groups - 1, 2):
        if i >= hop - 1:
            pairs.append((i, i + 1))
        if i + hop < groups:
            pairs.append((i + 1, i))
    return pairs


def line_project(hidden, key_weight, value_weight, own_query, early):
    groups, owners = lax.axis_size("seq"), lax.axis_size("rep")
    depth = key_weight.shape[0]
    barrier = lax.optimization_barrier

    def send(x, hop, parity):
        return lax.ppermute(x, "seq", line_pairs(hop, parity, groups))

    def absorb(name, blocks, hops, first=0, part=None):
        part = part or (0, depth)
        passed = [[shifted(block, "rep", k) for block in blocks] for k in range(1, owners)]
        for k, ready in enumerate([blocks] + passed):
            if k < first:
                continue
            totals[name] = project(
                hidden, totals[name], ready, depth, part, early[0], hops, k, groups, owners
            )

    totals = {}
    ka1 = send(key_weight, 1, 0)
    kb1 = send(key_weight, 1, 1)
    value_block = pack(value_weight, own_query)
    va1 = send(value_block, 1, 0)
    early, first = barrier((early, (key_weight, value_block)))
    hidden, totals["k"], totals["v"] = load(hidden, *first, early[0], owners)

    ka1, kb1, value_block, totals = barrier((ka1, kb1, value_block, totals))
    kb2 = send(ka1, 2, 1)
    ka2 = send(kb1, 2, 0)
    vb1 = send(value_block, 1, 1)
    for name, weight in (("k", key_weight), ("v", value_weight)):
        absorb(name, [weight], (((0, 0),),), 1)
    absorb("k", [ka1, kb1], (((0, 1),), ((1, 1),)))

    kb2, va1, own_block, totals = barrier((kb2, va1, value_block, totals))
    ends = [(0, groups - 1), (groups - 1, 0)]
    far_query = lax.ppermute(own_block[depth:], "seq", ends)
    ka3 = send(kb2, 3, 0)
    vb2 = send(va1, 2, 1)
    absorb("v", [va1], (((0, 1),),))

    ka2, totals = barrier((ka2, totals))
    absorb("k", [ka2 + kb2], (((0, 2), (1, 2)),))

    va2 = send(vb1, 2, 0)

    ka3, totals = barrier((ka3, totals))
    absorb("k", [ka3], (((0, 3),),))
    raw_keys = totals["k"]
    top = chip_top(raw_keys)
    smooth = smooth_of(top)
    vb1, vb2, top = barrier((vb1, vb2, top))
    cut = depth * 3 // 4
    va3 = send(vb2[:cut], 3, 0)
    va3_rest = lax.ppermute(vb2[cut:depth], "seq", line_pairs(3, 0, groups))
    absorb("v", [vb1], (((1, 1),),))
    va2, vb2, smooth = barrier((va2, vb2, smooth))
    absorb("v", [va2 + vb2], (((0, 2), (1, 2)),))
    queries = [
        value_block[depth:],
        va1[depth:],
        va2[depth:] + vb2[depth:],
        vb1[depth:] + far_query,
    ]

    def finish_values(scored, *args):
        args, totals["v"] = barrier((args, totals["v"]))
        probs, stats = scored(*args)
        block, stats = barrier((va3, stats))
        absorb("v", [block], (((0, 3),),), part=(0, cut))
        rest, totals["v"] = barrier((va3_rest, totals["v"]))
        absorb("v", [rest], (((0, 3),),), part=(cut, depth))
        return probs, stats, totals["v"]

    return raw_keys, smooth, queries, early, finish_values


def on_device(
    hidden, key_weight, value_weight, group_scale, new_kv, decode_query, page_table, lengths
):
    tokens = hidden.shape[0]
    columns = key_weight.shape[1]
    groups, owners = lax.axis_size("seq"), lax.axis_size("rep")
    my_group, my_owner = lax.axis_index("seq"), lax.axis_index("rep")
    assert columns // HD == owners
    pages_dev = tokens // PAGE
    step_count, per_group = decode_query.shape[:2]

    owner_is = [my_owner == owner for owner in range(owners)]
    own_query = my_part(decode_query, 2, owner_is).reshape(step_count * per_group, -1)

    first_pages = [
        (my_group * owners + (my_owner - k) % owners) * pages_dev for k in range(owners)
    ]
    early = (
        jnp.stack([my_group, my_owner]),
        owner_is,
        first_pages,
        partner(my_group, jnp.arange(groups, dtype=jnp.int32), groups),
        own_query,
    )
    if groups == LINE:
        raw_keys, smooth, queries, early, finish_values = line_project(
            hidden, key_weight, value_weight, own_query, early
        )
    else:
        raw_keys, raw_values = (
            jnp.dot(
                hidden,
                lax.all_gather(weight, ("seq", "rep"), axis=0, tiled=True),
                preferred_element_type=jnp.float32,
            )
            for weight in (key_weight, value_weight)
        )
        queries = from_groups(
            jnp.concatenate(jnp.split(own_query, own_query.shape[1] // columns, axis=1))
        )
        smooth = smooth_of(chip_top(raw_keys))
    _, owner_is, first_pages, group_at, own_query = early
    counts = token_counts(page_table, lengths, first_pages, pages_dev)
    counts = counts.reshape(groups, per_group, -1)
    my_kv = my_part(new_kv, 3, owner_is).astype(jnp.float32)
    my_new = (my_kv[:, :, 0], my_kv[:, :, 1], my_part(group_scale, 1, owner_is))

    def by_head(x):
        return [my_part(x, 1, owner_is)] + [
            shifted(my_part(x, 1, owner_is, k), "rep", k) for k in range(1, owners)
        ]

    smoothing = smooth.reshape(-1)
    my_smooth = my_part(smooth, 1, owner_is)
    keys = clip_keys(raw_keys, smooth, group_scale)
    score_scale = HD ** (-0.5)
    scored = functools.partial(score, steps=step_count, scale=score_scale)
    args = (group_at, jnp.stack(queries), my_smooth, counts, by_head(keys))
    if groups == LINE:
        probs, stats, raw_values = finish_values(scored, *args)
    else:
        probs, stats = scored(*args)
    values = clip_values(raw_values, group_scale)
    messages = weigh(probs, by_head(values), stats)

    messages, keys, values, late = lax.optimization_barrier(
        (messages, keys, values, (own_query, my_smooth))
    )
    messages = to_groups(messages)
    is_key = lax.broadcasted_iota(jnp.int32, (1, 2, 1), 1) == 0
    kv_cache = jnp.where(is_key, keys[:, None, :], values[:, None, :])
    kv_cache = with_layout_constraint(kv_cache, Layout((0, 1, 2)))
    own = fresh(late[0], late[1], *my_new, score_scale)
    messages, kv_cache, own = lax.optimization_barrier((messages, kv_cache, own))
    attention = finish(messages, own, step_count * per_group)
    by_owner = from_owners(attention)
    attention = jnp.concatenate(
        [
            functools.reduce(
                lambda out, k: jnp.where(owner_is[(head + k) % owners], by_owner[k], out),
                range(1, owners),
                by_owner[0],
            )
            for head in range(owners)
        ],
        axis=1,
    ).reshape(decode_query.shape)
    return (kv_cache, smoothing, attention)


def solution(mesh):
    placed = (
        P(("seq", "rep"), None),
        P(("seq", "rep"), "head"),
        P(("seq", "rep"), "head"),
        P(None, "head"),
        P(None, "seq", None, "head"),
        P(None, "seq", "head"),
        P(),
        P(),
    )

    return jax.shard_map(
        on_device,
        mesh=mesh,
        in_specs=placed,
        out_specs=(P(("seq", "rep"), None, "head"), P("head"), P(None, "seq", "head")),
        check_vma=False,
    )
```

```python
import functools
import math

import jax
import jax.numpy as jnp
from jax import lax
from jax.experimental import pallas as pl
from jax.experimental.layout import Layout, with_layout_constraint
from jax.experimental.pallas import tpu as pltpu
from jax.sharding import PartitionSpec as P


HD = 128
PAGE = 32


EPSILON = 1e-05
NEGATIVE = -1e30
LINE = 4


def shifted(x, axis, k):
    n = lax.axis_size(axis)
    return lax.ppermute(x, axis, [(i, (i + k) % n) for i in range(n)])


def partner(me, k, n):
    return me ^ k if n == LINE else (k - me) % n


def swapped(x, axis, k):
    n = lax.axis_size(axis)
    return lax.ppermute(x, axis, [(i, partner(i, k, n)) for i in range(n)])


def from_owners(x):
    return [x] + [shifted(x, "rep", k) for k in range(1, lax.axis_size("rep"))]


def from_groups(x):
    n = lax.axis_size("seq")
    if n != LINE:
        return list(lax.all_gather(x, "seq")[partner(lax.axis_index("seq"), jnp.arange(n), n)])
    return [x] + [swapped(x, "seq", k) for k in range(1, n)]


def to_groups(x):
    n = lax.axis_size("seq")
    if n != LINE:
        order = partner(lax.axis_index("seq"), jnp.arange(n), n)
        back = lax.all_to_all(jnp.stack(x)[order], "seq", split_axis=0, concat_axis=0)
        return list(back[order])
    out = [x[0]]
    for k in range(1, n):
        out.append(swapped(x[k], "seq", k))
    return out


def pack_kernel(weight, query, out, sem):
    depth, columns = weight.shape
    copy = pltpu.make_async_copy(weight, out.at[pl.ds(0, depth)], sem)
    copy.start()
    lines = query.shape[0]
    for k in range(query.shape[1] // columns):
        at = pl.ds(depth + k * lines, lines)
        out[at, :] = query[:, k * columns : (k + 1) * columns]
    copy.wait()


def pack(weight, query):
    depth, columns = weight.shape
    whole = pl.BlockSpec(memory_space=pltpu.VMEM)
    return pl.pallas_call(
        pack_kernel,
        out_shape=jax.ShapeDtypeStruct((depth + query.size // columns, columns), weight.dtype),
        in_specs=[pl.BlockSpec(memory_space=pl.ANY), whole],
        out_specs=whole,
        scratch_shapes=[pltpu.SemaphoreType.DMA],
        compiler_params=pltpu.CompilerParams(vmem_limit_bytes=8 * 2**20),
        name="pack",
    )(weight, query)


def load_kernel(owners, place, hidden, *refs):
    weights, (held, keys, values, taken, arrived, taken_arrived) = refs[:2], refs[2:]
    depth = taken.shape[1]
    blocks = held.shape[1] // depth
    takes = [
        pltpu.make_async_copy(weight.at[pl.ds(0, depth)], taken.at[j], taken_arrived.at[j])
        for j, weight in enumerate(weights)
    ]

    def block(j):
        index = lax.rem(place[0] * owners + place[1] + j, blocks)
        return pl.ds(pl.multiple_of(index * depth, depth), depth)

    def copy(j):
        return pltpu.make_async_copy(hidden.at[:, block(j)], held.at[:, block(j)], arrived.at[j])

    copy(0).start()
    for take in takes:
        take.start()
    for j in range(1, blocks):
        copy(j).start()
    copy(0).wait()
    for j, out in enumerate((keys, values)):
        takes[j].wait()
        out[...] = jnp.dot(held[:, block(0)], taken[j], preferred_element_type=jnp.float32)
    for j in range(1, blocks):
        copy(j).wait()


def load(hidden, key_weight, value_weight, place, owners):
    tokens, width = hidden.shape
    depth, columns = key_weight.shape
    whole = pl.BlockSpec(memory_space=pltpu.VMEM)
    total = jax.ShapeDtypeStruct((tokens, columns), jnp.float32)
    return pl.pallas_call(
        functools.partial(load_kernel, owners),
        out_shape=(jax.ShapeDtypeStruct(hidden.shape, hidden.dtype), total, total),
        in_specs=[
            pl.BlockSpec(memory_space=pltpu.SMEM),
            pl.BlockSpec(memory_space=pltpu.HBM),
            pl.BlockSpec(memory_space=pl.ANY),
            pl.BlockSpec(memory_space=pl.ANY),
        ],
        out_specs=(whole,) * 3,
        scratch_shapes=[
            pltpu.VMEM((2, depth, columns), key_weight.dtype),
            pltpu.SemaphoreType.DMA((width // depth,)),
            pltpu.SemaphoreType.DMA((2,)),
        ],
        compiler_params=pltpu.CompilerParams(vmem_limit_bytes=30 * 2**20),
        cost_estimate=pl.CostEstimate(
            flops=4 * tokens * depth * columns,
            bytes_accessed=2 * tokens * width,
            transcendentals=0,
        ),
        name="load",
    )(place, hidden, key_weight, value_weight)


def project_kernel(depth, start, hops, back, groups, owners, place, left, *refs):
    count = len(hops)
    weights = refs[:count]
    out, held, arrived = refs[-3:]
    size = held.shape[1]
    copies = [
        pltpu.make_async_copy(weights[j].at[pl.ds(0, size)], held.at[j], arrived.at[j])
        for j in range(count)
    ]
    owner = lax.rem(place[1] + owners - back, owners)
    sources = []
    for j in range(count):
        group = jnp.int32(-1)
        for parity, hop in hops[j]:
            there = place[0] + jnp.where(lax.rem(place[0], 2) == parity, hop, -hop)
            group = jnp.where((there >= 0) & (there < groups), there, group)
        sources.append(group)

        @pl.when(group >= 0)
        def _(j=j):
            copies[j].start()

    for j, group in enumerate(sources):

        @pl.when(group >= 0)
        def _(j=j, group=group):
            copies[j].wait()
            first = (group * owners + owner) * depth + start
            block = pl.ds(pl.multiple_of(first, math.gcd(depth, start)), size)
            out[...] += jnp.dot(left[:, block], held[j], preferred_element_type=jnp.float32)


def project(hidden, total, weights, depth, part, place, hops, back, groups, owners):
    tokens = hidden.shape[0]
    columns = weights[0].shape[1]
    count = len(weights)
    size = part[1] - part[0]
    whole = pl.BlockSpec(memory_space=pltpu.VMEM)
    return pl.pallas_call(
        functools.partial(project_kernel, depth, part[0], hops, back, groups, owners),
        out_shape=jax.ShapeDtypeStruct((tokens, columns), jnp.float32),
        in_specs=[pl.BlockSpec(memory_space=pltpu.SMEM), whole]
        + [pl.BlockSpec(memory_space=pl.ANY)] * count
        + [whole],
        out_specs=whole,
        scratch_shapes=[
            pltpu.VMEM((count, size, columns), weights[0].dtype),
            pltpu.SemaphoreType.DMA((count,)),
        ],
        compiler_params=pltpu.CompilerParams(vmem_limit_bytes=12 * 2**20),
        cost_estimate=pl.CostEstimate(
            flops=2 * tokens * size * columns * count,
            bytes_accessed=2 * count * size * (tokens + columns) + 8 * tokens * columns,
            transcendentals=0,
        ),
        input_output_aliases={2 + count: 0},
        name="project",
    )(place, hidden, *weights, total)


def score_kernel(slots, parts, steps, scale, group, query, smooth, count, *refs):
    keys, probs, stats = refs[:parts], refs[parts], refs[parts + 1 : parts + 1 + slots]
    scores, tops, sums = refs[-3:]
    tokens = keys[0].shape[0]
    width = keys[0].shape[1]
    requests = count.shape[1]
    rows = scores.shape[0]
    heads = query.shape[1] * query.shape[2] // (steps * requests * width)
    per_line = query.shape[2] // width
    raw = [
        query[0][
            (head // per_line) * steps * requests : (head // per_line + 1) * steps * requests,
            (head % per_line) * width : (head % per_line + 1) * width,
        ]
        for head in range(heads)
    ]
    raw = jnp.concatenate(raw, axis=0)
    scaled = (raw.astype(jnp.float32) * smooth[...]).astype(jnp.bfloat16)
    for p in range(parts):
        scores[:, p * tokens : (p + 1) * tokens] = lax.dot_general(
            scaled, keys[p][...], (((1,), (1,)), ((), ())), preferred_element_type=jnp.float32
        )
    again = 2 if (rows // requests) % 2 == 0 else 1
    times = jnp.concatenate([count[0]] * again, axis=0)
    bias = jnp.where(times > 0.0, 0.0, NEGATIVE)
    for start in range(0, rows, again * requests):
        at = pl.ds(start, again * requests)
        raw = scores[at, :] * scale + bias
        top = jnp.max(raw, axis=1, keepdims=True)
        counted = jnp.exp(raw - top) * times
        probs[0, at, :] = counted.astype(jnp.bfloat16)
        tops[at, :] = jnp.broadcast_to(top, (again * requests, 128))
        sums[at, :] = jnp.broadcast_to(
            jnp.sum(counted, axis=1, keepdims=True), (again * requests, 128)
        )
    for slot in range(slots):

        @pl.when(pl.program_id(0) == slot)
        def _(slot=slot):
            stats[slot][0:1, :] = jnp.transpose(tops[...])[0:1, :]
            stats[slot][1:2, :] = jnp.transpose(sums[...])[0:1, :]


def score(groups, query, smooth, count, keys, steps, scale):
    slots, packed, columns = query.shape
    tokens, width = keys[0].shape
    rows = packed * columns // width
    parts = len(keys)
    requests = count.shape[1]
    probs, *stats = pl.pallas_call(
        functools.partial(score_kernel, slots, parts, steps, scale),
        out_shape=[jax.ShapeDtypeStruct((slots, rows, parts * tokens), jnp.bfloat16)]
        + [jax.ShapeDtypeStruct((2, rows), jnp.float32)] * slots,
        grid_spec=pltpu.PrefetchScalarGridSpec(
            num_scalar_prefetch=1,
            grid=(slots,),
            in_specs=[
                pl.BlockSpec((1, packed, columns), lambda k, group: (k, 0, 0)),
                pl.BlockSpec((1, width), lambda k, group: (0, 0)),
                pl.BlockSpec((1, requests, parts * tokens), lambda k, group: (group[k], 0, 0)),
            ]
            + [pl.BlockSpec((tokens, width), lambda k, group: (0, 0))] * parts,
            out_specs=[pl.BlockSpec((1, rows, parts * tokens), lambda k, group: (k, 0, 0))]
            + [pl.BlockSpec((2, rows), lambda k, group: (0, 0))] * slots,
            scratch_shapes=[
                pltpu.VMEM((rows, parts * tokens), jnp.float32),
                pltpu.VMEM((rows, 128), jnp.float32),
                pltpu.VMEM((rows, 128), jnp.float32),
            ],
        ),
        compiler_params=pltpu.CompilerParams(vmem_limit_bytes=16 * 2**20),
        cost_estimate=pl.CostEstimate(
            flops=2 * slots * rows * width * parts * tokens,
            bytes_accessed=2 * slots * rows * parts * tokens,
            transcendentals=slots * rows * parts * tokens,
        ),
        name="score",
    )(groups, query, smooth, count, *keys)
    return probs, stats


def thirds(x):
    out = []
    for _ in range(3):
        out.append(x.astype(jnp.bfloat16))
        x = x - out[-1].astype(jnp.float32)
    return out


def weigh_own_kernel(probs, values, out):
    out[0] = jnp.dot(probs[0], values[...], preferred_element_type=jnp.float32)


def weigh_kernel(slots, parts, own, *refs):
    probs, values = refs[:parts], refs[parts : 2 * parts]
    stats, outs = refs[2 * parts : 2 * parts + slots], refs[2 * parts + slots :]
    rows, width = own.shape[1:]
    summed = own[0]
    for p in range(parts):
        summed += jnp.dot(probs[p][0], values[p][...], preferred_element_type=jnp.float32)
    for slot in range(slots):

        @pl.when(pl.program_id(0) == slot)
        def _(slot=slot):
            outs[slot][0:rows, :] = summed.astype(jnp.bfloat16)
            lines = []
            for third in thirds(stats[slot][...]):
                third = third.astype(jnp.float32)
                lines += [third[:, c : c + width] for c in range(0, rows, width)]
            tail = outs[slot].shape[0] - rows
            lines.append(jnp.zeros((tail - 2 * len(lines), width), jnp.float32))
            outs[slot][rows:, :] = jnp.concatenate(lines, axis=0).astype(jnp.bfloat16)


def packed_rows(rows, width):
    return rows + (6 * (rows // width) // 16 + 1) * 16


def weigh(probs, values, stats):
    slots, rows, _ = probs.shape
    tokens, width = values[0].shape
    parts = len(values) - 1
    total_rows = packed_rows(rows, width)
    flops = 2 * slots * rows * width * tokens

    def probs_spec(p):
        return pl.BlockSpec((1, rows, tokens), lambda k, p=p: (k, 0, p))

    values_spec = pl.BlockSpec((tokens, width), lambda k: (0, 0))
    own_spec = pl.BlockSpec((1, rows, width), lambda k: (k, 0, 0))
    own = pl.pallas_call(
        weigh_own_kernel,
        out_shape=jax.ShapeDtypeStruct((slots, rows, width), jnp.float32),
        grid=(slots,),
        in_specs=[probs_spec(0), values_spec],
        out_specs=own_spec,
        compiler_params=pltpu.CompilerParams(vmem_limit_bytes=16 * 2**20),
        cost_estimate=pl.CostEstimate(
            flops=flops, bytes_accessed=2 * slots * rows * tokens, transcendentals=0
        ),
        name="weigh_own",
    )(probs, values[0])
    return pl.pallas_call(
        functools.partial(weigh_kernel, slots, parts),
        out_shape=[jax.ShapeDtypeStruct((total_rows, width), jnp.bfloat16)] * slots,
        grid=(slots,),
        in_specs=[own_spec]
        + [probs_spec(p + 1) for p in range(parts)]
        + [values_spec] * parts
        + [pl.BlockSpec((2, rows), lambda k: (0, 0))] * slots,
        out_specs=[pl.BlockSpec((total_rows, width), lambda k: (0, 0))] * slots,
        compiler_params=pltpu.CompilerParams(vmem_limit_bytes=16 * 2**20),
        cost_estimate=pl.CostEstimate(
            flops=flops * parts,
            bytes_accessed=2 * slots * rows * tokens * parts,
            transcendentals=0,
        ),
        name="weigh",
    )(own, *([probs] * parts), *values[1:], *stats)


def fresh_kernel(scale, query, smooth, new_keys, new_values, group_scale, summed, highest, total):
    steps, requests, width = new_keys.shape
    lines = steps * requests

    def by_line(x):
        x = x.astype(jnp.bfloat16).astype(jnp.float32)
        return jnp.concatenate([x] * steps, axis=0)

    def clip(x, row):
        limit = group_scale[row : row + 1, :]
        return jnp.clip(x, -8.0 * limit, 7.0 * limit)

    keys = [by_line(clip(new_keys[u] / smooth[...], 0)) for u in range(steps)]
    values = [by_line(clip(new_values[u], 1)) for u in range(steps)]
    line = lax.broadcasted_iota(jnp.int32, (lines, 1), 0)
    seen = [line >= u * requests for u in range(steps)]
    for head in range(query.shape[1] // width):
        at = pl.ds(head * lines, lines)
        mine = query[:, head * width : (head + 1) * width].astype(jnp.float32) * smooth[...]
        mine = mine.astype(jnp.bfloat16).astype(jnp.float32)
        scores = [
            jnp.where(seen[u], jnp.sum(mine * keys[u], axis=1, keepdims=True) * scale, NEGATIVE)
            for u in range(steps)
        ]
        top = functools.reduce(jnp.maximum, scores)
        expd = [jnp.where(seen[u], jnp.exp(scores[u] - top), 0.0) for u in range(steps)]
        highest[at, :] = jnp.broadcast_to(top, (lines, width))
        total[at, :] = jnp.broadcast_to(sum(expd), (lines, width))
        summed[at, :] = sum(
            e.astype(jnp.bfloat16).astype(jnp.float32) * value for e, value in zip(expd, values)
        )


def fresh(query, smooth, new_keys, new_values, group_scale, scale):
    lines, columns = query.shape
    width = smooth.shape[1]
    part = jax.ShapeDtypeStruct((lines * columns // width, width), jnp.float32)
    return pl.pallas_call(
        functools.partial(fresh_kernel, scale),
        out_shape=(part,) * 3,
        compiler_params=pltpu.CompilerParams(vmem_limit_bytes=16 * 2**20),
        name="fresh",
    )(query, smooth, new_keys, new_values, group_scale)


def finish_kernel(slots, *refs):
    messages, (summed, highest, total, out) = refs[:slots], refs[slots:]
    rows, width = summed.shape
    lines = out.shape[0]
    tails = [message[rows:, :].astype(jnp.float32) for message in messages]
    pieces = rows // width

    def column(slot, piece, which):
        row = [tails[slot][2 * (j * pieces + piece) + which :][:1] for j in range(3)]
        return jnp.transpose(jnp.broadcast_to(row[0] + row[1] + row[2], (width, width)))

    for piece in range(pieces):
        at = pl.ds(piece * width, width)
        parts = [
            (messages[k][at, :].astype(jnp.float32), column(k, piece, 0), column(k, piece, 1))
            for k in range(slots)
        ]
        parts.append((summed[at, :], highest[at, :], total[at, :]))
        top = functools.reduce(jnp.maximum, [part[1] for part in parts])
        shares = [jnp.exp(part[1] - top) for part in parts]
        norm = sum(share * part[2] for share, part in zip(shares, parts))
        merged = sum(share * part[0] for share, part in zip(shares, parts)) / norm
        merged = merged.astype(out.dtype)
        for first in range(0, width, lines):
            head = (piece * width + first) // lines
            out[:, head * width : (head + 1) * width] = merged[first : first + lines]


def finish(messages, own, lines):
    rows, width = own[0].shape
    return pl.pallas_call(
        functools.partial(finish_kernel, len(messages)),
        out_shape=jax.ShapeDtypeStruct((lines, rows * width // lines), jnp.bfloat16),
        compiler_params=pltpu.CompilerParams(vmem_limit_bytes=16 * 2**20),
        name="finish",
    )(*messages, *own)


def token_counts(page_table, lengths, first_pages, pages_dev):
    slots = page_table.shape[1]
    slot_ids = jnp.arange(slots, dtype=jnp.int32)
    whole_slots, rest = lengths // PAGE, lengths % PAGE
    pages = jnp.concatenate(
        [first + jnp.arange(pages_dev, dtype=jnp.int32) for first in first_pages]
    )
    same = page_table[:, :, None] == pages[None, None, :]
    whole = jnp.sum(same & (slot_ids[None, :] < whole_slots[:, None])[:, :, None], axis=1)
    last = jnp.sum(same & (slot_ids[None, :] == whole_slots[:, None])[:, :, None], axis=1)
    token = jnp.arange(pages.shape[0] * PAGE, dtype=jnp.int32)
    spread = token[None, :] // PAGE == jnp.arange(pages.shape[0], dtype=jnp.int32)[:, None]
    spread = spread.astype(jnp.bfloat16)
    whole = jnp.dot(whole.astype(jnp.bfloat16), spread, preferred_element_type=jnp.float32)
    last = jnp.dot(last.astype(jnp.bfloat16), spread, preferred_element_type=jnp.float32)
    return whole + jnp.where((token % PAGE)[None, :] < rest[:, None], last, 0.0)


def clip_keys(raw, smooth, scale):
    return jnp.clip(raw / smooth, -8.0 * scale[0], 7.0 * scale[0]).astype(jnp.bfloat16)


def clip_values(raw, scale):
    return jnp.clip(raw, -8.0 * scale[1], 7.0 * scale[1]).astype(jnp.bfloat16)


def my_part(x, axis, owner_is, ahead=0):
    owners = len(owner_is)
    size = x.shape[axis] // owners
    pieces = [lax.slice_in_dim(x, p * size, (p + 1) * size, axis=axis) for p in range(owners)]
    out = pieces[0]
    for p in range(1, owners):
        out = jnp.where(owner_is[(p - ahead) % owners], pieces[p], out)
    return out


def chip_top(raw_keys):
    top = jnp.max(jnp.abs(raw_keys), axis=0, keepdims=True)
    return functools.reduce(jnp.maximum, from_owners(top))


def smooth_of(top):
    top = functools.reduce(jnp.maximum, from_groups(top))
    return jnp.sqrt(top + EPSILON)


def line_pairs(hop, parity, groups):
    pairs = []
    for i in range(parity, groups - 1, 2):
        if i >= hop - 1:
            pairs.append((i, i + 1))
        if i + hop < groups:
            pairs.append((i + 1, i))
    return pairs


def line_project(hidden, key_weight, value_weight, own_query, early):
    groups, owners = lax.axis_size("seq"), lax.axis_size("rep")
    depth = key_weight.shape[0]
    barrier = lax.optimization_barrier

    def send(x, hop, parity):
        return lax.ppermute(x, "seq", line_pairs(hop, parity, groups))

    def absorb(name, blocks, hops, first=0, part=None):
        part = part or (0, depth)
        passed = [[shifted(block, "rep", k) for block in blocks] for k in range(1, owners)]
        for k, ready in enumerate([blocks] + passed):
            if k < first:
                continue
            totals[name] = project(
                hidden, totals[name], ready, depth, part, early[0], hops, k, groups, owners
            )

    totals = {}
    ka1 = send(key_weight, 1, 0)
    kb1 = send(key_weight, 1, 1)
    value_block = pack(value_weight, own_query)
    va1 = send(value_block, 1, 0)
    early, first = barrier((early, (key_weight, value_block)))
    hidden, totals["k"], totals["v"] = load(hidden, *first, early[0], owners)

    ka1, kb1, value_block, totals = barrier((ka1, kb1, value_block, totals))
    kb2 = send(ka1, 2, 1)
    ka2 = send(kb1, 2, 0)
    vb1 = send(value_block, 1, 1)
    for name, weight in (("k", key_weight), ("v", value_weight)):
        absorb(name, [weight], (((0, 0),),), 1)
    absorb("k", [ka1, kb1], (((0, 1),), ((1, 1),)))

    kb2, va1, own_block, totals = barrier((kb2, va1, value_block, totals))
    ends = [(0, groups - 1), (groups - 1, 0)]
    far_query = lax.ppermute(own_block[depth:], "seq", ends)
    ka3 = send(kb2, 3, 0)
    vb2 = send(va1, 2, 1)
    absorb("v", [va1], (((0, 1),),))

    ka2, totals = barrier((ka2, totals))
    absorb("k", [ka2 + kb2], (((0, 2), (1, 2)),))

    va2 = send(vb1, 2, 0)

    ka3, totals = barrier((ka3, totals))
    absorb("k", [ka3], (((0, 3),),))
    raw_keys = totals["k"]
    top = chip_top(raw_keys)
    smooth = smooth_of(top)
    vb1, vb2, top = barrier((vb1, vb2, top))
    cut = depth * 3 // 4
    va3 = send(vb2[:cut], 3, 0)
    va3_rest = lax.ppermute(vb2[cut:depth], "seq", line_pairs(3, 0, groups))
    absorb("v", [vb1], (((1, 1),),))
    va2, vb2, smooth = barrier((va2, vb2, smooth))
    absorb("v", [va2 + vb2], (((0, 2), (1, 2)),))
    queries = [
        value_block[depth:],
        va1[depth:],
        va2[depth:] + vb2[depth:],
        vb1[depth:] + far_query,
    ]

    def finish_values(scored, *args):
        args, totals["v"] = barrier((args, totals["v"]))
        probs, stats = scored(*args)
        block, stats = barrier((va3, stats))
        absorb("v", [block], (((0, 3),),), part=(0, cut))
        rest, totals["v"] = barrier((va3_rest, totals["v"]))
        absorb("v", [rest], (((0, 3),),), part=(cut, depth))
        return probs, stats, totals["v"]

    return raw_keys, smooth, queries, early, finish_values


def on_device(
    hidden, key_weight, value_weight, group_scale, new_kv, decode_query, page_table, lengths
):
    tokens = hidden.shape[0]
    columns = key_weight.shape[1]
    groups, owners = lax.axis_size("seq"), lax.axis_size("rep")
    my_group, my_owner = lax.axis_index("seq"), lax.axis_index("rep")
    assert columns // HD == owners
    pages_dev = tokens // PAGE
    step_count, per_group = decode_query.shape[:2]

    owner_is = [my_owner == owner for owner in range(owners)]
    own_query = my_part(decode_query, 2, owner_is).reshape(step_count * per_group, -1)

    first_pages = [
        (my_group * owners + (my_owner - k) % owners) * pages_dev for k in range(owners)
    ]
    early = (
        jnp.stack([my_group, my_owner]),
        owner_is,
        first_pages,
        partner(my_group, jnp.arange(groups, dtype=jnp.int32), groups),
        own_query,
    )
    if groups == LINE:
        raw_keys, smooth, queries, early, finish_values = line_project(
            hidden, key_weight, value_weight, own_query, early
        )
    else:
        raw_keys, raw_values = (
            jnp.dot(
                hidden,
                lax.all_gather(weight, ("seq", "rep"), axis=0, tiled=True),
                preferred_element_type=jnp.float32,
            )
            for weight in (key_weight, value_weight)
        )
        queries = from_groups(
            jnp.concatenate(jnp.split(own_query, own_query.shape[1] // columns, axis=1))
        )
        smooth = smooth_of(chip_top(raw_keys))
    _, owner_is, first_pages, group_at, own_query = early
    counts = token_counts(page_table, lengths, first_pages, pages_dev)
    counts = counts.reshape(groups, per_group, -1)
    my_kv = my_part(new_kv, 3, owner_is).astype(jnp.float32)
    my_new = (my_kv[:, :, 0], my_kv[:, :, 1], my_part(group_scale, 1, owner_is))

    def by_head(x):
        return [my_part(x, 1, owner_is)] + [
            shifted(my_part(x, 1, owner_is, k), "rep", k) for k in range(1, owners)
        ]

    smoothing = smooth.reshape(-1)
    my_smooth = my_part(smooth, 1, owner_is)
    keys = clip_keys(raw_keys, smooth, group_scale)
    score_scale = HD ** (-0.5)
    scored = functools.partial(score, steps=step_count, scale=score_scale)
    args = (group_at, jnp.stack(queries), my_smooth, counts, by_head(keys))
    if groups == LINE:
        probs, stats, raw_values = finish_values(scored, *args)
    else:
        probs, stats = scored(*args)
    values = clip_values(raw_values, group_scale)
    messages = weigh(probs, by_head(values), stats)

    messages, keys, values, late = lax.optimization_barrier(
        (messages, keys, values, (own_query, my_smooth))
    )
    messages = to_groups(messages)
    is_key = lax.broadcasted_iota(jnp.int32, (1, 2, 1), 1) == 0
    kv_cache = jnp.where(is_key, keys[:, None, :], values[:, None, :])
    kv_cache = with_layout_constraint(kv_cache, Layout((0, 1, 2)))
    own = fresh(late[0], late[1], *my_new, score_scale)
    messages, kv_cache, own = lax.optimization_barrier((messages, kv_cache, own))
    attention = finish(messages, own, step_count * per_group)
    by_owner = from_owners(attention)
    attention = jnp.concatenate(
        [
            functools.reduce(
                lambda out, k: jnp.where(owner_is[(head + k) % owners], by_owner[k], out),
                range(1, owners),
                by_owner[0],
            )
            for head in range(owners)
        ],
        axis=1,
    ).reshape(decode_query.shape)
    return (kv_cache, smoothing, attention)


def solution(mesh):
    placed = (
        P(("seq", "rep"), None),
        P(("seq", "rep"), "head"),
        P(("seq", "rep"), "head"),
        P(None, "head"),
        P(None, "seq", None, "head"),
        P(None, "seq", "head"),
        P(),
        P(),
    )

    return jax.shard_map(
        on_device,
        mesh=mesh,
        in_specs=placed,
        out_specs=(P(("seq", "rep"), None, "head"), P("head"), P(None, "seq", "head")),
        check_vma=False,
    )
```

```python
import functools

import jax
import jax.numpy as jnp
from jax import lax
from jax.experimental import pallas as pl
from jax.experimental.layout import Layout, with_layout_constraint
from jax.experimental.pallas import tpu as pltpu
from jax.sharding import PartitionSpec as P


HD = 128
PAGE = 32


EPSILON = 1e-05
NEGATIVE = -1e30
LINE = 4


def shifted(x, axis, k):
    n = lax.axis_size(axis)
    return lax.ppermute(x, axis, [(i, (i + k) % n) for i in range(n)])


def partner(me, k, n):
    return me ^ k if n == LINE else (k - me) % n


def swapped(x, axis, k):
    n = lax.axis_size(axis)
    return lax.ppermute(x, axis, [(i, partner(i, k, n)) for i in range(n)])


def from_owners(x):
    return [x] + [shifted(x, "rep", k) for k in range(1, lax.axis_size("rep"))]


def from_groups(x):
    n = lax.axis_size("seq")
    if n != LINE:
        return list(lax.all_gather(x, "seq")[partner(lax.axis_index("seq"), jnp.arange(n), n)])
    return [x] + [swapped(x, "seq", k) for k in range(1, n)]


def to_groups(x):
    n = lax.axis_size("seq")
    if n != LINE:
        order = partner(lax.axis_index("seq"), jnp.arange(n), n)
        back = lax.all_to_all(jnp.stack(x)[order], "seq", split_axis=0, concat_axis=0)
        return list(back[order])
    out = [x[0]]
    for k in range(1, n):
        out.append(swapped(x[k], "seq", k))
    return out


def pack_kernel(weight, query, out, sem):
    depth, columns = weight.shape
    copy = pltpu.make_async_copy(weight, out.at[pl.ds(0, depth)], sem)
    copy.start()
    lines = query.shape[0]
    for k in range(query.shape[1] // columns):
        at = pl.ds(depth + k * lines, lines)
        out[at, :] = query[:, k * columns : (k + 1) * columns]
    copy.wait()


def pack(weight, query):
    depth, columns = weight.shape
    whole = pl.BlockSpec(memory_space=pltpu.VMEM)
    return pl.pallas_call(
        pack_kernel,
        out_shape=jax.ShapeDtypeStruct((depth + query.size // columns, columns), weight.dtype),
        in_specs=[pl.BlockSpec(memory_space=pl.ANY), whole],
        out_specs=whole,
        scratch_shapes=[pltpu.SemaphoreType.DMA],
        compiler_params=pltpu.CompilerParams(vmem_limit_bytes=8 * 2**20),
        name="pack",
    )(weight, query)


def load_kernel(owners, place, hidden, *refs):
    weights, (held, keys, values, taken, arrived, taken_arrived) = refs[:2], refs[2:]
    depth = taken.shape[1]
    blocks = held.shape[1] // depth
    takes = [
        pltpu.make_async_copy(weight.at[pl.ds(0, depth)], taken.at[j], taken_arrived.at[j])
        for j, weight in enumerate(weights)
    ]

    def block(j):
        index = lax.rem(place[0] * owners + place[1] + j, blocks)
        return pl.ds(pl.multiple_of(index * depth, depth), depth)

    def copy(j):
        return pltpu.make_async_copy(hidden.at[:, block(j)], held.at[:, block(j)], arrived.at[j])

    copy(0).start()
    for take in takes:
        take.start()
    for j in range(1, blocks):
        copy(j).start()
    copy(0).wait()
    for j, out in enumerate((keys, values)):
        takes[j].wait()
        out[...] = jnp.dot(held[:, block(0)], taken[j], preferred_element_type=jnp.float32)
    for j in range(1, blocks):
        copy(j).wait()


def load(hidden, key_weight, value_weight, place, owners):
    tokens, width = hidden.shape
    depth, columns = key_weight.shape
    whole = pl.BlockSpec(memory_space=pltpu.VMEM)
    total = jax.ShapeDtypeStruct((tokens, columns), jnp.float32)
    return pl.pallas_call(
        functools.partial(load_kernel, owners),
        out_shape=(jax.ShapeDtypeStruct(hidden.shape, hidden.dtype), total, total),
        in_specs=[
            pl.BlockSpec(memory_space=pltpu.SMEM),
            pl.BlockSpec(memory_space=pltpu.HBM),
            pl.BlockSpec(memory_space=pl.ANY),
            pl.BlockSpec(memory_space=pl.ANY),
        ],
        out_specs=(whole,) * 3,
        scratch_shapes=[
            pltpu.VMEM((2, depth, columns), key_weight.dtype),
            pltpu.SemaphoreType.DMA((width // depth,)),
            pltpu.SemaphoreType.DMA((2,)),
        ],
        compiler_params=pltpu.CompilerParams(vmem_limit_bytes=30 * 2**20),
        cost_estimate=pl.CostEstimate(
            flops=4 * tokens * depth * columns,
            bytes_accessed=2 * tokens * width,
            transcendentals=0,
        ),
        name="load",
    )(place, hidden, key_weight, value_weight)


def project_kernel(hops, back, groups, owners, place, left, *refs):
    count = len(hops)
    weights = refs[:count]
    out, held, arrived = refs[-3:]
    depth = held.shape[1]
    copies = [
        pltpu.make_async_copy(weights[j].at[pl.ds(0, depth)], held.at[j], arrived.at[j])
        for j in range(count)
    ]
    owner = lax.rem(place[1] + owners - back, owners)
    sources = []
    for j in range(count):
        group = jnp.int32(-1)
        for parity, hop in hops[j]:
            there = place[0] + jnp.where(lax.rem(place[0], 2) == parity, hop, -hop)
            group = jnp.where((there >= 0) & (there < groups), there, group)
        sources.append(group)

        @pl.when(group >= 0)
        def _(j=j):
            copies[j].start()

    for j, group in enumerate(sources):

        @pl.when(group >= 0)
        def _(j=j, group=group):
            copies[j].wait()
            block = pl.ds(pl.multiple_of((group * owners + owner) * depth, depth), depth)
            out[...] += jnp.dot(left[:, block], held[j], preferred_element_type=jnp.float32)


def project(hidden, total, weights, depth, place, hops, back, groups, owners):
    tokens = hidden.shape[0]
    columns = weights[0].shape[1]
    count = len(weights)
    whole = pl.BlockSpec(memory_space=pltpu.VMEM)
    return pl.pallas_call(
        functools.partial(project_kernel, hops, back, groups, owners),
        out_shape=jax.ShapeDtypeStruct((tokens, columns), jnp.float32),
        in_specs=[pl.BlockSpec(memory_space=pltpu.SMEM), whole]
        + [pl.BlockSpec(memory_space=pl.ANY)] * count
        + [whole],
        out_specs=whole,
        scratch_shapes=[
            pltpu.VMEM((count, depth, columns), weights[0].dtype),
            pltpu.SemaphoreType.DMA((count,)),
        ],
        compiler_params=pltpu.CompilerParams(vmem_limit_bytes=12 * 2**20),
        cost_estimate=pl.CostEstimate(
            flops=2 * tokens * depth * columns * count,
            bytes_accessed=2 * count * depth * (tokens + columns) + 8 * tokens * columns,
            transcendentals=0,
        ),
        input_output_aliases={2 + count: 0},
        name="project",
    )(place, hidden, *weights, total)


def score_kernel(slots, parts, steps, scale, group, query, smooth, count, *refs):
    keys, probs, stats = refs[:parts], refs[parts], refs[parts + 1 : parts + 1 + slots]
    scores, tops, sums = refs[-3:]
    tokens = keys[0].shape[0]
    width = keys[0].shape[1]
    requests = count.shape[1]
    rows = scores.shape[0]
    heads = query.shape[1] * query.shape[2] // (steps * requests * width)
    per_line = query.shape[2] // width
    raw = [
        query[0][
            (head // per_line) * steps * requests : (head // per_line + 1) * steps * requests,
            (head % per_line) * width : (head % per_line + 1) * width,
        ]
        for head in range(heads)
    ]
    raw = jnp.concatenate(raw, axis=0)
    scaled = (raw.astype(jnp.float32) * smooth[...]).astype(jnp.bfloat16)
    for p in range(parts):
        scores[:, p * tokens : (p + 1) * tokens] = lax.dot_general(
            scaled, keys[p][...], (((1,), (1,)), ((), ())), preferred_element_type=jnp.float32
        )
    again = 2 if (rows // requests) % 2 == 0 else 1
    times = jnp.concatenate([count[0]] * again, axis=0)
    bias = jnp.where(times > 0.0, 0.0, NEGATIVE)
    for start in range(0, rows, again * requests):
        at = pl.ds(start, again * requests)
        raw = scores[at, :] * scale + bias
        top = jnp.max(raw, axis=1, keepdims=True)
        counted = jnp.exp(raw - top) * times
        probs[0, at, :] = counted.astype(jnp.bfloat16)
        tops[at, :] = jnp.broadcast_to(top, (again * requests, 128))
        sums[at, :] = jnp.broadcast_to(
            jnp.sum(counted, axis=1, keepdims=True), (again * requests, 128)
        )
    for slot in range(slots):

        @pl.when(pl.program_id(0) == slot)
        def _(slot=slot):
            stats[slot][0:1, :] = jnp.transpose(tops[...])[0:1, :]
            stats[slot][1:2, :] = jnp.transpose(sums[...])[0:1, :]


def score(groups, query, smooth, count, keys, steps, scale):
    slots, packed, columns = query.shape
    tokens, width = keys[0].shape
    rows = packed * columns // width
    parts = len(keys)
    requests = count.shape[1]
    probs, *stats = pl.pallas_call(
        functools.partial(score_kernel, slots, parts, steps, scale),
        out_shape=[jax.ShapeDtypeStruct((slots, rows, parts * tokens), jnp.bfloat16)]
        + [jax.ShapeDtypeStruct((2, rows), jnp.float32)] * slots,
        grid_spec=pltpu.PrefetchScalarGridSpec(
            num_scalar_prefetch=1,
            grid=(slots,),
            in_specs=[
                pl.BlockSpec((1, packed, columns), lambda k, group: (k, 0, 0)),
                pl.BlockSpec((1, width), lambda k, group: (0, 0)),
                pl.BlockSpec((1, requests, parts * tokens), lambda k, group: (group[k], 0, 0)),
            ]
            + [pl.BlockSpec((tokens, width), lambda k, group: (0, 0))] * parts,
            out_specs=[pl.BlockSpec((1, rows, parts * tokens), lambda k, group: (k, 0, 0))]
            + [pl.BlockSpec((2, rows), lambda k, group: (0, 0))] * slots,
            scratch_shapes=[
                pltpu.VMEM((rows, parts * tokens), jnp.float32),
                pltpu.VMEM((rows, 128), jnp.float32),
                pltpu.VMEM((rows, 128), jnp.float32),
            ],
        ),
        compiler_params=pltpu.CompilerParams(vmem_limit_bytes=16 * 2**20),
        cost_estimate=pl.CostEstimate(
            flops=2 * slots * rows * width * parts * tokens,
            bytes_accessed=2 * slots * rows * parts * tokens,
            transcendentals=slots * rows * parts * tokens,
        ),
        name="score",
    )(groups, query, smooth, count, *keys)
    return probs, stats


def thirds(x):
    out = []
    for _ in range(3):
        out.append(x.astype(jnp.bfloat16))
        x = x - out[-1].astype(jnp.float32)
    return out


def weigh_own_kernel(probs, values, out):
    out[0] = jnp.dot(probs[0], values[...], preferred_element_type=jnp.float32)


def weigh_kernel(slots, parts, own, *refs):
    probs, values = refs[:parts], refs[parts : 2 * parts]
    stats, outs = refs[2 * parts : 2 * parts + slots], refs[2 * parts + slots :]
    rows, width = own.shape[1:]
    summed = own[0]
    for p in range(parts):
        summed += jnp.dot(probs[p][0], values[p][...], preferred_element_type=jnp.float32)
    for slot in range(slots):

        @pl.when(pl.program_id(0) == slot)
        def _(slot=slot):
            outs[slot][0:rows, :] = summed.astype(jnp.bfloat16)
            lines = []
            for third in thirds(stats[slot][...]):
                third = third.astype(jnp.float32)
                lines += [third[:, c : c + width] for c in range(0, rows, width)]
            tail = outs[slot].shape[0] - rows
            lines.append(jnp.zeros((tail - 2 * len(lines), width), jnp.float32))
            outs[slot][rows:, :] = jnp.concatenate(lines, axis=0).astype(jnp.bfloat16)


def packed_rows(rows, width):
    return rows + (6 * (rows // width) // 16 + 1) * 16


def weigh(probs, values, stats):
    slots, rows, _ = probs.shape
    tokens, width = values[0].shape
    parts = len(values) - 1
    total_rows = packed_rows(rows, width)
    flops = 2 * slots * rows * width * tokens

    def probs_spec(p):
        return pl.BlockSpec((1, rows, tokens), lambda k, p=p: (k, 0, p))

    values_spec = pl.BlockSpec((tokens, width), lambda k: (0, 0))
    own_spec = pl.BlockSpec((1, rows, width), lambda k: (k, 0, 0))
    own = pl.pallas_call(
        weigh_own_kernel,
        out_shape=jax.ShapeDtypeStruct((slots, rows, width), jnp.float32),
        grid=(slots,),
        in_specs=[probs_spec(0), values_spec],
        out_specs=own_spec,
        compiler_params=pltpu.CompilerParams(vmem_limit_bytes=16 * 2**20),
        cost_estimate=pl.CostEstimate(
            flops=flops, bytes_accessed=2 * slots * rows * tokens, transcendentals=0
        ),
        name="weigh_own",
    )(probs, values[0])
    return pl.pallas_call(
        functools.partial(weigh_kernel, slots, parts),
        out_shape=[jax.ShapeDtypeStruct((total_rows, width), jnp.bfloat16)] * slots,
        grid=(slots,),
        in_specs=[own_spec]
        + [probs_spec(p + 1) for p in range(parts)]
        + [values_spec] * parts
        + [pl.BlockSpec((2, rows), lambda k: (0, 0))] * slots,
        out_specs=[pl.BlockSpec((total_rows, width), lambda k: (0, 0))] * slots,
        compiler_params=pltpu.CompilerParams(vmem_limit_bytes=16 * 2**20),
        cost_estimate=pl.CostEstimate(
            flops=flops * parts,
            bytes_accessed=2 * slots * rows * tokens * parts,
            transcendentals=0,
        ),
        name="weigh",
    )(own, *([probs] * parts), *values[1:], *stats)


def fresh_kernel(scale, query, smooth, new_keys, new_values, group_scale, summed, highest, total):
    steps, requests, width = new_keys.shape
    lines = steps * requests

    def by_line(x):
        x = x.astype(jnp.bfloat16).astype(jnp.float32)
        return jnp.concatenate([x] * steps, axis=0)

    def clip(x, row):
        limit = group_scale[row : row + 1, :]
        return jnp.clip(x, -8.0 * limit, 7.0 * limit)

    keys = [by_line(clip(new_keys[u] / smooth[...], 0)) for u in range(steps)]
    values = [by_line(clip(new_values[u], 1)) for u in range(steps)]
    line = lax.broadcasted_iota(jnp.int32, (lines, 1), 0)
    seen = [line >= u * requests for u in range(steps)]
    for head in range(query.shape[1] // width):
        at = pl.ds(head * lines, lines)
        mine = query[:, head * width : (head + 1) * width].astype(jnp.float32) * smooth[...]
        mine = mine.astype(jnp.bfloat16).astype(jnp.float32)
        scores = [
            jnp.where(seen[u], jnp.sum(mine * keys[u], axis=1, keepdims=True) * scale, NEGATIVE)
            for u in range(steps)
        ]
        top = functools.reduce(jnp.maximum, scores)
        expd = [jnp.where(seen[u], jnp.exp(scores[u] - top), 0.0) for u in range(steps)]
        highest[at, :] = jnp.broadcast_to(top, (lines, width))
        total[at, :] = jnp.broadcast_to(sum(expd), (lines, width))
        summed[at, :] = sum(
            e.astype(jnp.bfloat16).astype(jnp.float32) * value for e, value in zip(expd, values)
        )


def fresh(query, smooth, new_keys, new_values, group_scale, scale):
    lines, columns = query.shape
    width = smooth.shape[1]
    part = jax.ShapeDtypeStruct((lines * columns // width, width), jnp.float32)
    return pl.pallas_call(
        functools.partial(fresh_kernel, scale),
        out_shape=(part,) * 3,
        compiler_params=pltpu.CompilerParams(vmem_limit_bytes=16 * 2**20),
        name="fresh",
    )(query, smooth, new_keys, new_values, group_scale)


def finish_kernel(slots, *refs):
    messages, (summed, highest, total, out) = refs[:slots], refs[slots:]
    rows, width = summed.shape
    lines = out.shape[0]
    tails = [message[rows:, :].astype(jnp.float32) for message in messages]
    pieces = rows // width

    def column(slot, piece, which):
        row = [tails[slot][2 * (j * pieces + piece) + which :][:1] for j in range(3)]
        return jnp.transpose(jnp.broadcast_to(row[0] + row[1] + row[2], (width, width)))

    for piece in range(pieces):
        at = pl.ds(piece * width, width)
        parts = [
            (messages[k][at, :].astype(jnp.float32), column(k, piece, 0), column(k, piece, 1))
            for k in range(slots)
        ]
        parts.append((summed[at, :], highest[at, :], total[at, :]))
        top = functools.reduce(jnp.maximum, [part[1] for part in parts])
        shares = [jnp.exp(part[1] - top) for part in parts]
        norm = sum(share * part[2] for share, part in zip(shares, parts))
        merged = sum(share * part[0] for share, part in zip(shares, parts)) / norm
        merged = merged.astype(out.dtype)
        for first in range(0, width, lines):
            head = (piece * width + first) // lines
            out[:, head * width : (head + 1) * width] = merged[first : first + lines]


def finish(messages, own, lines):
    rows, width = own[0].shape
    return pl.pallas_call(
        functools.partial(finish_kernel, len(messages)),
        out_shape=jax.ShapeDtypeStruct((lines, rows * width // lines), jnp.bfloat16),
        compiler_params=pltpu.CompilerParams(vmem_limit_bytes=16 * 2**20),
        name="finish",
    )(*messages, *own)


def token_counts(page_table, lengths, first_pages, pages_dev):
    slots = page_table.shape[1]
    slot_ids = jnp.arange(slots, dtype=jnp.int32)
    whole_slots, rest = lengths // PAGE, lengths % PAGE
    pages = jnp.concatenate(
        [first + jnp.arange(pages_dev, dtype=jnp.int32) for first in first_pages]
    )
    same = page_table[:, :, None] == pages[None, None, :]
    whole = jnp.sum(same & (slot_ids[None, :] < whole_slots[:, None])[:, :, None], axis=1)
    last = jnp.sum(same & (slot_ids[None, :] == whole_slots[:, None])[:, :, None], axis=1)
    token = jnp.arange(pages.shape[0] * PAGE, dtype=jnp.int32)
    spread = token[None, :] // PAGE == jnp.arange(pages.shape[0], dtype=jnp.int32)[:, None]
    spread = spread.astype(jnp.bfloat16)
    whole = jnp.dot(whole.astype(jnp.bfloat16), spread, preferred_element_type=jnp.float32)
    last = jnp.dot(last.astype(jnp.bfloat16), spread, preferred_element_type=jnp.float32)
    return whole + jnp.where((token % PAGE)[None, :] < rest[:, None], last, 0.0)


def clip_keys(raw, smooth, scale):
    return jnp.clip(raw / smooth, -8.0 * scale[0], 7.0 * scale[0]).astype(jnp.bfloat16)


def clip_values(raw, scale):
    return jnp.clip(raw, -8.0 * scale[1], 7.0 * scale[1]).astype(jnp.bfloat16)


def my_part(x, axis, owner_is, ahead=0):
    owners = len(owner_is)
    size = x.shape[axis] // owners
    pieces = [lax.slice_in_dim(x, p * size, (p + 1) * size, axis=axis) for p in range(owners)]
    out = pieces[0]
    for p in range(1, owners):
        out = jnp.where(owner_is[(p - ahead) % owners], pieces[p], out)
    return out


def chip_top(raw_keys):
    top = jnp.max(jnp.abs(raw_keys), axis=0, keepdims=True)
    return functools.reduce(jnp.maximum, from_owners(top))


def smooth_of(top):
    top = functools.reduce(jnp.maximum, from_groups(top))
    return jnp.sqrt(top + EPSILON)


def line_pairs(hop, parity, groups):
    pairs = []
    for i in range(parity, groups - 1, 2):
        if i >= hop - 1:
            pairs.append((i, i + 1))
        if i + hop < groups:
            pairs.append((i + 1, i))
    return pairs


def line_project(hidden, key_weight, value_weight, own_query, early):
    groups, owners = lax.axis_size("seq"), lax.axis_size("rep")
    depth = key_weight.shape[0]
    barrier = lax.optimization_barrier

    def send(x, hop, parity):
        return lax.ppermute(x, "seq", line_pairs(hop, parity, groups))

    def absorb(name, blocks, hops, first=0):
        passed = [[shifted(block, "rep", k) for block in blocks] for k in range(1, owners)]
        for k, ready in enumerate([blocks] + passed):
            if k < first:
                continue
            totals[name] = project(
                hidden, totals[name], ready, depth, early[0], hops, k, groups, owners
            )

    totals = {}
    ka1 = send(key_weight, 1, 0)
    kb1 = send(key_weight, 1, 1)
    value_block = pack(value_weight, own_query)
    va1 = send(value_block, 1, 0)
    early, first = barrier((early, (key_weight, value_block)))
    hidden, totals["k"], totals["v"] = load(hidden, *first, early[0], owners)

    ka1, kb1, value_block, totals = barrier((ka1, kb1, value_block, totals))
    kb2 = send(ka1, 2, 1)
    ka2 = send(kb1, 2, 0)
    vb1 = send(value_block, 1, 1)
    for name, weight in (("k", key_weight), ("v", value_weight)):
        absorb(name, [weight], (((0, 0),),), 1)
    absorb("k", [ka1, kb1], (((0, 1),), ((1, 1),)))

    kb2, va1, own_block, totals = barrier((kb2, va1, value_block, totals))
    ends = [(0, groups - 1), (groups - 1, 0)]
    far_query = lax.ppermute(own_block[depth:], "seq", ends)
    ka3 = send(kb2, 3, 0)
    vb2 = send(va1, 2, 1)
    absorb("v", [va1], (((0, 1),),))

    ka2, totals = barrier((ka2, totals))
    absorb("k", [ka2 + kb2], (((0, 2), (1, 2)),))

    va2 = send(vb1, 2, 0)

    ka3, totals = barrier((ka3, totals))
    absorb("k", [ka3], (((0, 3),),))
    raw_keys = totals["k"]
    top = chip_top(raw_keys)
    smooth = smooth_of(top)
    vb1, vb2, top = barrier((vb1, vb2, top))
    va3 = send(vb2, 3, 0)
    absorb("v", [vb1], (((1, 1),),))
    va2, vb2, smooth = barrier((va2, vb2, smooth))
    absorb("v", [va2 + vb2], (((0, 2), (1, 2)),))
    queries = [
        value_block[depth:],
        va1[depth:],
        va2[depth:] + vb2[depth:],
        vb1[depth:] + far_query,
    ]

    def finish_values(scored, *args):
        args, totals["v"] = barrier((args, totals["v"]))
        probs, stats = scored(*args)
        block, stats = barrier((va3, stats))
        absorb("v", [block], (((0, 3),),))
        return probs, stats, totals["v"]

    return raw_keys, smooth, queries, early, finish_values


def on_device(
    hidden, key_weight, value_weight, group_scale, new_kv, decode_query, page_table, lengths
):
    tokens = hidden.shape[0]
    columns = key_weight.shape[1]
    groups, owners = lax.axis_size("seq"), lax.axis_size("rep")
    my_group, my_owner = lax.axis_index("seq"), lax.axis_index("rep")
    assert columns // HD == owners
    pages_dev = tokens // PAGE
    step_count, per_group = decode_query.shape[:2]

    owner_is = [my_owner == owner for owner in range(owners)]
    own_query = my_part(decode_query, 2, owner_is).reshape(step_count * per_group, -1)

    first_pages = [
        (my_group * owners + (my_owner - k) % owners) * pages_dev for k in range(owners)
    ]
    early = (
        jnp.stack([my_group, my_owner]),
        owner_is,
        first_pages,
        partner(my_group, jnp.arange(groups, dtype=jnp.int32), groups),
        own_query,
    )
    if groups == LINE:
        raw_keys, smooth, queries, early, finish_values = line_project(
            hidden, key_weight, value_weight, own_query, early
        )
    else:
        raw_keys, raw_values = (
            jnp.dot(
                hidden,
                lax.all_gather(weight, ("seq", "rep"), axis=0, tiled=True),
                preferred_element_type=jnp.float32,
            )
            for weight in (key_weight, value_weight)
        )
        queries = from_groups(
            jnp.concatenate(jnp.split(own_query, own_query.shape[1] // columns, axis=1))
        )
        smooth = smooth_of(chip_top(raw_keys))
    _, owner_is, first_pages, group_at, own_query = early
    counts = token_counts(page_table, lengths, first_pages, pages_dev)
    counts = counts.reshape(groups, per_group, -1)
    my_kv = my_part(new_kv, 3, owner_is).astype(jnp.float32)
    my_new = (my_kv[:, :, 0], my_kv[:, :, 1], my_part(group_scale, 1, owner_is))

    def by_head(x):
        return [my_part(x, 1, owner_is)] + [
            shifted(my_part(x, 1, owner_is, k), "rep", k) for k in range(1, owners)
        ]

    smoothing = smooth.reshape(-1)
    my_smooth = my_part(smooth, 1, owner_is)
    keys = clip_keys(raw_keys, smooth, group_scale)
    score_scale = HD ** (-0.5)
    scored = functools.partial(score, steps=step_count, scale=score_scale)
    args = (group_at, jnp.stack(queries), my_smooth, counts, by_head(keys))
    if groups == LINE:
        probs, stats, raw_values = finish_values(scored, *args)
    else:
        probs, stats = scored(*args)
    values = clip_values(raw_values, group_scale)
    messages = weigh(probs, by_head(values), stats)

    messages, keys, values, late = lax.optimization_barrier(
        (messages, keys, values, (own_query, my_smooth))
    )
    messages = to_groups(messages)
    is_key = lax.broadcasted_iota(jnp.int32, (1, 2, 1), 1) == 0
    kv_cache = jnp.where(is_key, keys[:, None, :], values[:, None, :])
    kv_cache = with_layout_constraint(kv_cache, Layout((0, 1, 2)))
    own = fresh(late[0], late[1], *my_new, score_scale)
    messages, kv_cache, own = lax.optimization_barrier((messages, kv_cache, own))
    attention = finish(messages, own, step_count * per_group)
    by_owner = from_owners(attention)
    attention = jnp.concatenate(
        [
            functools.reduce(
                lambda out, k: jnp.where(owner_is[(head + k) % owners], by_owner[k], out),
                range(1, owners),
                by_owner[0],
            )
            for head in range(owners)
        ],
        axis=1,
    ).reshape(decode_query.shape)
    return (kv_cache, smoothing, attention)


def solution(mesh):
    placed = (
        P(("seq", "rep"), None),
        P(("seq", "rep"), "head"),
        P(("seq", "rep"), "head"),
        P(None, "head"),
        P(None, "seq", None, "head"),
        P(None, "seq", "head"),
        P(),
        P(),
    )

    return jax.shard_map(
        on_device,
        mesh=mesh,
        in_specs=placed,
        out_specs=(P(("seq", "rep"), None, "head"), P("head"), P(None, "seq", "head")),
        check_vma=False,
    )
```
